32 devices in a mesh: dp: 8 (over z, x), seq: 4 (over y, core).
Axes of the slice: x: 2, y: 2, z: 4, core: 2. Of those that a mesh axis runs over, the one named last changes fastest.
Arguments:
- tokens: bfloat16 [1, 16384, 768], P(None, ('dp', 'seq')), may hold values from -6 to 6
- starts: int32 [1, 16384], P(None, ('dp', 'seq')), may hold values from 0 to 1024, as said below
- cotangent: bfloat16 [1, 16384, 768], P(None, ('dp', 'seq')), may hold values from -6 to 6
- attn_gain: bfloat16 [768], P(('dp', 'seq')), may hold values from 0.25 to 1.75
- attn_shift: bfloat16 [768], P(('dp', 'seq')), may hold values from -3 to 3
- attn_weight: bfloat16 [768, 2304], P(('dp', 'seq')), may hold values from -0.3125 to 0.3125
- attn_bias: bfloat16 [1536], P(('dp', 'seq')), may hold values from -3 to 3
- proj_weight: bfloat16 [768, 768], P(('dp', 'seq')), may hold values from -4 to 4
- proj_bias: bfloat16 [768], P(('dp', 'seq')), may hold values from -18 to 18
- mlp_gain: bfloat16 [768], P(('dp', 'seq')), may hold values from 0.25 to 1.75
- mlp_shift: bfloat16 [768], P(('dp', 'seq')), may hold values from -3 to 3
- up_weight: bfloat16 [768, 3072], P(('dp', 'seq')), may hold values from -0.21875 to 0.21875
- up_bias: bfloat16 [3072], P(('dp', 'seq')), may hold values from -3 to 3
- down_weight: bfloat16 [3072, 768], P(('dp', 'seq')), may hold values from -1.25 to 1.25
- down_bias: bfloat16 [768], P(('dp', 'seq')), may hold values from -18 to 18
Outputs:
- block_out: bfloat16 [1, 16384, 768], P(None, ('dp', 'seq'))
- input_grad: bfloat16 [1, 16384, 768], P(None, ('dp', 'seq'))
- attn_gain_grad: float32 [768], P(('dp', 'seq'))
- attn_shift_grad: float32 [768], P(('dp', 'seq'))
- attn_weight_grad: float32 [768, 2304], P(('dp', 'seq'))
- attn_bias_grad: float32 [1536], P(('dp', 'seq'))
- proj_weight_grad: float32 [768, 768], P(('dp', 'seq'))
- proj_bias_grad: float32 [768], P(('dp', 'seq'))
- mlp_gain_grad: float32 [768], P(('dp', 'seq'))
- mlp_shift_grad: float32 [768], P(('dp', 'seq'))
- up_weight_grad: float32 [768, 3072], P(('dp', 'seq'))
- up_bias_grad: float32 [3072], P(('dp', 'seq'))
- down_weight_grad: float32 [3072, 768], P(('dp', 'seq'))
- down_bias_grad: float32 [768], P(('dp', 'seq'))
The draws below stay inside these ranges and needn't reach their ends.
Inputs may be any that keep to these rules, and one draw needn't show every extreme that they name: Within each pack of 2048 tokens, starts is 0 for every token (one sequence), or 0 for the first 1024 tokens and 1024 for the rest (two sequences); both kinds occur in every draw.
All inputs are finite; a program needn't handle non-finite values.
Results may differ from the reference program's by a relative error of at most 0.015.
The reference program's roundings to bfloat16 on the way count: a program that leaves them out, or rounds other values in their place, can miss the bound.
Values may be sent and summed in bfloat16 or wider, within the bound.
No kernel may reach another device: no remote copies, remote signals or barrier semaphores. Data moves between devices by JAX's collectives and lax.ppermute only.
A program may use at most 192 MiB of HBM per device.

```python
import math
import jax
import jax.numpy as jnp
from jax import lax

D = 768
HD = 64
FF = 3072
PACK_LEN = 2048
PACKS = 1
TOKENS = 16384


def draw_starts(key, part):
    pack_count = PACKS * (TOKENS // PACK_LEN)
    split_flags = jax.random.randint(key, (pack_count,), 0, 2, dtype=jnp.int32)
    split_flags = split_flags.at[0].set(1).at[pack_count - 1].set(0)
    split_flags = split_flags.reshape(PACKS, TOKENS // PACK_LEN)
    places = jnp.arange(PACK_LEN, dtype=jnp.int32)
    half_len = PACK_LEN // 2
    later = (places >= half_len).astype(jnp.int32) * half_len
    start_table = split_flags[:, :, None] * later[None, None, :]
    return start_table.reshape(PACKS, TOKENS)


def shard_levels(rng, extent, split, least, top_value):
    level, own = 1.0, jax.random.fold_in(rng, 6)
    for position, blocks in split:
        heights = jnp.exp(jax.random.uniform(jax.random.fold_in(own, position), (blocks,), jnp.float32, least / len(split), top_value / len(split)))
        level = level * jnp.repeat(heights, extent[position] // blocks).reshape([-1 if axis == position else 1 for axis in range(len(extent))])
    return level


def gaussian(key, dims, scale, limit, split=(), kind=jnp.bfloat16):
    result = jax.random.normal(key, dims, jnp.float32) * scale
    if len(split) > 0:
        result = shard_levels(key, dims, split, -0.22, 0.18) * result
    return jnp.clip(result, min=-limit, max=limit).astype(kind)


def setup_inputs(seed: int = 0) -> dict:
    key_list = jax.random.split(jax.random.key(seed), 16)
    return {
        "tokens": gaussian(key_list[0], (PACKS, TOKENS, D), 1.0, 6.0, ((1, 32),)),
        "starts": draw_starts(jax.random.fold_in(key_list[15], 71), 0),
        "cotangent": gaussian(key_list[2], (PACKS, TOKENS, D), 1.0, 6.0, ((1, 32),)),
        "attn_gain": jnp.clip(1.0 + 0.15 * jax.random.normal(key_list[3], (D,), jnp.float32), 0.25, 1.75).astype(jnp.bfloat16),
        "attn_shift": gaussian(key_list[4], (D,), 0.5, 3.0, ((0, 32),)),
        "attn_weight": gaussian(key_list[5], (D, 3 * D), (D // 2) ** -0.5, 0.3125, ((0, 32),)),
        "attn_bias": gaussian(key_list[6], (2 * D,), 0.5, 3.0, ((0, 32),)),
        "proj_weight": gaussian(key_list[7], (D, D), 2 ** -0.5, 4.0, ((0, 32),)),
        "proj_bias": gaussian(key_list[8], (D,), 3.0, 18.0, ((0, 32),)),
        "mlp_gain": jnp.clip(1.0 + 0.15 * jax.random.normal(key_list[9], (D,), jnp.float32), 0.25, 1.75).astype(jnp.bfloat16),
        "mlp_shift": gaussian(key_list[10], (D,), 0.5, 3.0, ((0, 32),)),
        "up_weight": gaussian(key_list[11], (D, FF), D ** -0.5, 0.21875, ((0, 32),)),
        "up_bias": gaussian(key_list[12], (FF,), 0.5, 3.0, ((0, 32),)),
        "down_weight": gaussian(key_list[13], (FF, D), (FF // 128) ** -0.5, 1.25, ((0, 32),)),
        "down_bias": gaussian(key_list[14], (D,), 3.0, 18.0, ((0, 32),)),
    }


@jax.custom_vjp
def low(v):
    return lax.optimization_barrier(v.astype(jnp.bfloat16)).astype(jnp.float32)

@jax.custom_vjp
def low_back(v):
    return v

def low_keep(v):
    return (low(v), None)

def low_pass(kept, grad):
    return (grad,)

def back_keep(v):
    return (v, None)

def back_low(kept, grad):
    return (low(grad),)
low.defvjp(low_keep, low_pass)
low_back.defvjp(back_keep, back_low)
branch_scale = 1.0 / math.sqrt(48.0)
norm_eps = 1e-05
neg_fill = -1e+30

def matmul(first_op, second_op):
    return jnp.dot(first_op, second_op, precision=lax.Precision.HIGHEST, preferred_element_type=jnp.float32)

def layer_norm(values, norm_gain, norm_shift):
    center = values - lax.optimization_barrier(jnp.mean(values, axis=-1, keepdims=True))
    spread = lax.optimization_barrier(jnp.mean(center * center, axis=-1, keepdims=True))
    return center * lax.rsqrt(spread + norm_eps) * norm_gain + norm_shift

def pack_forward(inputs, start_rows, params):
    attn_gain, attn_shift, attn_weight, attn_bias, proj_weight, proj_bias, mlp_gain, mlp_shift, up_weight, up_bias, down_weight, down_bias = params
    length = inputs.shape[0]
    feature_count = inputs.shape[1]
    head_count = feature_count // HD
    normed = low(layer_norm(inputs, attn_gain, attn_shift))
    bias_full = jnp.concatenate([attn_bias[:feature_count], jnp.zeros((feature_count,), jnp.float32), attn_bias[feature_count:]])
    mixed_rows = low(low_back(matmul(normed, attn_weight) + bias_full))

    def heads_of(matrix):
        return matrix.reshape(length, head_count, HD).transpose(1, 0, 2)
    query_heads = heads_of(mixed_rows[:, :feature_count])
    key_heads = heads_of(mixed_rows[:, feature_count:2 * feature_count])
    value_heads = heads_of(mixed_rows[:, 2 * feature_count:])
    places = jnp.arange(length, dtype=jnp.int32)
    allowed = (places[None, :] <= places[:, None]) & (places[None, :] >= start_rows[:, None])

    def one_head(operands):
        query_head, key_head, value_head = operands
        scores = low_back(jnp.where(allowed, matmul(query_head, key_head.T) * HD ** (-0.5), neg_fill))
        prob_rows = jax.nn.softmax(scores, axis=-1)
        return matmul(low(prob_rows), value_head)
    head_out = lax.map(jax.checkpoint(one_head), (query_heads, key_heads, value_heads))
    attended = low(low_back(head_out.transpose(1, 0, 2).reshape(length, feature_count)))
    branch = low_back(matmul(attended, proj_weight) + proj_bias)
    middle = inputs + branch_scale * branch
    normed_mlp = low(layer_norm(middle, mlp_gain, mlp_shift))
    hidden_pre = low_back(matmul(normed_mlp, up_weight) + up_bias)
    hidden = low(jax.nn.gelu(hidden_pre, approximate=True))
    ffn_out = low_back(matmul(hidden, down_weight) + down_bias)
    return middle + branch_scale * ffn_out

def reference(tokens, starts, cotangent, attn_gain, attn_shift, attn_weight, attn_bias, proj_weight, proj_bias, mlp_gain, mlp_shift, up_weight, up_bias, down_weight, down_bias):
    params = tuple((param.astype(jnp.float32) for param in (attn_gain, attn_shift, attn_weight, attn_bias, proj_weight, proj_bias, mlp_gain, mlp_shift, up_weight, up_bias, down_weight, down_bias)))
    feature_count = tokens.shape[2]
    flat_tokens = tokens.reshape(-1, PACK_LEN, feature_count)
    flat_starts = starts.reshape(-1, PACK_LEN)
    flat_cot = cotangent.reshape(-1, PACK_LEN, feature_count)

    def step(totals, item):
        tokens_pack, starts_pack, cot_pack = item

        def forward_fn(values, weights):
            return pack_forward(values, starts_pack, weights)
        output, pull = jax.vjp(forward_fn, tokens_pack.astype(jnp.float32), params)
        grad_in, weight_grads = pull(cot_pack.astype(jnp.float32))
        totals = jax.tree.map(lambda first_term, second_term: first_term + second_term, totals, weight_grads)
        return (totals, (output.astype(jnp.bfloat16), grad_in.astype(jnp.bfloat16)))
    zeros_tree = jax.tree.map(jnp.zeros_like, params)
    totals, (outputs, grads_in) = lax.scan(step, zeros_tree, (flat_tokens, flat_starts, flat_cot))
    return (outputs.reshape(tokens.shape), grads_in.reshape(tokens.shape), totals[0], totals[1], totals[2], totals[3], totals[4], totals[5], totals[6], totals[7], totals[8], totals[9], totals[10], totals[11])
```

```python
import functools
import math

import jax
import jax.numpy as jnp
from jax import lax
from jax.experimental import pallas as pl
from jax.experimental.pallas import tpu as pltpu
from jax.sharding import PartitionSpec as P

HD = 64
AXES = ("dp", "seq")

branch_scale = 1.0 / math.sqrt(48.0)
norm_eps = 1e-05
neg_fill = -1e30
head_scale = HD ** (-0.5)


def layer_norm(values, norm_gain, norm_shift):
    center = values - jnp.mean(values, axis=-1, keepdims=True)
    spread = jnp.mean(center * center, axis=-1, keepdims=True)
    return center * lax.rsqrt(spread + norm_eps) * norm_gain + norm_shift


def gelu_tanh(values):
    return jax.nn.gelu(values, approximate=True)


def product(first_op, second_op):
    return jnp.dot(first_op, second_op, preferred_element_type=jnp.float32)


def transpose_times(first_op, second_op):
    return jnp.einsum("tk,tn->kn", first_op, second_op, preferred_element_type=jnp.float32)


def times_transpose(first_op, second_op):
    return jnp.einsum("tn,kn->tk", first_op, second_op, preferred_element_type=jnp.float32)


def flip(array, bit, count):
    return lax.ppermute(array, AXES, [(i, i ^ bit) for i in range(count)])


def stage_axis(done, bit):
    return sum(1 for other in done if other > bit)


def gather_rows(shard, order, me, count):
    done = []
    held = shard
    for bit in order:
        other = flip(held, bit, count)
        axis = stage_axis(done, bit)
        upper = (me & bit) != 0
        held = jnp.where(
            upper, jnp.stack([other, held], axis=axis), jnp.stack([held, other], axis=axis)
        )
        done.append(bit)
    return held.reshape(count * shard.shape[0], shard.shape[1])


def scatter_rows(total, order, me, count):
    done = list(order)
    rows = total.shape[0] // count
    held = total.reshape([2] * len(order) + [rows, total.shape[1]])
    for place, bit in enumerate(order):
        axis = stage_axis(done, bit)
        mine = jnp.where((me & bit) != 0, 1, 0)
        gone = lax.dynamic_index_in_dim(held, 1 - mine, axis, keepdims=False)
        kept = lax.dynamic_index_in_dim(held, mine, axis, keepdims=False)
        other = flip(gone, bit, count)
        held = kept.astype(jnp.float32) + other.astype(jnp.float32)
        if place + 1 < len(order):
            held = held.astype(jnp.bfloat16)
        done.remove(bit)
    return held


def nt(first_op, second_op):
    return lax.dot_general(
        first_op, second_op, (((1,), (1,)), ((), ())), preferred_element_type=jnp.float32
    )


def nn(first_op, second_op):
    return lax.dot_general(
        first_op, second_op, (((1,), (0,)), ((), ())), preferred_element_type=jnp.float32
    )


def lane_mask(shape, axis, head):
    place = lax.broadcasted_iota(jnp.int32, shape, axis)
    return (place < HD) if head == 0 else (place >= HD)


def fwd_kernel(info, qa_ref, qb_ref, kv_ref, o_ref, lse_ref, k_s, vt_s, acc_s, m_s):
    which = pl.program_id(1)
    rows = qa_ref.shape[1]
    width = 2 * HD

    @pl.when(which == 0)
    def _():
        for slot in range(4):
            if slot < 2:
                block = (qa_ref, qb_ref)[slot][0]
                key, value = block[:, width : 2 * width], block[:, 2 * width :]
            else:
                block = kv_ref[slot - 2, 0]
                key, value = block[:, :width], block[:, width:]
            k_s[slot] = key
            turned = value.astype(jnp.float32).T
            top = lane_mask((width, rows), 0, 0)
            vt_s[slot, 0] = jnp.where(top, turned, 1.0).astype(jnp.bfloat16)
            vt_s[slot, 1] = jnp.where(top, 1.0, turned).astype(jnp.bfloat16)

    query = jnp.where(which == 0, qa_ref[0, :, :width], qb_ref[0, :, :width])
    query = query * jnp.bfloat16(head_scale)
    queries = [
        jnp.where(lane_mask((rows, width), 1, head), query, jnp.bfloat16(0)) for head in range(2)
    ]
    block_id = info[which]

    def visit(slot, diagonal):
        for head in range(2):
            scores = nt(k_s[slot], queries[head])
            if diagonal:
                below = lax.broadcasted_iota(jnp.int32, (rows, rows), 0) <= (
                    lax.broadcasted_iota(jnp.int32, (rows, rows), 1)
                )
                scores = jnp.where(below, scores, neg_fill)
                peak = jnp.max(scores, axis=0, keepdims=True)
                raised = jnp.exp(scores - peak).astype(jnp.bfloat16)
                acc_s[head] = nn(vt_s[slot, head], raised)
            else:
                before = m_s[head : head + 1, :]
                peak = jnp.maximum(before, jnp.max(scores, axis=0, keepdims=True))
                raised = jnp.exp(scores - peak).astype(jnp.bfloat16)
                acc_s[head] = acc_s[head] * jnp.exp(before - peak) + nn(vt_s[slot, head], raised)
            m_s[head : head + 1, :] = peak

    visit(which, True)

    def step(block, carry):
        visit(info[4 + block], False)
        return carry

    lax.fori_loop(info[2 + which], block_id, step, 0)
    first, second = acc_s[0], acc_s[1]
    total0, total1 = first[HD : HD + 1, :], second[0:1, :]
    out = jnp.where(lane_mask((width, rows), 0, 0), first / total0, second / total1)
    o_ref[0, 0] = out.T.astype(jnp.bfloat16)
    lse_ref[0, 0, 0:1, :] = m_s[0:1, :] + jnp.log(total0)
    lse_ref[0, 0, 1:2, :] = m_s[1:2, :] + jnp.log(total1)


def bwd_kernel(
    info, qa_ref, qb_ref, kv_ref, o_ref, lse_ref, ga_ref, gb_ref, da_ref, dkv_ref,
    k_s, kt_s, v_s, dk_s, dv_s, dq_s,
):
    which = pl.program_id(1)
    rows = qa_ref.shape[1]
    width = 2 * HD

    @pl.when(which == 0)
    def _():
        for slot in range(4):
            if slot < 2:
                block = (qa_ref, qb_ref)[slot][0]
                key, value = block[:, width : 2 * width], block[:, 2 * width :]
            else:
                block = kv_ref[slot - 2, 0]
                key, value = block[:, :width], block[:, width:]
            k_s[slot] = key
            v_s[slot] = value
            kt_s[slot] = key.astype(jnp.float32).T.astype(jnp.bfloat16)
        dk_s[...] = jnp.zeros_like(dk_s)
        dv_s[...] = jnp.zeros_like(dv_s)

    query = jnp.where(which == 0, qa_ref[0, :, :width], qb_ref[0, :, :width])
    query = query * jnp.bfloat16(head_scale)
    grad = jnp.where(which == 0, ga_ref[0], gb_ref[0])
    joint = (grad.astype(jnp.float32) * o_ref[0, 0].astype(jnp.float32)).T
    queries, grads, dots = [], [], []
    for head in range(2):
        lanes = lane_mask((rows, width), 1, head)
        queries.append(jnp.where(lanes, query, jnp.bfloat16(0)))
        grads.append(jnp.where(lanes, grad, jnp.bfloat16(0)))
        dots.append(jnp.sum(joint[head * HD : (head + 1) * HD], axis=0, keepdims=True))
    block_id = info[which]
    dq_s[...] = jnp.zeros_like(dq_s)

    def visit(slot, diagonal):
        for head in range(2):
            scores = nt(k_s[slot], queries[head])
            probs = jnp.exp(scores - lse_ref[0, 0, head : head + 1, :])
            if diagonal:
                below = lax.broadcasted_iota(jnp.int32, (rows, rows), 0) <= (
                    lax.broadcasted_iota(jnp.int32, (rows, rows), 1)
                )
                probs = jnp.where(below, probs, 0.0)
            dv_s[slot] += nn(probs.astype(jnp.bfloat16), grads[head])
            pulled = nt(v_s[slot], grads[head])
            score_grad = (probs * (pulled - dots[head])).astype(jnp.bfloat16)
            dk_s[slot] += nn(score_grad, queries[head])
            part = nn(kt_s[slot], score_grad)
            span = slice(head * HD, (head + 1) * HD)
            dq_s[span, :] += part[span]

    visit(which, True)

    def step(block, carry):
        visit(info[4 + block], False)
        return carry

    lax.fori_loop(info[2 + which], block_id, step, 0)
    da_ref[0, 0] = (dq_s[...] * head_scale).T.astype(jnp.bfloat16)

    @pl.when(which == 1)
    def _():
        for slot in range(4):
            dkv_ref[slot, 0, :, :width] = dk_s[slot].astype(jnp.bfloat16)
            dkv_ref[slot, 0, :, width:] = dv_s[slot].astype(jnp.bfloat16)


def attend_forward(info, own, far, side):
    pairs, rows, columns = own.shape
    width = 2 * HD
    return pl.pallas_call(
        fwd_kernel,
        grid_spec=pltpu.PrefetchScalarGridSpec(
            num_scalar_prefetch=1,
            grid=(pairs, 2),
            in_specs=[
                pl.BlockSpec((1, rows, columns), lambda p, w, s: (p, 0, 0)),
                pl.BlockSpec((1, rows, columns), lambda p, w, s: (p, 0, 0)),
                pl.BlockSpec((2, 1, rows, 2 * width), lambda p, w, s: (0, p, 0, 0)),
            ],
            out_specs=[
                pl.BlockSpec((1, 1, rows, width), lambda p, w, s: (w, p, 0, 0)),
                pl.BlockSpec((1, 1, 8, rows), lambda p, w, s: (w, p, 0, 0)),
            ],
            scratch_shapes=[
                pltpu.VMEM((4, rows, width), jnp.bfloat16),
                pltpu.VMEM((4, 2, width, rows), jnp.bfloat16),
                pltpu.VMEM((2, width, rows), jnp.float32),
                pltpu.VMEM((8, rows), jnp.float32),
            ],
        ),
        out_shape=[
            jax.ShapeDtypeStruct((2, pairs, rows, width), jnp.bfloat16),
            jax.ShapeDtypeStruct((2, pairs, 8, rows), jnp.float32),
        ],
        cost_estimate=pl.CostEstimate(
            flops=pairs * 2 * 5 * 4 * rows * rows * width,
            bytes_accessed=8 * pairs * rows * columns,
            transcendentals=pairs * 2 * 5 * rows * rows,
        ),
        name="attend_forward",
    )(info, own, far, side)


def attend_backward(info, own, far, side, out, logsum, grad_own, grad_far):
    pairs, rows, columns = own.shape
    width = 2 * HD
    return pl.pallas_call(
        bwd_kernel,
        grid_spec=pltpu.PrefetchScalarGridSpec(
            num_scalar_prefetch=1,
            grid=(pairs, 2),
            in_specs=[
                pl.BlockSpec((1, rows, columns), lambda p, w, s: (p, 0, 0)),
                pl.BlockSpec((1, rows, columns), lambda p, w, s: (p, 0, 0)),
                pl.BlockSpec((2, 1, rows, 2 * width), lambda p, w, s: (0, p, 0, 0)),
                pl.BlockSpec((1, 1, rows, width), lambda p, w, s: (w, p, 0, 0)),
                pl.BlockSpec((1, 1, 8, rows), lambda p, w, s: (w, p, 0, 0)),
                pl.BlockSpec((1, rows, width), lambda p, w, s: (p, 0, 0)),
                pl.BlockSpec((1, rows, width), lambda p, w, s: (p, 0, 0)),
            ],
            out_specs=[
                pl.BlockSpec((1, 1, rows, width), lambda p, w, s: (w, p, 0, 0)),
                pl.BlockSpec((4, 1, rows, 2 * width), lambda p, w, s: (0, p, 0, 0)),
            ],
            scratch_shapes=[
                pltpu.VMEM((4, rows, width), jnp.bfloat16),
                pltpu.VMEM((4, width, rows), jnp.bfloat16),
                pltpu.VMEM((4, rows, width), jnp.bfloat16),
                pltpu.VMEM((4, rows, width), jnp.float32),
                pltpu.VMEM((4, rows, width), jnp.float32),
                pltpu.VMEM((width, rows), jnp.float32),
            ],
        ),
        out_shape=[
            jax.ShapeDtypeStruct((2, pairs, rows, width), jnp.bfloat16),
            jax.ShapeDtypeStruct((4, pairs, rows, 2 * width), jnp.bfloat16),
        ],
        cost_estimate=pl.CostEstimate(
            flops=pairs * 2 * 5 * 10 * rows * rows * width,
            bytes_accessed=16 * pairs * rows * columns,
            transcendentals=pairs * 2 * 5 * rows * rows,
        ),
        name="attend_backward",
    )(info, own, far, side, out, logsum, grad_own, grad_far)


def shards(
    dp_count, seq_count, tokens, starts, cotangent, attn_gain, attn_shift, attn_weight, attn_bias,
    proj_weight, proj_bias, mlp_gain, mlp_shift, up_weight, up_bias, down_weight, down_bias,
):
    count = dp_count * seq_count
    bits = [1 << i for i in range(count.bit_length() - 1)]
    core_bit, y_bit, x_bit, z_bits = bits[0], bits[1], bits[2], bits[3:]
    place = lax.axis_index("seq")
    me = lax.axis_index("dp") * seq_count + place
    half = place // (seq_count // 2)
    feature_count = tokens.shape[2]
    row_count = tokens.shape[1]
    ff_count = up_weight.shape[1]
    part = feature_count // count
    width = 2 * HD
    pair_count = feature_count // width
    near = pair_count // 2

    def order_in(first, second):
        return z_bits[::-1] + [first, second, core_bit]

    def order_out(first, second):
        return [core_bit, first, second] + z_bits

    def across(array):
        return lax.ppermute(array, "seq", [(i, seq_count - 1 - i) for i in range(seq_count)])

    def beside(array):
        return lax.ppermute(array, "seq", [(i, i ^ 1) for i in range(seq_count)])

    vectors = [attn_gain, attn_shift, attn_bias, proj_bias, mlp_gain, mlp_shift, up_bias, down_bias]
    columns = jnp.concatenate([vector.reshape(-1, part) for vector in vectors], axis=0).T
    columns = jnp.pad(columns, ((0, 0), (0, 128 - columns.shape[1])))
    attn_all = gather_rows(
        jnp.concatenate([attn_weight, columns], axis=1), order_in(x_bit, y_bit), me, count
    )
    updown = gather_rows(
        jnp.concatenate([up_weight, proj_weight], axis=1), order_in(y_bit, x_bit), me, count
    )
    down_full = gather_rows(down_weight, order_in(x_bit, y_bit), me, count)
    attn_full = attn_all[:, : 3 * feature_count]
    up_full, proj_full = updown[:, :ff_count], updown[:, ff_count:]
    lanes = attn_all[:, 3 * feature_count :].astype(jnp.float32).T
    full_vectors, spot = [], 0
    for vector in vectors:
        size = vector.shape[0] // part
        rows = lanes[spot : spot + size].reshape(size, count, part)
        full_vectors.append(rows.transpose(1, 0, 2).reshape(-1))
        spot += size
    (
        attn_gain_full, attn_shift_full, attn_bias_full, proj_bias_full,
        mlp_gain_full, mlp_shift_full, up_bias_full, down_bias_full,
    ) = full_vectors

    last_start = starts[0, -128:].reshape(1, 128)
    split = jnp.maximum(jnp.max(last_start), jnp.max(across(last_start))) > 0
    own_block, far_block = place, seq_count - 1 - place
    side_block, side_far = place ^ 1, seq_count - 1 - (place ^ 1)
    blocks = jnp.stack([own_block, far_block, side_block, side_far])
    lows = jnp.where(split & (blocks[:2] >= seq_count // 2), seq_count // 2, 0)
    slots = jnp.argsort(blocks)
    info = jnp.concatenate([blocks[:2], lows, slots]).astype(jnp.int32)

    inputs = tokens[0].astype(jnp.float32)
    normed = layer_norm(inputs, attn_gain_full, attn_shift_full).astype(jnp.bfloat16)
    bias_full = jnp.concatenate(
        [
            attn_bias_full[:feature_count],
            jnp.zeros((feature_count,), jnp.float32),
            attn_bias_full[feature_count:],
        ]
    )
    mixed = (product(normed, attn_full) + bias_full).astype(jnp.bfloat16)
    by_pair = mixed.reshape(row_count, 3, pair_count, width).transpose(2, 0, 1, 3)
    by_pair = by_pair.reshape(2, near, row_count, 3 * width)
    own = lax.dynamic_index_in_dim(by_pair, half, 0, keepdims=False)
    far = across(lax.dynamic_index_in_dim(by_pair, 1 - half, 0, keepdims=False))
    side = beside(jnp.stack([own[:, :, width:], far[:, :, width:]]))
    out, logsum = attend_forward(info, own, far, side)
    returned = across(out[1])
    first_half = jnp.where(half == 0, out[0], returned)
    second_half = jnp.where(half == 0, returned, out[0])
    attended = jnp.concatenate([first_half, second_half], axis=0)
    attended = attended.transpose(1, 0, 2).reshape(row_count, feature_count)
    middle = inputs + branch_scale * (product(attended, proj_full) + proj_bias_full)
    normed_mlp = layer_norm(middle, mlp_gain_full, mlp_shift_full).astype(jnp.bfloat16)
    hidden_pre = product(normed_mlp, up_full) + up_bias_full
    hidden = gelu_tanh(hidden_pre).astype(jnp.bfloat16)
    output = middle + branch_scale * (product(hidden, down_full) + down_bias_full)

    out_grad = cotangent[0].astype(jnp.float32)
    down_in = (branch_scale * out_grad).astype(jnp.bfloat16)
    down_weight_grad = transpose_times(hidden, down_in).astype(jnp.bfloat16)
    down_bias_grad = jnp.sum(down_in, axis=0, dtype=jnp.float32)
    hidden_grad = times_transpose(down_in, down_full)
    gelu_pull = jax.vjp(gelu_tanh, hidden_pre)[1]
    pre_grad = gelu_pull(hidden_grad)[0].astype(jnp.bfloat16)
    up_weight_grad = transpose_times(normed_mlp, pre_grad).astype(jnp.bfloat16)
    up_bias_grad = jnp.sum(pre_grad, axis=0, dtype=jnp.float32)
    mlp_pull = jax.vjp(layer_norm, middle, mlp_gain_full, mlp_shift_full)[1]
    middle_part, mlp_gain_grad, mlp_shift_grad = mlp_pull(times_transpose(pre_grad, up_full))
    middle_grad = out_grad + middle_part
    proj_in = (branch_scale * middle_grad).astype(jnp.bfloat16)
    proj_weight_grad = transpose_times(attended, proj_in).astype(jnp.bfloat16)
    proj_bias_grad = jnp.sum(proj_in, axis=0, dtype=jnp.float32)
    attended_grad = times_transpose(proj_in, proj_full).astype(jnp.bfloat16)
    grad_pair = attended_grad.reshape(row_count, pair_count, width).transpose(1, 0, 2)
    grad_pair = grad_pair.reshape(2, near, row_count, width)
    grad_own = lax.dynamic_index_in_dim(grad_pair, half, 0, keepdims=False)
    grad_far = across(lax.dynamic_index_in_dim(grad_pair, 1 - half, 0, keepdims=False))
    down_done = scatter_rows(down_weight_grad, order_out(y_bit, x_bit), me, count)
    updown_done = scatter_rows(
        jnp.concatenate([up_weight_grad, proj_weight_grad], axis=1),
        order_out(x_bit, y_bit), me, count,
    )
    query_grad, pair_grad = attend_backward(
        info, own, far, side, out, logsum, grad_own, grad_far
    )
    came = beside(pair_grad[2:])
    kept = (pair_grad[:2].astype(jnp.float32) + came.astype(jnp.float32)).astype(jnp.bfloat16)
    joined = jnp.concatenate([query_grad, kept], axis=-1)
    back = across(joined[1])
    first_half = jnp.where(half == 0, joined[0], back)
    second_half = jnp.where(half == 0, back, joined[0])
    mixed_grad = jnp.concatenate([first_half, second_half], axis=0)
    mixed_grad = mixed_grad.reshape(pair_count, row_count, 3, width).transpose(1, 2, 0, 3)
    mixed_grad = mixed_grad.reshape(row_count, 3 * feature_count)
    attn_weight_grad = transpose_times(normed, mixed_grad).astype(jnp.bfloat16)
    column_sums = jnp.sum(mixed_grad, axis=0, dtype=jnp.float32)
    attn_bias_grad = jnp.concatenate(
        [column_sums[:feature_count], column_sums[2 * feature_count :]]
    )
    attn_pull = jax.vjp(layer_norm, inputs, attn_gain_full, attn_shift_full)[1]
    input_part, attn_gain_grad, attn_shift_grad = attn_pull(
        times_transpose(mixed_grad, attn_full)
    )
    grad_in = (middle_grad + input_part).astype(jnp.bfloat16)

    vector_grads = [
        attn_gain_grad, attn_shift_grad, attn_bias_grad, proj_bias_grad,
        mlp_gain_grad, mlp_shift_grad, up_bias_grad, down_bias_grad,
    ]
    grad_columns = jnp.concatenate(
        [
            grad.reshape(count, -1, part).transpose(1, 0, 2).reshape(-1, feature_count)
            for grad in vector_grads
        ],
        axis=0,
    ).T
    grad_columns = jnp.pad(grad_columns, ((0, 0), (0, 128 - grad_columns.shape[1])))
    attn_done = scatter_rows(
        jnp.concatenate([attn_weight_grad, grad_columns.astype(jnp.bfloat16)], axis=1),
        order_out(x_bit, y_bit), me, count,
    )
    done_vectors, spot = [], 0
    done_lanes = attn_done[:, 3 * feature_count :].T
    for vector in vectors:
        size = vector.shape[0] // part
        done_vectors.append(done_lanes[spot : spot + size].reshape(-1))
        spot += size
    return (
        output.astype(jnp.bfloat16)[None],
        grad_in[None],
        done_vectors[0],
        done_vectors[1],
        attn_done[:, : 3 * feature_count],
        done_vectors[2],
        updown_done[:, ff_count:],
        done_vectors[3],
        done_vectors[4],
        done_vectors[5],
        updown_done[:, :ff_count],
        done_vectors[6],
        down_done,
        done_vectors[7],
    )


def solution(mesh):
    rows = P(AXES)
    tiles = P(AXES, None)
    pack = P(None, AXES, None)
    return jax.shard_map(
        functools.partial(shards, mesh.shape["dp"], mesh.shape["seq"]),
        mesh=mesh,
        in_specs=(
            pack, P(None, AXES), pack, rows, rows, tiles, rows, tiles, rows, rows, rows, tiles,
            rows, tiles, rows,
        ),
        out_specs=(
            pack, pack, rows, rows, tiles, rows, tiles, rows, rows, rows, tiles, rows, tiles, rows,
        ),
        check_vma=False,
    )
```

```python
import functools
import math

import jax
import jax.numpy as jnp
from jax import lax
from jax.experimental import pallas as pl
from jax.experimental.pallas import tpu as pltpu
from jax.sharding import PartitionSpec as P

HD = 64
AXES = ("dp", "seq")

branch_scale = 1.0 / math.sqrt(48.0)
norm_eps = 1e-05
neg_fill = -1e30
head_scale = HD ** (-0.5)


def layer_norm(values, norm_gain, norm_shift):
    center = values - jnp.mean(values, axis=-1, keepdims=True)
    spread = jnp.mean(center * center, axis=-1, keepdims=True)
    return center * lax.rsqrt(spread + norm_eps) * norm_gain + norm_shift


def gelu_tanh(values):
    return jax.nn.gelu(values, approximate=True)


def product(first_op, second_op):
    return jnp.dot(first_op, second_op, preferred_element_type=jnp.float32)


def transpose_times(first_op, second_op):
    return jnp.einsum("tk,tn->kn", first_op, second_op, preferred_element_type=jnp.float32)


def times_transpose(first_op, second_op):
    return jnp.einsum("tn,kn->tk", first_op, second_op, preferred_element_type=jnp.float32)


def flip(array, bit, count):
    return lax.ppermute(array, AXES, [(i, i ^ bit) for i in range(count)])


def distance(place, order):
    return sum(bit for i, bit in enumerate(order) if (place >> i) & 1)


def assemble(pieces, order, me, count):
    size, rows, columns = pieces[0].shape

    def body(me_ref, *refs):
        sources, target, sem = refs[:-2], refs[-2], refs[-1]
        for place in range(count):
            owner = me_ref[0] ^ distance(place, order)
            pltpu.make_async_copy(
                sources[place // size].at[place % size], target.at[owner], sem
            ).start()
        pltpu.make_async_copy(target, target, sem).wait()

    return pl.pallas_call(
        body,
        grid_spec=pltpu.PrefetchScalarGridSpec(
            num_scalar_prefetch=1,
            grid=(1,),
            in_specs=[pl.BlockSpec(memory_space=pl.ANY)] * len(pieces),
            out_specs=pl.BlockSpec((count, rows, columns), lambda i, me_ref: (0, 0, 0)),
            scratch_shapes=[pltpu.SemaphoreType.DMA],
        ),
        out_shape=jax.ShapeDtypeStruct((count, rows, columns), pieces[0].dtype),
        cost_estimate=pl.CostEstimate(
            flops=0, transcendentals=0, bytes_accessed=4 * count * rows * columns
        ),
        name="assemble",
    )(me.reshape(1), *pieces)


def gather_rows(held, order, me, count):
    stages = len(order)
    done = held.shape[0].bit_length() - 1
    for bit in order[done : stages - 2]:
        held = jnp.concatenate([held, flip(held, bit, count)], axis=0)
    near = flip(held, order[-2], count)
    pieces = [held, near, flip(held, order[-1], count), flip(near, order[-1], count)]
    return assemble(pieces, order, me, count).reshape(count * held.shape[1], held.shape[2])


def disperse(parts, order, me, count):
    rows = parts[0].shape[0] // count
    columns = sum(part.shape[1] for part in parts)
    half = count // 2

    def body(me_ref, *refs):
        sources, (kept, gone, near, far) = refs[: len(parts)], refs[len(parts) : -4]
        near_sem, far_sem, kept_sem, gone_sem = refs[-4:]
        for target, sem, base in ((far, far_sem, half), (near, near_sem, 0)):
            for place in range(half):
                owner, left = me_ref[0] ^ distance(base + place, order[::-1]), 0
                for source in sources:
                    span = slice(left, left + source.shape[2])
                    pltpu.make_async_copy(
                        source.at[owner], target.at[place, :, span], sem
                    ).start()
                    left = span.stop
        pltpu.make_async_copy(far, far, far_sem).wait()
        send = pltpu.make_async_copy(far, gone, gone_sem)
        send.start()
        pltpu.make_async_copy(near, near, near_sem).wait()
        keep = pltpu.make_async_copy(near, kept, kept_sem)
        keep.start()
        send.wait()
        keep.wait()

    shape = (half, rows, columns)
    return pl.pallas_call(
        body,
        grid_spec=pltpu.PrefetchScalarGridSpec(
            num_scalar_prefetch=1,
            grid=(1,),
            in_specs=[pl.BlockSpec(memory_space=pl.ANY)] * len(parts),
            out_specs=[pl.BlockSpec(memory_space=pl.ANY)] * 2,
            scratch_shapes=[pltpu.VMEM(shape, parts[0].dtype)] * 2
            + [pltpu.SemaphoreType.DMA] * 4,
        ),
        out_shape=[jax.ShapeDtypeStruct(shape, parts[0].dtype)] * 2,
        cost_estimate=pl.CostEstimate(
            flops=0, transcendentals=0, bytes_accessed=4 * count * rows * columns
        ),
        name="disperse",
    )(me.reshape(1), *[part.reshape(count, rows, part.shape[1]) for part in parts])


def add(first_term, second_term):
    return first_term.astype(jnp.float32) + second_term.astype(jnp.float32)


def begin_sum(parts, order, me, count):
    kept, gone = disperse(parts, order, me, count)
    return reduce_stage(kept, flip(gone, order[0], count), order[1], count)


def reduce_stage(kept, other, bit, count):
    half = kept.shape[0] // 2
    gone = add(kept[half:], other[half:]).astype(jnp.bfloat16)
    kept = add(kept[:half], other[:half]).astype(jnp.bfloat16)
    return kept, flip(gone, bit, count)


def finish_sum(kept, other, order, count):
    for bit in order[2:]:
        kept, other = reduce_stage(kept, other, bit, count)
    return add(kept[0], other[0])


def after(array, *others):
    return lax.optimization_barrier((array, *others))[0]


def nt(first_op, second_op):
    return lax.dot_general(
        first_op, second_op, (((1,), (1,)), ((), ())), preferred_element_type=jnp.float32
    )


def nn(first_op, second_op):
    return lax.dot_general(
        first_op, second_op, (((1,), (0,)), ((), ())), preferred_element_type=jnp.float32
    )


def lane_mask(shape, axis, head):
    place = lax.broadcasted_iota(jnp.int32, shape, axis)
    return (place < HD) if head == 0 else (place >= HD)


def fwd_kernel(info, q_ref, k_ref, v_ref, o_ref, lse_ref, vt_s, acc_s, m_s):
    which = pl.program_id(1)
    rows, width = q_ref.shape

    @pl.when(which == 0)
    def _():
        for slot in range(4):
            turned = v_ref[slot * rows : (slot + 1) * rows, :].astype(jnp.float32).T
            top = lane_mask((width, rows), 0, 0)
            vt_s[slot, 0] = jnp.where(top, turned, 1.0).astype(jnp.bfloat16)
            vt_s[slot, 1] = jnp.where(top, 1.0, turned).astype(jnp.bfloat16)

    query = q_ref[...] * jnp.bfloat16(head_scale)
    queries = [
        jnp.where(lane_mask((rows, width), 1, head), query, jnp.bfloat16(0)) for head in range(2)
    ]
    block_id = info[which]

    def visit(slot, diagonal):
        keys = k_ref[pl.ds(pl.multiple_of(slot * rows, rows), rows), :]
        for head in range(2):
            scores = nt(keys, queries[head])
            if diagonal:
                below = lax.broadcasted_iota(jnp.int32, (rows, rows), 0) <= (
                    lax.broadcasted_iota(jnp.int32, (rows, rows), 1)
                )
                scores = jnp.where(below, scores, neg_fill)
                peak = jnp.max(scores, axis=0, keepdims=True)
                raised = jnp.exp(scores - peak).astype(jnp.bfloat16)
                acc_s[head] = nn(vt_s[slot, head], raised)
            else:
                before = m_s[head : head + 1, :]
                peak = jnp.maximum(before, jnp.max(scores, axis=0, keepdims=True))
                raised = jnp.exp(scores - peak).astype(jnp.bfloat16)
                acc_s[head] = acc_s[head] * jnp.exp(before - peak) + nn(vt_s[slot, head], raised)
            m_s[head : head + 1, :] = peak

    visit(which, True)

    def step(block, carry):
        visit(info[4 + block], False)
        return carry

    lax.fori_loop(info[2 + which], block_id, step, 0)
    first, second = acc_s[0], acc_s[1]
    total0, total1 = first[HD : HD + 1, :], second[0:1, :]
    out = jnp.where(lane_mask((width, rows), 0, 0), first / total0, second / total1)
    o_ref[...] = out.T.astype(jnp.bfloat16)
    lse_ref[0, 0, 0:1, :] = m_s[0:1, :] + jnp.log(total0)
    lse_ref[0, 0, 1:2, :] = m_s[1:2, :] + jnp.log(total1)


def bwd_kernel(
    info, q_ref, k_ref, v_ref, o_ref, lse_ref, ga_ref, gb_ref, dq_ref, keep_ref, send_ref,
    kt_s, dk_s, dv_s, dq_s,
):
    which = pl.program_id(1)
    rows, width = q_ref.shape

    @pl.when(which == 0)
    def _():
        for slot in range(4):
            keys = k_ref[slot * rows : (slot + 1) * rows, :]
            kt_s[slot] = keys.astype(jnp.float32).T.astype(jnp.bfloat16)
        dk_s[...] = jnp.zeros_like(dk_s)
        dv_s[...] = jnp.zeros_like(dv_s)

    query = q_ref[...] * jnp.bfloat16(head_scale)
    grad = jnp.where(which == 0, ga_ref[...], gb_ref[...])
    joint = (grad.astype(jnp.float32) * o_ref[...].astype(jnp.float32)).T
    queries, grads, dots = [], [], []
    for head in range(2):
        lanes = lane_mask((rows, width), 1, head)
        queries.append(jnp.where(lanes, query, jnp.bfloat16(0)))
        grads.append(jnp.where(lanes, grad, jnp.bfloat16(0)))
        dots.append(jnp.sum(joint[head * HD : (head + 1) * HD], axis=0, keepdims=True))
    block_id = info[which]
    dq_s[...] = jnp.zeros_like(dq_s)

    def visit(slot, diagonal):
        spot = pl.ds(pl.multiple_of(slot * rows, rows), rows)
        keys, values = k_ref[spot, :], v_ref[spot, :]
        for head in range(2):
            scores = nt(keys, queries[head])
            probs = jnp.exp(scores - lse_ref[0, 0, head : head + 1, :])
            if diagonal:
                below = lax.broadcasted_iota(jnp.int32, (rows, rows), 0) <= (
                    lax.broadcasted_iota(jnp.int32, (rows, rows), 1)
                )
                probs = jnp.where(below, probs, 0.0)
            dv_s[slot] += nn(probs.astype(jnp.bfloat16), grads[head])
            pulled = nt(values, grads[head])
            score_grad = (probs * (pulled - dots[head])).astype(jnp.bfloat16)
            dk_s[slot] += nn(score_grad, queries[head])
            part = nn(kt_s[slot], score_grad)
            span = slice(head * HD, (head + 1) * HD)
            dq_s[span, :] += part[span]

    visit(which, True)

    def step(block, carry):
        visit(info[4 + block], False)
        return carry

    lax.fori_loop(info[2 + which], block_id, step, 0)
    dq_ref[...] = (dq_s[...] * head_scale).T.astype(jnp.bfloat16)

    @pl.when(which == 1)
    def _():
        for slot in range(4):
            target = (keep_ref, send_ref)[slot // 2]
            spot = slice((slot % 2) * rows, (slot % 2 + 1) * rows)
            target[0, spot, :] = dk_s[slot].astype(jnp.bfloat16)
            target[1, spot, :] = dv_s[slot].astype(jnp.bfloat16)


def attend_forward(info, query, pair):
    rows, columns = query.shape[0] // 2, query.shape[1]
    width = 2 * HD
    near = columns // width
    return pl.pallas_call(
        fwd_kernel,
        grid_spec=pltpu.PrefetchScalarGridSpec(
            num_scalar_prefetch=1,
            grid=(near, 2),
            in_specs=[
                pl.BlockSpec((rows, width), lambda p, w, s: (w, p)),
                pl.BlockSpec((4 * rows, width), lambda p, w, s: (0, p)),
                pl.BlockSpec((4 * rows, width), lambda p, w, s: (0, near + p)),
            ],
            out_specs=[
                pl.BlockSpec((rows, width), lambda p, w, s: (w, p)),
                pl.BlockSpec((1, 1, 8, rows), lambda p, w, s: (w, p, 0, 0)),
            ],
            scratch_shapes=[
                pltpu.VMEM((4, 2, width, rows), jnp.bfloat16),
                pltpu.VMEM((2, width, rows), jnp.float32),
                pltpu.VMEM((8, rows), jnp.float32),
            ],
        ),
        out_shape=[
            jax.ShapeDtypeStruct((2 * rows, columns), jnp.bfloat16),
            jax.ShapeDtypeStruct((2, near, 8, rows), jnp.float32),
        ],
        cost_estimate=pl.CostEstimate(
            flops=near * 2 * 5 * 4 * rows * rows * width,
            bytes_accessed=16 * rows * columns,
            transcendentals=near * 2 * 5 * rows * rows,
        ),
        name="attend_forward",
    )(info, query, pair, pair)


def attend_backward(info, query, pair, out, logsum, grad_own, grad_far):
    rows, columns = query.shape[0] // 2, query.shape[1]
    width = 2 * HD
    near = columns // width
    return pl.pallas_call(
        bwd_kernel,
        grid_spec=pltpu.PrefetchScalarGridSpec(
            num_scalar_prefetch=1,
            grid=(near, 2),
            in_specs=[
                pl.BlockSpec((rows, width), lambda p, w, s: (w, p)),
                pl.BlockSpec((4 * rows, width), lambda p, w, s: (0, p)),
                pl.BlockSpec((4 * rows, width), lambda p, w, s: (0, near + p)),
                pl.BlockSpec((rows, width), lambda p, w, s: (w, p)),
                pl.BlockSpec((1, 1, 8, rows), lambda p, w, s: (w, p, 0, 0)),
                pl.BlockSpec((rows, width), lambda p, w, s: (0, p)),
                pl.BlockSpec((rows, width), lambda p, w, s: (0, p)),
            ],
            out_specs=[
                pl.BlockSpec((rows, width), lambda p, w, s: (w, p)),
                pl.BlockSpec((2, 2 * rows, width), lambda p, w, s: (0, 0, p)),
                pl.BlockSpec((2, 2 * rows, width), lambda p, w, s: (0, 0, p)),
            ],
            scratch_shapes=[
                pltpu.VMEM((4, width, rows), jnp.bfloat16),
                pltpu.VMEM((4, rows, width), jnp.float32),
                pltpu.VMEM((4, rows, width), jnp.float32),
                pltpu.VMEM((width, rows), jnp.float32),
            ],
        ),
        out_shape=[
            jax.ShapeDtypeStruct((2 * rows, columns), jnp.bfloat16),
            jax.ShapeDtypeStruct((2, 2 * rows, columns), jnp.bfloat16),
            jax.ShapeDtypeStruct((2, 2 * rows, columns), jnp.bfloat16),
        ],
        cost_estimate=pl.CostEstimate(
            flops=near * 2 * 5 * 10 * rows * rows * width,
            bytes_accessed=32 * rows * columns,
            transcendentals=near * 2 * 5 * rows * rows,
        ),
        name="attend_backward",
    )(info, query, pair, pair, out, logsum, grad_own, grad_far)


def shards(
    dp_count, seq_count, tokens, starts, cotangent, attn_gain, attn_shift, attn_weight, attn_bias,
    proj_weight, proj_bias, mlp_gain, mlp_shift, up_weight, up_bias, down_weight, down_bias,
):
    count = dp_count * seq_count
    bits = [1 << i for i in range(count.bit_length() - 1)]
    core_bit, y_bit, x_bit, z_bits = bits[0], bits[1], bits[2], bits[3:]
    place = lax.axis_index("seq")
    me = lax.axis_index("dp") * seq_count + place
    half = place // (seq_count // 2)
    feature_count = tokens.shape[2]
    row_count = tokens.shape[1]
    ff_count = up_weight.shape[1]
    part = feature_count // count
    side_count = feature_count // 2

    def across(array):
        return lax.ppermute(array, "seq", [(i, seq_count - 1 - i) for i in range(seq_count)])

    def beside(array):
        return lax.ppermute(array, "seq", [(i, i ^ 1) for i in range(seq_count)])

    def sides(matrix):
        parts = matrix.reshape(matrix.shape[0], -1, 2, side_count)
        first = parts[:, :, 0].reshape(matrix.shape[0], -1)
        second = parts[:, :, 1].reshape(matrix.shape[0], -1)
        return jnp.where(half == 0, first, second), jnp.where(half == 0, second, first)

    vectors = [attn_gain, attn_shift, attn_bias, proj_bias, mlp_gain, mlp_shift, up_bias, down_bias]
    columns = jnp.concatenate([vector.reshape(-1, part) for vector in vectors], axis=0).T
    columns = jnp.pad(columns, ((0, 0), (0, 128 - columns.shape[1])))
    mine, theirs = sides(attn_weight)
    mine = jnp.concatenate([mine, columns], axis=1)
    theirs = flip(jnp.concatenate([theirs, columns], axis=1), y_bit, count)
    attn_all = gather_rows(
        jnp.stack([mine, theirs]), [y_bit] + z_bits[::-1] + [x_bit, core_bit], me, count
    )
    inputs = tokens[0]
    inputs_far = across(inputs)
    inputs_side = beside(inputs)
    inputs_side_far = beside(inputs_far)
    last_start = starts[0, -128:].reshape(1, 128)
    split = jnp.maximum(jnp.max(last_start), jnp.max(across(last_start))) > 0
    updown = lax.all_gather(
        jnp.concatenate([up_weight, proj_weight], axis=1), AXES, axis=0, tiled=True
    )
    down_full = lax.all_gather(down_weight, AXES, axis=0, tiled=True)
    attn_full = attn_all[:, : 3 * side_count]
    up_full, proj_full = updown[:, :ff_count], updown[:, ff_count:]
    lanes = attn_all[:, 3 * side_count :].astype(jnp.float32).T
    full_vectors, spot = [], 0
    for vector in vectors:
        size = vector.shape[0] // part
        rows = lanes[spot : spot + size].reshape(size, count, part)
        full_vectors.append(rows.transpose(1, 0, 2).reshape(-1))
        spot += size
    (
        attn_gain_full, attn_shift_full, attn_bias_full, proj_bias_full,
        mlp_gain_full, mlp_shift_full, up_bias_full, down_bias_full,
    ) = full_vectors

    far_place = seq_count - 1 - place
    spots = jnp.arange(8, dtype=jnp.int32)
    low = jnp.where(split, seq_count // 2, 0).astype(jnp.int32)
    block = spots - 4
    slot = jnp.where(
        block == place,
        0,
        jnp.where(block == far_place, 1, jnp.where(block == (place ^ 1), 2, 3)),
    )
    asked = jnp.where(spots % 2 == 0, place, far_place)
    info = jnp.where(
        spots < 2, asked, jnp.where(spots < 4, jnp.where(asked >= seq_count // 2, low, 0), slot)
    ).astype(jnp.int32)

    everyone = jnp.concatenate([inputs, inputs_far, inputs_side, inputs_side_far], axis=0)
    everyone = everyone.astype(jnp.float32)
    normed = layer_norm(everyone, attn_gain_full, attn_shift_full).astype(jnp.bfloat16)
    normed_pair = normed[: 2 * row_count]
    query_bias = lax.dynamic_slice_in_dim(attn_bias_full, half * side_count, side_count)
    value_bias = lax.dynamic_slice_in_dim(
        attn_bias_full, feature_count + half * side_count, side_count
    )
    pair_bias = jnp.concatenate([jnp.zeros((side_count,), jnp.float32), value_bias])
    query = (product(normed_pair, attn_full[:, :side_count]) + query_bias).astype(jnp.bfloat16)
    pair = (product(normed, attn_full[:, side_count:]) + pair_bias).astype(jnp.bfloat16)
    out, logsum = attend_forward(info, query, pair)
    returned = across(out[row_count:])
    out_own = out[:row_count]
    attended = jnp.where(
        half == 0,
        jnp.concatenate([out_own, returned], axis=1),
        jnp.concatenate([returned, out_own], axis=1),
    )
    inputs = inputs.astype(jnp.float32)
    middle = inputs + branch_scale * (product(attended, proj_full) + proj_bias_full)
    normed_mlp = layer_norm(middle, mlp_gain_full, mlp_shift_full).astype(jnp.bfloat16)
    hidden_pre = product(normed_mlp, up_full) + up_bias_full
    hidden = gelu_tanh(hidden_pre).astype(jnp.bfloat16)
    output = middle + branch_scale * (product(hidden, down_full) + down_bias_full)

    out_grad = cotangent[0].astype(jnp.float32)
    down_in = (branch_scale * out_grad).astype(jnp.bfloat16)
    down_weight_grad = transpose_times(hidden, down_in).astype(jnp.bfloat16)
    down_bias_grad = jnp.sum(down_in, axis=0, dtype=jnp.float32)
    hidden_grad = times_transpose(down_in, down_full)
    gelu_pull = jax.vjp(gelu_tanh, hidden_pre)[1]
    pre_grad = gelu_pull(hidden_grad)[0].astype(jnp.bfloat16)
    up_weight_grad = transpose_times(normed_mlp, pre_grad).astype(jnp.bfloat16)
    up_bias_grad = jnp.sum(pre_grad, axis=0, dtype=jnp.float32)
    mlp_pull = jax.vjp(layer_norm, middle, mlp_gain_full, mlp_shift_full)[1]
    middle_part, mlp_gain_grad, mlp_shift_grad = mlp_pull(times_transpose(pre_grad, up_full))
    middle_grad = out_grad + middle_part
    proj_in = (branch_scale * middle_grad).astype(jnp.bfloat16)
    proj_weight_grad = transpose_times(attended, proj_in).astype(jnp.bfloat16)
    proj_bias_grad = jnp.sum(proj_in, axis=0, dtype=jnp.float32)
    attended_grad = times_transpose(proj_in, proj_full).astype(jnp.bfloat16)
    grad_own, grad_gone = sides(attended_grad)
    grad_far = across(grad_gone)
    down_order = [core_bit, x_bit, y_bit] + z_bits
    down_sum = begin_sum([down_weight_grad], down_order, me, count)
    updown_order = [core_bit, y_bit, x_bit] + z_bits
    updown_sum = begin_sum([up_weight_grad, proj_weight_grad], updown_order, me, count)
    grad_own = after(grad_own, down_sum[0], updown_sum[0])
    query_grad, pair_grad, pair_gone = attend_backward(
        info, query, pair, out, logsum, grad_own, grad_far
    )
    down_done = finish_sum(*down_sum, down_order, count)
    updown_done = finish_sum(*updown_sum, updown_order, count)
    pair_grad = add(pair_grad, beside(pair_gone)).astype(jnp.bfloat16)
    mixed_grad = jnp.concatenate([query_grad, pair_grad[0], pair_grad[1]], axis=1)
    normed_grad = times_transpose(mixed_grad, attn_full)
    far_grad = across(normed_grad[row_count:].astype(jnp.bfloat16))
    normed_grad = normed_grad[:row_count] + far_grad.astype(jnp.float32)
    attn_weight_grad = transpose_times(normed_pair, mixed_grad).astype(jnp.bfloat16)
    column_sums = jnp.sum(mixed_grad, axis=0, dtype=jnp.float32).reshape(3, side_count)[::2]
    attn_bias_grad = jnp.where(
        half == 0,
        jnp.pad(column_sums, ((0, 0), (0, side_count))),
        jnp.pad(column_sums, ((0, 0), (side_count, 0))),
    ).reshape(-1)
    attn_pull = jax.vjp(layer_norm, inputs, attn_gain_full, attn_shift_full)[1]
    input_part, attn_gain_grad, attn_shift_grad = attn_pull(normed_grad)
    grad_in = (middle_grad + input_part).astype(jnp.bfloat16)

    vector_grads = [
        attn_gain_grad, attn_shift_grad, attn_bias_grad, proj_bias_grad,
        mlp_gain_grad, mlp_shift_grad, up_bias_grad, down_bias_grad,
    ]
    grad_columns = jnp.concatenate(
        [
            grad.reshape(count, -1, part).transpose(1, 0, 2).reshape(-1, feature_count)
            for grad in vector_grads
        ],
        axis=0,
    ).T
    grad_columns = jnp.pad(grad_columns, ((0, 0), (0, 128 - grad_columns.shape[1])))
    attn_order = [core_bit, x_bit] + z_bits + [y_bit]
    kept, other = begin_sum(
        [attn_weight_grad, grad_columns.astype(jnp.bfloat16)], attn_order, me, count
    )
    for bit in z_bits:
        kept, other = reduce_stage(kept, other, bit, count)
    mine = add(kept[0], other[0])
    other = flip(add(kept[1], other[1]).astype(jnp.bfloat16), y_bit, count).astype(jnp.float32)
    first = jnp.where(half == 0, mine, other)[:, : 3 * side_count].reshape(part, 3, 1, side_count)
    second = jnp.where(half == 0, other, mine)[:, : 3 * side_count].reshape(part, 3, 1, side_count)
    attn_done = jnp.concatenate([first, second], axis=2).reshape(part, 3 * feature_count)
    done_lanes = (mine + other)[:, 3 * side_count :].T
    done_vectors, spot = [], 0
    for vector in vectors:
        size = vector.shape[0] // part
        done_vectors.append(done_lanes[spot : spot + size].reshape(-1))
        spot += size
    return (
        output.astype(jnp.bfloat16)[None],
        grad_in[None],
        done_vectors[0],
        done_vectors[1],
        attn_done,
        done_vectors[2],
        updown_done[:, ff_count:],
        done_vectors[3],
        done_vectors[4],
        done_vectors[5],
        updown_done[:, :ff_count],
        done_vectors[6],
        down_done,
        done_vectors[7],
    )


def solution(mesh):
    rows = P(AXES)
    tiles = P(AXES, None)
    pack = P(None, AXES, None)
    return jax.shard_map(
        functools.partial(shards, mesh.shape["dp"], mesh.shape["seq"]),
        mesh=mesh,
        in_specs=(
            pack, P(None, AXES), pack, rows, rows, tiles, rows, tiles, rows, rows, rows, tiles,
            rows, tiles, rows,
        ),
        out_specs=(
            pack, pack, rows, rows, tiles, rows, tiles, rows, rows, rows, tiles, rows, tiles, rows,
        ),
        check_vma=False,
    )
```

```python
import functools
import math

import jax
import jax.numpy as jnp
from jax import lax
from jax.experimental import pallas as pl
from jax.experimental.pallas import tpu as pltpu
from jax.sharding import PartitionSpec as P

HD = 64
AXES = ("dp", "seq")

branch_scale = 1.0 / math.sqrt(48.0)
norm_eps = 1e-05
neg_fill = -1e30
head_scale = HD ** (-0.5)


def layer_norm(values, norm_gain, norm_shift):
    center = values - jnp.mean(values, axis=-1, keepdims=True)
    spread = jnp.mean(center * center, axis=-1, keepdims=True)
    return center * lax.rsqrt(spread + norm_eps) * norm_gain + norm_shift


def gelu_tanh(values):
    return jax.nn.gelu(values, approximate=True)


def product(first_op, second_op):
    return jnp.dot(first_op, second_op, preferred_element_type=jnp.float32)


def transpose_times(first_op, second_op):
    return jnp.einsum("tk,tn->kn", first_op, second_op, preferred_element_type=jnp.float32)


def times_transpose(first_op, second_op):
    return jnp.einsum("tn,kn->tk", first_op, second_op, preferred_element_type=jnp.float32)


def flip(array, bit, count):
    return lax.ppermute(array, AXES, [(i, i ^ bit) for i in range(count)])


def distance(place, order):
    return sum(bit for i, bit in enumerate(order) if (place >> i) & 1)


def assemble(pieces, order, me, count):
    size, rows, columns = pieces[0].shape

    def body(me_ref, *refs):
        sources, target, sem = refs[:-2], refs[-2], refs[-1]
        for place in range(count):
            owner = me_ref[0] ^ distance(place, order)
            pltpu.make_async_copy(
                sources[place // size].at[place % size], target.at[owner], sem
            ).start()
        pltpu.make_async_copy(target, target, sem).wait()

    return pl.pallas_call(
        body,
        grid_spec=pltpu.PrefetchScalarGridSpec(
            num_scalar_prefetch=1,
            grid=(1,),
            in_specs=[pl.BlockSpec(memory_space=pl.ANY)] * len(pieces),
            out_specs=pl.BlockSpec((count, rows, columns), lambda i, me_ref: (0, 0, 0)),
            scratch_shapes=[pltpu.SemaphoreType.DMA],
        ),
        out_shape=jax.ShapeDtypeStruct((count, rows, columns), pieces[0].dtype),
        cost_estimate=pl.CostEstimate(
            flops=0, transcendentals=0, bytes_accessed=4 * count * rows * columns
        ),
        name="assemble",
    )(me.reshape(1), *pieces)


def gather_rows(held, order, me, count, ties):
    stages = len(order)
    done = held.shape[0].bit_length() - 1
    for bit in order[done : stages - 2]:
        held = after(held, *ties.get(bit, ()))
        held = jnp.concatenate([held, flip(held, bit, count)], axis=0)
    held = after(held, *ties.get(order[-2], ()))
    near = flip(held, order[-2], count)
    beside = flip(held, order[-1], count)
    near = after(near, *ties.get(order[-1], ()))
    pieces = [held, near, beside, flip(near, order[-1], count)]
    return assemble(pieces, order, me, count).reshape(count * held.shape[1], held.shape[2])


def unpack(packed, parts):
    count, total, rows, columns = packed.shape
    rest = total - parts - 1

    def body(source, side_ref, one_ref, rest_ref, sem):
        pairs = [
            (source.at[:, i], side_ref.at[:, :, pl.ds(i * columns, columns)])
            for i in range(parts)
        ]
        pairs += [(source.at[:, parts], one_ref), (source.at[:, pl.ds(parts + 1, rest)], rest_ref)]
        copies = [
            pltpu.make_async_copy(first, second, sem.at[i])
            for i, (first, second) in enumerate(pairs)
        ]
        for copy in copies:
            copy.start()
        for copy in copies:
            copy.wait()

    shapes = [(count, rows, parts * columns), (count, rows, columns), (count, rest, rows, columns)]
    out = pl.pallas_call(
        body,
        grid=(1,),
        in_specs=[pl.BlockSpec(memory_space=pl.ANY)],
        out_specs=[
            pl.BlockSpec(shape, lambda i, rank=len(shape): (0,) * rank) for shape in shapes
        ],
        scratch_shapes=[pltpu.SemaphoreType.DMA((parts + 2,))],
        out_shape=[jax.ShapeDtypeStruct(shape, packed.dtype) for shape in shapes],
        cost_estimate=pl.CostEstimate(
            flops=0, transcendentals=0, bytes_accessed=4 * count * total * rows * columns
        ),
        name="unpack",
    )(packed)
    return [array.reshape(-1, array.shape[-1]) for array in out]


def disperse(parts, order, me, count):
    rows = parts[0].shape[0] // count
    columns = sum(part.shape[1] for part in parts)
    half = count // 2

    def body(me_ref, *refs):
        sources, (kept, gone, near, far) = refs[: len(parts)], refs[len(parts) : -4]
        near_sem, far_sem, kept_sem, gone_sem = refs[-4:]
        for target, sem, base in ((far, far_sem, half), (near, near_sem, 0)):
            for place in range(half):
                owner, left = me_ref[0] ^ distance(base + place, order[::-1]), 0
                for source in sources:
                    span = slice(left, left + source.shape[2])
                    pltpu.make_async_copy(
                        source.at[owner], target.at[place, :, span], sem
                    ).start()
                    left = span.stop
        pltpu.make_async_copy(far, far, far_sem).wait()
        send = pltpu.make_async_copy(far, gone, gone_sem)
        send.start()
        pltpu.make_async_copy(near, near, near_sem).wait()
        keep = pltpu.make_async_copy(near, kept, kept_sem)
        keep.start()
        send.wait()
        keep.wait()

    shape = (half, rows, columns)
    return pl.pallas_call(
        body,
        grid_spec=pltpu.PrefetchScalarGridSpec(
            num_scalar_prefetch=1,
            grid=(1,),
            in_specs=[pl.BlockSpec(memory_space=pl.ANY)] * len(parts),
            out_specs=[pl.BlockSpec(memory_space=pl.ANY)] * 2,
            scratch_shapes=[pltpu.VMEM(shape, parts[0].dtype)] * 2
            + [pltpu.SemaphoreType.DMA] * 4,
        ),
        out_shape=[jax.ShapeDtypeStruct(shape, parts[0].dtype)] * 2,
        cost_estimate=pl.CostEstimate(
            flops=0, transcendentals=0, bytes_accessed=4 * count * rows * columns
        ),
        name="disperse",
    )(me.reshape(1), *[part.reshape(count, rows, part.shape[1]) for part in parts])


def add(first_term, second_term):
    return first_term.astype(jnp.float32) + second_term.astype(jnp.float32)


def begin_sum(parts, order, me, count):
    kept, gone = disperse(parts, order, me, count)
    return reduce_stage(kept, flip(gone, order[0], count), order[1], count)


def reduce_stage(kept, other, bit, count):
    half = kept.shape[0] // 2
    gone = add(kept[half:], other[half:]).astype(jnp.bfloat16)
    kept = add(kept[:half], other[:half]).astype(jnp.bfloat16)
    return kept, flip(gone, bit, count)


def finish_sum(kept, other, order, count):
    for bit in order[2:]:
        kept, other = reduce_stage(kept, other, bit, count)
    return add(kept[0], other[0])


def after(array, *others):
    return lax.optimization_barrier((array, *others))[0]


def nt(first_op, second_op):
    return lax.dot_general(
        first_op, second_op, (((1,), (1,)), ((), ())), preferred_element_type=jnp.float32
    )


def nn(first_op, second_op):
    return lax.dot_general(
        first_op, second_op, (((1,), (0,)), ((), ())), preferred_element_type=jnp.float32
    )


def lane_mask(shape, axis, head):
    place = lax.broadcasted_iota(jnp.int32, shape, axis)
    return (place < HD) if head == 0 else (place >= HD)


def fwd_kernel(info, q_ref, k_ref, v_ref, o_ref, lse_ref, vt_s, acc_s, m_s):
    which = pl.program_id(1)
    rows, width = q_ref.shape

    @pl.when(which == 0)
    def _():
        for slot in range(4):
            turned = v_ref[slot * rows : (slot + 1) * rows, :].astype(jnp.float32).T
            top = lane_mask((width, rows), 0, 0)
            vt_s[slot, 0] = jnp.where(top, turned, 1.0).astype(jnp.bfloat16)
            vt_s[slot, 1] = jnp.where(top, 1.0, turned).astype(jnp.bfloat16)

    query = q_ref[...] * jnp.bfloat16(head_scale)
    queries = [
        jnp.where(lane_mask((rows, width), 1, head), query, jnp.bfloat16(0)) for head in range(2)
    ]
    block_id = info[which]

    def visit(slot, diagonal):
        keys = k_ref[pl.ds(pl.multiple_of(slot * rows, rows), rows), :]
        for head in range(2):
            scores = nt(keys, queries[head])
            if diagonal:
                below = lax.broadcasted_iota(jnp.int32, (rows, rows), 0) <= (
                    lax.broadcasted_iota(jnp.int32, (rows, rows), 1)
                )
                scores = jnp.where(below, scores, neg_fill)
                peak = jnp.max(scores, axis=0, keepdims=True)
                raised = jnp.exp(scores - peak).astype(jnp.bfloat16)
                acc_s[head] = nn(vt_s[slot, head], raised)
            else:
                before = m_s[head : head + 1, :]
                peak = jnp.maximum(before, jnp.max(scores, axis=0, keepdims=True))
                raised = jnp.exp(scores - peak).astype(jnp.bfloat16)
                acc_s[head] = acc_s[head] * jnp.exp(before - peak) + nn(vt_s[slot, head], raised)
            m_s[head : head + 1, :] = peak

    visit(which, True)

    def step(block, carry):
        visit(info[4 + block], False)
        return carry

    lax.fori_loop(info[2 + which], block_id, step, 0)
    first, second = acc_s[0], acc_s[1]
    total0, total1 = first[HD : HD + 1, :], second[0:1, :]
    out = jnp.where(lane_mask((width, rows), 0, 0), first / total0, second / total1)
    o_ref[...] = out.T.astype(jnp.bfloat16)
    lse_ref[0, 0, 0:1, :] = m_s[0:1, :] + jnp.log(total0)
    lse_ref[0, 0, 1:2, :] = m_s[1:2, :] + jnp.log(total1)


def bwd_kernel(
    info, q_ref, k_ref, v_ref, o_ref, lse_ref, ga_ref, gb_ref, dq_ref, keep_ref, send_ref,
    kt_s, dk_s, dv_s, dq_s,
):
    which = pl.program_id(1)
    rows, width = q_ref.shape

    @pl.when(which == 0)
    def _():
        for slot in range(4):
            keys = k_ref[slot * rows : (slot + 1) * rows, :]
            kt_s[slot] = keys.astype(jnp.float32).T.astype(jnp.bfloat16)
        dk_s[...] = jnp.zeros_like(dk_s)
        dv_s[...] = jnp.zeros_like(dv_s)

    query = q_ref[...] * jnp.bfloat16(head_scale)
    grad = jnp.where(which == 0, ga_ref[...], gb_ref[...])
    joint = (grad.astype(jnp.float32) * o_ref[...].astype(jnp.float32)).T
    queries, grads, dots = [], [], []
    for head in range(2):
        lanes = lane_mask((rows, width), 1, head)
        queries.append(jnp.where(lanes, query, jnp.bfloat16(0)))
        grads.append(jnp.where(lanes, grad, jnp.bfloat16(0)))
        dots.append(jnp.sum(joint[head * HD : (head + 1) * HD], axis=0, keepdims=True))
    block_id = info[which]
    dq_s[...] = jnp.zeros_like(dq_s)

    def visit(slot, diagonal):
        spot = pl.ds(pl.multiple_of(slot * rows, rows), rows)
        keys, values = k_ref[spot, :], v_ref[spot, :]
        for head in range(2):
            scores = nt(keys, queries[head])
            probs = jnp.exp(scores - lse_ref[0, 0, head : head + 1, :])
            if diagonal:
                below = lax.broadcasted_iota(jnp.int32, (rows, rows), 0) <= (
                    lax.broadcasted_iota(jnp.int32, (rows, rows), 1)
                )
                probs = jnp.where(below, probs, 0.0)
            dv_s[slot] += nn(probs.astype(jnp.bfloat16), grads[head])
            pulled = nt(values, grads[head])
            score_grad = (probs * (pulled - dots[head])).astype(jnp.bfloat16)
            dk_s[slot] += nn(score_grad, queries[head])
            part = nn(kt_s[slot], score_grad)
            span = slice(head * HD, (head + 1) * HD)
            dq_s[span, :] += part[span]

    visit(which, True)

    def step(block, carry):
        visit(info[4 + block], False)
        return carry

    lax.fori_loop(info[2 + which], block_id, step, 0)
    dq_ref[...] = (dq_s[...] * head_scale).T.astype(jnp.bfloat16)

    @pl.when(which == 1)
    def _():
        for slot in range(4):
            target = (keep_ref, send_ref)[slot // 2]
            spot = slice((slot % 2) * rows, (slot % 2 + 1) * rows)
            target[0, spot, :] = dk_s[slot].astype(jnp.bfloat16)
            target[1, spot, :] = dv_s[slot].astype(jnp.bfloat16)


def attend_forward(info, query, pair):
    rows, columns = query.shape[0] // 2, query.shape[1]
    width = 2 * HD
    near = columns // width
    return pl.pallas_call(
        fwd_kernel,
        grid_spec=pltpu.PrefetchScalarGridSpec(
            num_scalar_prefetch=1,
            grid=(near, 2),
            in_specs=[
                pl.BlockSpec((rows, width), lambda p, w, s: (w, p)),
                pl.BlockSpec((4 * rows, width), lambda p, w, s: (0, p)),
                pl.BlockSpec((4 * rows, width), lambda p, w, s: (0, near + p)),
            ],
            out_specs=[
                pl.BlockSpec((rows, width), lambda p, w, s: (w, p)),
                pl.BlockSpec((1, 1, 8, rows), lambda p, w, s: (w, p, 0, 0)),
            ],
            scratch_shapes=[
                pltpu.VMEM((4, 2, width, rows), jnp.bfloat16),
                pltpu.VMEM((2, width, rows), jnp.float32),
                pltpu.VMEM((8, rows), jnp.float32),
            ],
        ),
        out_shape=[
            jax.ShapeDtypeStruct((2 * rows, columns), jnp.bfloat16),
            jax.ShapeDtypeStruct((2, near, 8, rows), jnp.float32),
        ],
        cost_estimate=pl.CostEstimate(
            flops=near * 2 * 5 * 4 * rows * rows * width,
            bytes_accessed=16 * rows * columns,
            transcendentals=near * 2 * 5 * rows * rows,
        ),
        name="attend_forward",
    )(info, query, pair, pair)


def attend_backward(info, query, pair, out, logsum, grad_own, grad_far):
    rows, columns = query.shape[0] // 2, query.shape[1]
    width = 2 * HD
    near = columns // width
    return pl.pallas_call(
        bwd_kernel,
        grid_spec=pltpu.PrefetchScalarGridSpec(
            num_scalar_prefetch=1,
            grid=(near, 2),
            in_specs=[
                pl.BlockSpec((rows, width), lambda p, w, s: (w, p)),
                pl.BlockSpec((4 * rows, width), lambda p, w, s: (0, p)),
                pl.BlockSpec((4 * rows, width), lambda p, w, s: (0, near + p)),
                pl.BlockSpec((rows, width), lambda p, w, s: (w, p)),
                pl.BlockSpec((1, 1, 8, rows), lambda p, w, s: (w, p, 0, 0)),
                pl.BlockSpec((rows, width), lambda p, w, s: (0, p)),
                pl.BlockSpec((rows, width), lambda p, w, s: (0, p)),
            ],
            out_specs=[
                pl.BlockSpec((rows, width), lambda p, w, s: (w, p)),
                pl.BlockSpec((2, 2 * rows, width), lambda p, w, s: (0, 0, p)),
                pl.BlockSpec((2, 2 * rows, width), lambda p, w, s: (0, 0, p)),
            ],
            scratch_shapes=[
                pltpu.VMEM((4, width, rows), jnp.bfloat16),
                pltpu.VMEM((4, rows, width), jnp.float32),
                pltpu.VMEM((4, rows, width), jnp.float32),
                pltpu.VMEM((width, rows), jnp.float32),
            ],
        ),
        out_shape=[
            jax.ShapeDtypeStruct((2 * rows, columns), jnp.bfloat16),
            jax.ShapeDtypeStruct((2, 2 * rows, columns), jnp.bfloat16),
            jax.ShapeDtypeStruct((2, 2 * rows, columns), jnp.bfloat16),
        ],
        cost_estimate=pl.CostEstimate(
            flops=near * 2 * 5 * 10 * rows * rows * width,
            bytes_accessed=32 * rows * columns,
            transcendentals=near * 2 * 5 * rows * rows,
        ),
        name="attend_backward",
    )(info, query, pair, pair, out, logsum, grad_own, grad_far)


def shards(
    dp_count, seq_count, tokens, starts, cotangent, attn_gain, attn_shift, attn_weight, attn_bias,
    proj_weight, proj_bias, mlp_gain, mlp_shift, up_weight, up_bias, down_weight, down_bias,
):
    count = dp_count * seq_count
    bits = [1 << i for i in range(count.bit_length() - 1)]
    core_bit, y_bit, x_bit, z_bits = bits[0], bits[1], bits[2], bits[3:]
    place = lax.axis_index("seq")
    me = lax.axis_index("dp") * seq_count + place
    half = place // (seq_count // 2)
    feature_count = tokens.shape[2]
    row_count = tokens.shape[1]
    ff_count = up_weight.shape[1]
    part = feature_count // count
    side_count = feature_count // 2

    def across(array):
        return lax.ppermute(array, "seq", [(i, seq_count - 1 - i) for i in range(seq_count)])

    def beside(array):
        return lax.ppermute(array, "seq", [(i, i ^ 1) for i in range(seq_count)])

    def sides(matrix):
        parts = matrix.reshape(matrix.shape[0], -1, 2, side_count)
        first = parts[:, :, 0].reshape(matrix.shape[0], -1)
        second = parts[:, :, 1].reshape(matrix.shape[0], -1)
        return jnp.where(half == 0, first, second), jnp.where(half == 0, second, first)

    vectors = [attn_gain, attn_shift, attn_bias, proj_bias, mlp_gain, mlp_shift, up_bias, down_bias]
    columns = jnp.concatenate(vectors).reshape(-1, part).T
    columns = jnp.pad(columns, ((0, 0), (0, 128 - columns.shape[1])))
    mine, theirs = sides(attn_weight)
    mine = jnp.concatenate([mine, columns], axis=1)
    theirs = flip(jnp.concatenate([theirs, columns], axis=1), y_bit, count)
    ff_parts = ff_count // feature_count
    packed = lax.all_gather(
        jnp.concatenate(
            [up_weight[:, i * feature_count : (i + 1) * feature_count] for i in range(ff_parts)]
            + [proj_weight, down_weight],
            axis=0,
        ).reshape(-1, part, feature_count),
        AXES, axis=0,
    )
    up_full, proj_full, down_full = unpack(packed, ff_parts)
    last_start = starts[0, -128:].reshape(1, 128)
    last_far = across(last_start)
    inputs = tokens[0]
    inputs_far = across(inputs)
    inputs_side = beside(inputs)
    inputs_side_far = beside(inputs_far)
    everyone = jnp.concatenate([inputs, inputs_far, inputs_side, inputs_side_far], axis=0)
    everyone = everyone.astype(jnp.float32)
    mean = jnp.mean(everyone, axis=-1, keepdims=True)
    spread = lax.rsqrt(
        jnp.mean((everyone - mean) * (everyone - mean), axis=-1, keepdims=True) + norm_eps
    )
    attn_all = gather_rows(
        jnp.stack([mine, theirs]), [y_bit] + z_bits[::-1] + [x_bit, core_bit], me, count,
        {z_bits[0]: (last_far, inputs_side), x_bit: (inputs_far,), core_bit: (mean, spread)},
    )
    split = jnp.maximum(jnp.max(last_start), jnp.max(last_far)) > 0
    attn_full = attn_all[:, : 3 * side_count]
    lanes = attn_all[:, 3 * side_count :].astype(jnp.float32).T
    full_vectors, spot = [], 0
    for vector in vectors:
        size = vector.shape[0] // part
        rows = lanes[spot : spot + size].reshape(size, count, part)
        full_vectors.append(rows.transpose(1, 0, 2).reshape(-1))
        spot += size
    (
        attn_gain_full, attn_shift_full, attn_bias_full, proj_bias_full,
        mlp_gain_full, mlp_shift_full, up_bias_full, down_bias_full,
    ) = full_vectors

    far_place = seq_count - 1 - place
    spots = jnp.arange(8, dtype=jnp.int32)
    low = jnp.where(split, seq_count // 2, 0).astype(jnp.int32)
    block = spots - 4
    slot = jnp.where(
        block == place,
        0,
        jnp.where(block == far_place, 1, jnp.where(block == (place ^ 1), 2, 3)),
    )
    asked = jnp.where(spots % 2 == 0, place, far_place)
    info = jnp.where(
        spots < 2, asked, jnp.where(spots < 4, jnp.where(asked >= seq_count // 2, low, 0), slot)
    ).astype(jnp.int32)

    normed = (everyone - mean) * spread * attn_gain_full + attn_shift_full
    normed = normed.astype(jnp.bfloat16)
    normed_pair = normed[: 2 * row_count]
    query_bias = lax.dynamic_slice_in_dim(attn_bias_full, half * side_count, side_count)
    value_bias = lax.dynamic_slice_in_dim(
        attn_bias_full, feature_count + half * side_count, side_count
    )
    pair_bias = jnp.concatenate([jnp.zeros((side_count,), jnp.float32), value_bias])
    query = (product(normed_pair, attn_full[:, :side_count]) + query_bias).astype(jnp.bfloat16)
    pair = (product(normed, attn_full[:, side_count:]) + pair_bias).astype(jnp.bfloat16)
    out, logsum = attend_forward(info, query, pair)
    returned = across(out[row_count:])
    out_own = out[:row_count]
    attended = jnp.where(
        half == 0,
        jnp.concatenate([out_own, returned], axis=1),
        jnp.concatenate([returned, out_own], axis=1),
    )
    inputs = inputs.astype(jnp.float32)
    middle = inputs + branch_scale * (product(attended, proj_full) + proj_bias_full)
    normed_mlp = layer_norm(middle, mlp_gain_full, mlp_shift_full).astype(jnp.bfloat16)
    hidden_pre = product(normed_mlp, up_full) + up_bias_full
    hidden = gelu_tanh(hidden_pre).astype(jnp.bfloat16)
    output = middle + branch_scale * (product(hidden, down_full) + down_bias_full)

    out_grad = cotangent[0].astype(jnp.float32)
    down_in = (branch_scale * out_grad).astype(jnp.bfloat16)
    down_weight_grad = transpose_times(hidden, down_in).astype(jnp.bfloat16)
    down_bias_grad = jnp.sum(down_in, axis=0, dtype=jnp.float32)
    hidden_grad = times_transpose(down_in, down_full)
    gelu_pull = jax.vjp(gelu_tanh, hidden_pre)[1]
    pre_grad = gelu_pull(hidden_grad)[0].astype(jnp.bfloat16)
    up_weight_grad = transpose_times(normed_mlp, pre_grad).astype(jnp.bfloat16)
    up_bias_grad = jnp.sum(pre_grad, axis=0, dtype=jnp.float32)
    mlp_pull = jax.vjp(layer_norm, middle, mlp_gain_full, mlp_shift_full)[1]
    middle_part, mlp_gain_grad, mlp_shift_grad = mlp_pull(times_transpose(pre_grad, up_full))
    middle_grad = out_grad + middle_part
    proj_in = (branch_scale * middle_grad).astype(jnp.bfloat16)
    proj_weight_grad = transpose_times(attended, proj_in).astype(jnp.bfloat16)
    proj_bias_grad = jnp.sum(proj_in, axis=0, dtype=jnp.float32)
    attended_grad = times_transpose(proj_in, proj_full).astype(jnp.bfloat16)
    grad_own, grad_gone = sides(attended_grad)
    grad_far = across(grad_gone)
    down_order = [core_bit, x_bit, y_bit] + z_bits
    down_sum = begin_sum([down_weight_grad], down_order, me, count)
    updown_order = [core_bit, y_bit, x_bit] + z_bits
    updown_sum = begin_sum([up_weight_grad, proj_weight_grad], updown_order, me, count)
    output = output.astype(jnp.bfloat16)
    grad_own = after(grad_own, down_sum[0], updown_sum[0], output)
    query_grad, pair_grad, pair_gone = attend_backward(
        info, query, pair, out, logsum, grad_own, grad_far
    )
    down_sum = [after(array, query_grad) for array in down_sum]
    updown_sum = [after(array, query_grad) for array in updown_sum]
    down_done = finish_sum(*down_sum, down_order, count)
    updown_done = finish_sum(*updown_sum, updown_order, count)
    pair_grad = add(pair_grad, beside(pair_gone)).astype(jnp.bfloat16)
    mixed_grad = jnp.concatenate([query_grad, pair_grad[0], pair_grad[1]], axis=1)
    normed_grad = times_transpose(mixed_grad, attn_full)
    far_grad = across(normed_grad[row_count:].astype(jnp.bfloat16))
    centered = (everyone[: 2 * row_count] - mean[: 2 * row_count]) * spread[: 2 * row_count]
    attn_gain_grad = jnp.sum(normed_grad * centered, axis=0)
    attn_shift_grad = jnp.sum(normed_grad, axis=0)
    attn_weight_grad = transpose_times(normed_pair, mixed_grad).astype(jnp.bfloat16)
    column_sums = jnp.sum(mixed_grad, axis=0, dtype=jnp.float32).reshape(3, side_count)[::2]
    attn_bias_grad = jnp.where(
        half == 0,
        jnp.pad(column_sums, ((0, 0), (0, side_count))),
        jnp.pad(column_sums, ((0, 0), (side_count, 0))),
    ).reshape(-1)
    scaled = (normed_grad[:row_count] + far_grad.astype(jnp.float32)) * attn_gain_full
    centered_own = centered[:row_count]
    input_part = spread[:row_count] * (
        scaled
        - jnp.mean(scaled, axis=-1, keepdims=True)
        - centered_own * jnp.mean(scaled * centered_own, axis=-1, keepdims=True)
    )
    grad_in = (middle_grad + input_part).astype(jnp.bfloat16)

    vector_grads = [
        attn_gain_grad, attn_shift_grad, attn_bias_grad, proj_bias_grad,
        mlp_gain_grad, mlp_shift_grad, up_bias_grad, down_bias_grad,
    ]
    grad_columns = jnp.concatenate(
        [
            grad.reshape(count, -1, part).transpose(1, 0, 2).reshape(-1, feature_count)
            for grad in vector_grads
        ],
        axis=0,
    ).T
    grad_columns = jnp.pad(grad_columns, ((0, 0), (0, 128 - grad_columns.shape[1])))
    attn_order = [core_bit, x_bit] + z_bits + [y_bit]
    kept, other = begin_sum(
        [attn_weight_grad, grad_columns.astype(jnp.bfloat16)], attn_order, me, count
    )
    for bit in z_bits:
        kept, other = reduce_stage(kept, other, bit, count)
    mine = add(kept[0], other[0])
    other = flip(add(kept[1], other[1]).astype(jnp.bfloat16), y_bit, count).astype(jnp.float32)
    first = jnp.where(half == 0, mine, other)[:, : 3 * side_count].reshape(part, 3, 1, side_count)
    second = jnp.where(half == 0, other, mine)[:, : 3 * side_count].reshape(part, 3, 1, side_count)
    attn_done = jnp.concatenate([first, second], axis=2).reshape(part, 3 * feature_count)
    done_lanes = (mine + other)[:, 3 * side_count :].T
    done_vectors, spot = [], 0
    for vector in vectors:
        size = vector.shape[0] // part
        done_vectors.append(done_lanes[spot : spot + size].reshape(-1))
        spot += size
    return (
        output[None],
        grad_in[None],
        done_vectors[0],
        done_vectors[1],
        attn_done,
        done_vectors[2],
        updown_done[:, ff_count:],
        done_vectors[3],
        done_vectors[4],
        done_vectors[5],
        updown_done[:, :ff_count],
        done_vectors[6],
        down_done,
        done_vectors[7],
    )


def solution(mesh):
    rows = P(AXES)
    tiles = P(AXES, None)
    pack = P(None, AXES, None)
    return jax.shard_map(
        functools.partial(shards, mesh.shape["dp"], mesh.shape["seq"]),
        mesh=mesh,
        in_specs=(
            pack, P(None, AXES), pack, rows, rows, tiles, rows, tiles, rows, rows, rows, tiles,
            rows, tiles, rows,
        ),
        out_specs=(
            pack, pack, rows, rows, tiles, rows, tiles, rows, rows, rows, tiles, rows, tiles, rows,
        ),
        check_vma=False,
    )
```

```python
import functools
import math

import jax
import jax.numpy as jnp
from jax import lax
from jax.experimental import pallas as pl
from jax.experimental.pallas import tpu as pltpu
from jax.sharding import PartitionSpec as P

HD = 64
AXES = ("dp", "seq")

branch_scale = 1.0 / math.sqrt(48.0)
norm_eps = 1e-05
neg_fill = -1e30
head_scale = HD ** (-0.5)


def layer_norm(values, norm_gain, norm_shift):
    center = values - jnp.mean(values, axis=-1, keepdims=True)
    spread = jnp.mean(center * center, axis=-1, keepdims=True)
    return center * lax.rsqrt(spread + norm_eps) * norm_gain + norm_shift


def gelu_tanh(values):
    return jax.nn.gelu(values, approximate=True)


def product(first_op, second_op):
    return jnp.dot(first_op, second_op, preferred_element_type=jnp.float32)


def transpose_times(first_op, second_op):
    return jnp.einsum("tk,tn->kn", first_op, second_op, preferred_element_type=jnp.float32)


def times_transpose(first_op, second_op):
    return jnp.einsum("tn,kn->tk", first_op, second_op, preferred_element_type=jnp.float32)


def flip(array, bit, count):
    return lax.ppermute(array, AXES, [(i, i ^ bit) for i in range(count)])


def distance(place, order):
    return sum(bit for i, bit in enumerate(order) if (place >> i) & 1)


def assemble(pieces, order, me, count):
    size, rows, columns = pieces[0].shape

    def body(me_ref, *refs):
        sources, target, sem = refs[:-2], refs[-2], refs[-1]
        for place in range(count):
            owner = me_ref[0] ^ distance(place, order)
            pltpu.make_async_copy(
                sources[place // size].at[place % size], target.at[owner], sem
            ).start()
        pltpu.make_async_copy(target, target, sem).wait()

    return pl.pallas_call(
        body,
        grid_spec=pltpu.PrefetchScalarGridSpec(
            num_scalar_prefetch=1,
            grid=(1,),
            in_specs=[pl.BlockSpec(memory_space=pl.ANY)] * len(pieces),
            out_specs=pl.BlockSpec((count, rows, columns), lambda i, me_ref: (0, 0, 0)),
            scratch_shapes=[pltpu.SemaphoreType.DMA],
        ),
        out_shape=jax.ShapeDtypeStruct((count, rows, columns), pieces[0].dtype),
        cost_estimate=pl.CostEstimate(
            flops=0, transcendentals=0, bytes_accessed=4 * count * rows * columns
        ),
        name="assemble",
    )(me.reshape(1), *pieces)


def gather_rows(held, order, me, count, ties):
    stages = len(order)
    done = held.shape[0].bit_length() - 1
    for bit in order[done : stages - 2]:
        held = after(held, *ties.get(bit, ()))
        held = jnp.concatenate([held, flip(held, bit, count)], axis=0)
        early = held if bit == order[done] else early
    held = after(held, *ties.get(order[-2], ()))
    near = flip(held, order[-2], count)
    beside = flip(held, order[-1], count)
    near = after(near, *ties.get(order[-1], ()))
    pieces = [held, near, beside, flip(near, order[-1], count)]
    whole = assemble(pieces, order, me, count).reshape(count * held.shape[1], held.shape[2])
    return whole, early


def unpack(packed, parts):
    count, total, rows, columns = packed.shape
    rest = total - parts - 1

    def body(source, side_ref, one_ref, rest_ref, sem):
        pairs = [
            (source.at[:, i], side_ref.at[:, :, pl.ds(i * columns, columns)])
            for i in range(parts)
        ]
        pairs += [(source.at[:, parts], one_ref), (source.at[:, pl.ds(parts + 1, rest)], rest_ref)]
        copies = [
            pltpu.make_async_copy(first, second, sem.at[i])
            for i, (first, second) in enumerate(pairs)
        ]
        for copy in copies:
            copy.start()
        for copy in copies:
            copy.wait()

    shapes = [(count, rows, parts * columns), (count, rows, columns), (count, rest, rows, columns)]
    out = pl.pallas_call(
        body,
        grid=(1,),
        in_specs=[pl.BlockSpec(memory_space=pl.ANY)],
        out_specs=[
            pl.BlockSpec(shape, lambda i, rank=len(shape): (0,) * rank) for shape in shapes
        ],
        scratch_shapes=[pltpu.SemaphoreType.DMA((parts + 2,))],
        out_shape=[jax.ShapeDtypeStruct(shape, packed.dtype) for shape in shapes],
        cost_estimate=pl.CostEstimate(
            flops=0, transcendentals=0, bytes_accessed=4 * count * total * rows * columns
        ),
        name="unpack",
    )(packed)
    return [array.reshape(-1, array.shape[-1]) for array in out]


def disperse(parts, order, me, count):
    rows = parts[0].shape[0] // count
    columns = sum(part.shape[1] for part in parts)
    half = count // 2

    def body(me_ref, *refs):
        sources, (kept, gone, near, far) = refs[: len(parts)], refs[len(parts) : -4]
        near_sem, far_sem, kept_sem, gone_sem = refs[-4:]
        for target, sem, base in ((far, far_sem, half), (near, near_sem, 0)):
            for place in range(half):
                owner, left = me_ref[0] ^ distance(base + place, order[::-1]), 0
                for source in sources:
                    span = slice(left, left + source.shape[2])
                    pltpu.make_async_copy(
                        source.at[owner], target.at[place, :, span], sem
                    ).start()
                    left = span.stop
        pltpu.make_async_copy(far, far, far_sem).wait()
        send = pltpu.make_async_copy(far, gone, gone_sem)
        send.start()
        pltpu.make_async_copy(near, near, near_sem).wait()
        keep = pltpu.make_async_copy(near, kept, kept_sem)
        keep.start()
        send.wait()
        keep.wait()

    shape = (half, rows, columns)
    return pl.pallas_call(
        body,
        grid_spec=pltpu.PrefetchScalarGridSpec(
            num_scalar_prefetch=1,
            grid=(1,),
            in_specs=[pl.BlockSpec(memory_space=pl.ANY)] * len(parts),
            out_specs=[pl.BlockSpec(memory_space=pl.ANY)] * 2,
            scratch_shapes=[pltpu.VMEM(shape, parts[0].dtype)] * 2
            + [pltpu.SemaphoreType.DMA] * 4,
        ),
        out_shape=[jax.ShapeDtypeStruct(shape, parts[0].dtype)] * 2,
        cost_estimate=pl.CostEstimate(
            flops=0, transcendentals=0, bytes_accessed=4 * count * rows * columns
        ),
        name="disperse",
    )(me.reshape(1), *[part.reshape(count, rows, part.shape[1]) for part in parts])


def add(first_term, second_term):
    return first_term.astype(jnp.float32) + second_term.astype(jnp.float32)


def begin_sum(parts, order, me, count):
    kept, gone = disperse(parts, order, me, count)
    return kept, flip(gone, order[0], count), gone


def advance(state, bit, count, *ties):
    kept, other, _ = state
    kept = after(kept, *ties)
    half = kept.shape[0] // 2
    gone = add(kept[half:], other[half:]).astype(jnp.bfloat16)
    kept = add(kept[:half], other[:half]).astype(jnp.bfloat16)
    return kept, flip(gone, bit, count), gone


def after(array, *others):
    return lax.optimization_barrier((array, *others))[0]


def nt(first_op, second_op):
    return lax.dot_general(
        first_op, second_op, (((1,), (1,)), ((), ())), preferred_element_type=jnp.float32
    )


def nn(first_op, second_op):
    return lax.dot_general(
        first_op, second_op, (((1,), (0,)), ((), ())), preferred_element_type=jnp.float32
    )


def lane_mask(shape, axis, head):
    place = lax.broadcasted_iota(jnp.int32, shape, axis)
    return (place < HD) if head == 0 else (place >= HD)


def fwd_kernel(info, q_ref, k_ref, v_ref, o_ref, lse_ref, vt_s, acc_s, m_s):
    which = pl.program_id(1)
    rows, width = q_ref.shape

    @pl.when(which == 0)
    def _():
        for slot in range(4):
            turned = v_ref[slot * rows : (slot + 1) * rows, :].astype(jnp.float32).T
            top = lane_mask((width, rows), 0, 0)
            vt_s[slot, 0] = jnp.where(top, turned, 1.0).astype(jnp.bfloat16)
            vt_s[slot, 1] = jnp.where(top, 1.0, turned).astype(jnp.bfloat16)

    query = q_ref[...] * jnp.bfloat16(head_scale)
    queries = [
        jnp.where(lane_mask((rows, width), 1, head), query, jnp.bfloat16(0)) for head in range(2)
    ]
    block_id = info[which]

    def visit(slot, diagonal):
        keys = k_ref[pl.ds(pl.multiple_of(slot * rows, rows), rows), :]
        for head in range(2):
            scores = nt(keys, queries[head])
            if diagonal:
                below = lax.broadcasted_iota(jnp.int32, (rows, rows), 0) <= (
                    lax.broadcasted_iota(jnp.int32, (rows, rows), 1)
                )
                scores = jnp.where(below, scores, neg_fill)
                peak = jnp.max(scores, axis=0, keepdims=True)
                raised = jnp.exp(scores - peak).astype(jnp.bfloat16)
                acc_s[head] = nn(vt_s[slot, head], raised)
            else:
                before = m_s[head : head + 1, :]
                peak = jnp.maximum(before, jnp.max(scores, axis=0, keepdims=True))
                raised = jnp.exp(scores - peak).astype(jnp.bfloat16)
                acc_s[head] = acc_s[head] * jnp.exp(before - peak) + nn(vt_s[slot, head], raised)
            m_s[head : head + 1, :] = peak

    visit(which, True)

    def step(block, carry):
        visit(info[4 + block], False)
        return carry

    lax.fori_loop(info[2 + which], block_id, step, 0)
    first, second = acc_s[0], acc_s[1]
    total0, total1 = first[HD : HD + 1, :], second[0:1, :]
    out = jnp.where(lane_mask((width, rows), 0, 0), first / total0, second / total1)
    o_ref[...] = out.T.astype(jnp.bfloat16)
    lse_ref[0, 0, 0:1, :] = m_s[0:1, :] + jnp.log(total0)
    lse_ref[0, 0, 1:2, :] = m_s[1:2, :] + jnp.log(total1)


def bwd_kernel(
    info, q_ref, k_ref, v_ref, o_ref, lse_ref, ga_ref, gb_ref, dq_ref, keep_ref, send_ref,
    kt_s, dk_s, dv_s, dq_s,
):
    which = pl.program_id(1)
    rows, width = q_ref.shape

    @pl.when(which == 0)
    def _():
        for slot in range(4):
            keys = k_ref[slot * rows : (slot + 1) * rows, :]
            kt_s[slot] = keys.astype(jnp.float32).T.astype(jnp.bfloat16)
        dk_s[...] = jnp.zeros_like(dk_s)
        dv_s[...] = jnp.zeros_like(dv_s)

    query = q_ref[...] * jnp.bfloat16(head_scale)
    grad = jnp.where(which == 0, ga_ref[...], gb_ref[...])
    joint = (grad.astype(jnp.float32) * o_ref[...].astype(jnp.float32)).T
    queries, grads, dots = [], [], []
    for head in range(2):
        lanes = lane_mask((rows, width), 1, head)
        queries.append(jnp.where(lanes, query, jnp.bfloat16(0)))
        grads.append(jnp.where(lanes, grad, jnp.bfloat16(0)))
        dots.append(jnp.sum(joint[head * HD : (head + 1) * HD], axis=0, keepdims=True))
    block_id = info[which]
    dq_s[...] = jnp.zeros_like(dq_s)

    def visit(slot, diagonal):
        spot = pl.ds(pl.multiple_of(slot * rows, rows), rows)
        keys, values = k_ref[spot, :], v_ref[spot, :]
        for head in range(2):
            scores = nt(keys, queries[head])
            probs = jnp.exp(scores - lse_ref[0, 0, head : head + 1, :])
            if diagonal:
                below = lax.broadcasted_iota(jnp.int32, (rows, rows), 0) <= (
                    lax.broadcasted_iota(jnp.int32, (rows, rows), 1)
                )
                probs = jnp.where(below, probs, 0.0)
            dv_s[slot] += nn(probs.astype(jnp.bfloat16), grads[head])
            pulled = nt(values, grads[head])
            score_grad = (probs * (pulled - dots[head])).astype(jnp.bfloat16)
            dk_s[slot] += nn(score_grad, queries[head])
            part = nn(kt_s[slot], score_grad)
            span = slice(head * HD, (head + 1) * HD)
            dq_s[span, :] += part[span]

    visit(which, True)

    def step(block, carry):
        visit(info[4 + block], False)
        return carry

    lax.fori_loop(info[2 + which], block_id, step, 0)
    dq_ref[...] = (dq_s[...] * head_scale).T.astype(jnp.bfloat16)

    @pl.when(which == 1)
    def _():
        for slot in range(4):
            target = (keep_ref, send_ref)[slot // 2]
            spot = slice((slot % 2) * rows, (slot % 2 + 1) * rows)
            target[0, spot, :] = dk_s[slot].astype(jnp.bfloat16)
            target[1, spot, :] = dv_s[slot].astype(jnp.bfloat16)


def attend_forward(info, query, pair):
    rows, columns = query.shape[0] // 2, query.shape[1]
    width = 2 * HD
    near = columns // width
    return pl.pallas_call(
        fwd_kernel,
        grid_spec=pltpu.PrefetchScalarGridSpec(
            num_scalar_prefetch=1,
            grid=(near, 2),
            in_specs=[
                pl.BlockSpec((rows, width), lambda p, w, s: (w, p)),
                pl.BlockSpec((4 * rows, width), lambda p, w, s: (0, p)),
                pl.BlockSpec((4 * rows, width), lambda p, w, s: (0, near + p)),
            ],
            out_specs=[
                pl.BlockSpec((rows, width), lambda p, w, s: (w, p)),
                pl.BlockSpec((1, 1, 8, rows), lambda p, w, s: (w, p, 0, 0)),
            ],
            scratch_shapes=[
                pltpu.VMEM((4, 2, width, rows), jnp.bfloat16),
                pltpu.VMEM((2, width, rows), jnp.float32),
                pltpu.VMEM((8, rows), jnp.float32),
            ],
        ),
        out_shape=[
            jax.ShapeDtypeStruct((2 * rows, columns), jnp.bfloat16),
            jax.ShapeDtypeStruct((2, near, 8, rows), jnp.float32),
        ],
        cost_estimate=pl.CostEstimate(
            flops=near * 2 * 5 * 4 * rows * rows * width,
            bytes_accessed=16 * rows * columns,
            transcendentals=near * 2 * 5 * rows * rows,
        ),
        name="attend_forward",
    )(info, query, pair, pair)


def attend_backward(info, query, pair, out, logsum, grad_own, grad_far):
    rows, columns = query.shape[0] // 2, query.shape[1]
    width = 2 * HD
    near = columns // width
    return pl.pallas_call(
        bwd_kernel,
        grid_spec=pltpu.PrefetchScalarGridSpec(
            num_scalar_prefetch=1,
            grid=(near, 2),
            in_specs=[
                pl.BlockSpec((rows, width), lambda p, w, s: (w, p)),
                pl.BlockSpec((4 * rows, width), lambda p, w, s: (0, p)),
                pl.BlockSpec((4 * rows, width), lambda p, w, s: (0, near + p)),
                pl.BlockSpec((rows, width), lambda p, w, s: (w, p)),
                pl.BlockSpec((1, 1, 8, rows), lambda p, w, s: (w, p, 0, 0)),
                pl.BlockSpec((rows, width), lambda p, w, s: (0, p)),
                pl.BlockSpec((rows, width), lambda p, w, s: (0, p)),
            ],
            out_specs=[
                pl.BlockSpec((rows, width), lambda p, w, s: (w, p)),
                pl.BlockSpec((2, 2 * rows, width), lambda p, w, s: (0, 0, p)),
                pl.BlockSpec((2, 2 * rows, width), lambda p, w, s: (0, 0, p)),
            ],
            scratch_shapes=[
                pltpu.VMEM((4, width, rows), jnp.bfloat16),
                pltpu.VMEM((4, rows, width), jnp.float32),
                pltpu.VMEM((4, rows, width), jnp.float32),
                pltpu.VMEM((width, rows), jnp.float32),
            ],
        ),
        out_shape=[
            jax.ShapeDtypeStruct((2 * rows, columns), jnp.bfloat16),
            jax.ShapeDtypeStruct((2, 2 * rows, columns), jnp.bfloat16),
            jax.ShapeDtypeStruct((2, 2 * rows, columns), jnp.bfloat16),
        ],
        cost_estimate=pl.CostEstimate(
            flops=near * 2 * 5 * 10 * rows * rows * width,
            bytes_accessed=32 * rows * columns,
            transcendentals=near * 2 * 5 * rows * rows,
        ),
        name="attend_backward",
    )(info, query, pair, pair, out, logsum, grad_own, grad_far)


def shards(
    dp_count, seq_count, tokens, starts, cotangent, attn_gain, attn_shift, attn_weight, attn_bias,
    proj_weight, proj_bias, mlp_gain, mlp_shift, up_weight, up_bias, down_weight, down_bias,
):
    count = dp_count * seq_count
    bits = [1 << i for i in range(count.bit_length() - 1)]
    core_bit, y_bit, x_bit, z_bits = bits[0], bits[1], bits[2], bits[3:]
    place = lax.axis_index("seq")
    me = lax.axis_index("dp") * seq_count + place
    half = place // (seq_count // 2)
    feature_count = tokens.shape[2]
    row_count = tokens.shape[1]
    ff_count = up_weight.shape[1]
    part = feature_count // count
    side_count = feature_count // 2

    def across(array):
        return lax.ppermute(array, "seq", [(i, seq_count - 1 - i) for i in range(seq_count)])

    def beside(array):
        return lax.ppermute(array, "seq", [(i, i ^ 1) for i in range(seq_count)])

    vectors = [attn_gain, attn_shift, attn_bias, proj_bias, mlp_gain, mlp_shift, up_bias, down_bias]
    total = sum(vector.shape[0] for vector in vectors)
    joined, spot = 0, 0
    for vector in vectors:
        joined = joined + jnp.pad(vector, (spot, total - spot - vector.shape[0]))
        spot += vector.shape[0]
    columns = joined.reshape(-1, part).T
    columns = jnp.pad(columns, ((0, 0), (0, 128 - columns.shape[1])))
    thirds = [attn_weight[:, i * side_count : (i + 1) * side_count] for i in range(6)]
    first = jnp.concatenate(thirds[0::2] + [columns], axis=1)
    second = jnp.concatenate(thirds[1::2] + [columns], axis=1)
    mine = jnp.where(half == 0, first, second)
    theirs = flip(jnp.where(half == 0, second, first), y_bit, count)
    ff_parts = ff_count // feature_count
    last_start = starts[0, -128:].reshape(1, 128)
    last_far = across(last_start)
    inputs = tokens[0]
    inputs_far = across(after(inputs, last_far))
    inputs_side = beside(inputs)
    inputs_side_far = beside(inputs_far)
    everyone = jnp.concatenate([inputs, inputs_far, inputs_side, inputs_side_far], axis=0)
    everyone = everyone.astype(jnp.float32)
    mean = jnp.mean(everyone, axis=-1, keepdims=True)
    spread = lax.rsqrt(
        jnp.mean((everyone - mean) * (everyone - mean), axis=-1, keepdims=True) + norm_eps
    )
    attn_all, early = gather_rows(
        jnp.stack([mine, theirs]), [y_bit] + z_bits[::-1] + [x_bit, core_bit], me, count,
        {z_bits[0]: (inputs_side,), x_bit: (inputs_far,), core_bit: (mean, spread)},
    )
    packed = lax.all_gather(
        after(
            jnp.concatenate(
                [
                    up_weight[:, i * feature_count : (i + 1) * feature_count]
                    for i in range(ff_parts)
                ]
                + [proj_weight, down_weight],
                axis=0,
            ),
            early,
        ).reshape(-1, part, feature_count),
        AXES, axis=0,
    )
    up_full, proj_full, down_full = unpack(packed, ff_parts)
    split = jnp.maximum(jnp.max(last_start), jnp.max(last_far)) > 0
    attn_full = attn_all[:, : 3 * side_count]
    lanes = attn_all[:, 3 * side_count :].astype(jnp.float32).T
    full_vectors, spot = [], 0
    for vector in vectors:
        size = vector.shape[0] // part
        rows = lanes[spot : spot + size].reshape(size, count, part)
        full_vectors.append(rows.transpose(1, 0, 2).reshape(-1))
        spot += size
    (
        attn_gain_full, attn_shift_full, attn_bias_full, proj_bias_full,
        mlp_gain_full, mlp_shift_full, up_bias_full, down_bias_full,
    ) = full_vectors

    far_place = seq_count - 1 - place
    spots = jnp.arange(8, dtype=jnp.int32)
    low = jnp.where(split, seq_count // 2, 0).astype(jnp.int32)
    block = spots - 4
    slot = jnp.where(
        block == place,
        0,
        jnp.where(block == far_place, 1, jnp.where(block == (place ^ 1), 2, 3)),
    )
    asked = jnp.where(spots % 2 == 0, place, far_place)
    info = jnp.where(
        spots < 2, asked, jnp.where(spots < 4, jnp.where(asked >= seq_count // 2, low, 0), slot)
    ).astype(jnp.int32)

    normed = (everyone - mean) * spread * attn_gain_full + attn_shift_full
    normed = normed.astype(jnp.bfloat16)
    normed_pair = normed[: 2 * row_count]
    query_bias = lax.dynamic_slice_in_dim(attn_bias_full, half * side_count, side_count)
    value_bias = lax.dynamic_slice_in_dim(
        attn_bias_full, feature_count + half * side_count, side_count
    )
    pair_bias = jnp.concatenate([jnp.zeros((side_count,), jnp.float32), value_bias])
    query = (product(normed_pair, attn_full[:, :side_count]) + query_bias).astype(jnp.bfloat16)
    pair = (product(normed, attn_full[:, side_count:]) + pair_bias).astype(jnp.bfloat16)
    out, logsum = attend_forward(info, query, pair)
    returned = across(out[row_count:])
    out_own = out[:row_count]
    attended = jnp.where(
        half == 0,
        jnp.concatenate([out_own, returned], axis=1),
        jnp.concatenate([returned, out_own], axis=1),
    )
    inputs = inputs.astype(jnp.float32)
    middle = inputs + branch_scale * (product(attended, proj_full) + proj_bias_full)
    normed_mlp = layer_norm(middle, mlp_gain_full, mlp_shift_full).astype(jnp.bfloat16)
    hidden_pre = product(normed_mlp, up_full) + up_bias_full
    hidden = gelu_tanh(hidden_pre).astype(jnp.bfloat16)

    out_grad = cotangent[0].astype(jnp.float32)
    down_in = (branch_scale * out_grad).astype(jnp.bfloat16)
    down_bias_grad = jnp.sum(down_in, axis=0, dtype=jnp.float32)
    orders = [core_bit, x_bit, y_bit] + z_bits
    down_weight_grad = transpose_times(hidden, down_in).astype(jnp.bfloat16)
    down_sum = begin_sum([down_weight_grad], orders, me, count)
    hidden_grad = times_transpose(after(down_in, down_sum[2]), down_full)
    gelu_pull = jax.vjp(gelu_tanh, hidden_pre)[1]
    pre_grad = gelu_pull(hidden_grad)[0].astype(jnp.bfloat16)
    down_sum = advance(down_sum, orders[1], count, pre_grad)
    up_bias_grad = jnp.sum(pre_grad, axis=0, dtype=jnp.float32)
    mlp_pull = jax.vjp(layer_norm, middle, mlp_gain_full, mlp_shift_full)[1]
    middle_part, mlp_gain_grad, mlp_shift_grad = mlp_pull(
        times_transpose(after(pre_grad, down_sum[2]), up_full)
    )
    middle_grad = out_grad + middle_part
    proj_in = (branch_scale * middle_grad).astype(jnp.bfloat16)
    proj_bias_grad = jnp.sum(proj_in, axis=0, dtype=jnp.float32)
    proj_mine = lax.dynamic_slice_in_dim(proj_full, half * side_count, side_count)
    proj_theirs = lax.dynamic_slice_in_dim(proj_full, (1 - half) * side_count, side_count)
    grad_gone = times_transpose(proj_in, proj_theirs).astype(jnp.bfloat16)
    grad_far = across(grad_gone)
    grad_own = times_transpose(proj_in, proj_mine).astype(jnp.bfloat16)
    up_weight_grad = transpose_times(normed_mlp, after(pre_grad, grad_gone)).astype(jnp.bfloat16)
    proj_weight_grad = transpose_times(attended, after(proj_in, grad_gone)).astype(jnp.bfloat16)
    updown_sum = begin_sum([up_weight_grad, proj_weight_grad], orders, me, count)
    down_sum = advance(down_sum, orders[2], count, updown_sum[2])
    updown_sum = advance(updown_sum, orders[1], count, down_sum[2])
    query_grad, pair_grad, pair_gone = attend_backward(
        info, query, pair, out, logsum, after(grad_own, updown_sum[2]), grad_far
    )
    down_sum = advance(down_sum, orders[3], count, query_grad)
    updown_sum = advance(updown_sum, orders[2], count, query_grad, down_sum[2])
    pair_grad = add(after(pair_grad, updown_sum[2]), beside(pair_gone)).astype(jnp.bfloat16)
    mixed_grad = jnp.concatenate([query_grad, pair_grad[0], pair_grad[1]], axis=1)
    normed_grad = times_transpose(mixed_grad, attn_full)
    far_grad = across(normed_grad[row_count:].astype(jnp.bfloat16))
    centered = (everyone[: 2 * row_count] - mean[: 2 * row_count]) * spread[: 2 * row_count]
    attn_gain_grad = jnp.sum(normed_grad * centered, axis=0)
    attn_shift_grad = jnp.sum(normed_grad, axis=0)
    attn_weight_grad = transpose_times(normed_pair, mixed_grad).astype(jnp.bfloat16)
    column_sums = jnp.sum(mixed_grad, axis=0, dtype=jnp.float32).reshape(3, side_count)[::2]
    attn_bias_grad = jnp.where(
        half == 0,
        jnp.pad(column_sums, ((0, 0), (0, side_count))),
        jnp.pad(column_sums, ((0, 0), (side_count, 0))),
    ).reshape(-1)
    scaled = (normed_grad[:row_count] + far_grad.astype(jnp.float32)) * attn_gain_full
    centered_own = centered[:row_count]
    input_part = spread[:row_count] * (
        scaled
        - jnp.mean(scaled, axis=-1, keepdims=True)
        - centered_own * jnp.mean(scaled * centered_own, axis=-1, keepdims=True)
    )
    grad_in = (middle_grad + input_part).astype(jnp.bfloat16)

    vector_grads = [
        attn_gain_grad, attn_shift_grad, attn_bias_grad, proj_bias_grad,
        mlp_gain_grad, mlp_shift_grad, up_bias_grad, down_bias_grad,
    ]
    grad_columns = jnp.concatenate(
        [
            grad.reshape(count, -1, part).transpose(1, 0, 2).reshape(-1, feature_count)
            for grad in vector_grads
        ],
        axis=0,
    ).T
    grad_columns = jnp.pad(grad_columns, ((0, 0), (0, 128 - grad_columns.shape[1])))
    attn_order = [core_bit, x_bit] + z_bits + [y_bit]
    attn_sum = begin_sum(
        [attn_weight_grad, grad_columns.astype(jnp.bfloat16)], attn_order, me, count
    )
    for bit in orders[4:]:
        down_sum = advance(down_sum, bit, count, attn_sum[2])
    attn_sum = advance(attn_sum, x_bit, count, down_sum[2])
    output = middle + branch_scale * (
        product(after(hidden, attn_sum[2]), down_full) + down_bias_full
    )
    output = output.astype(jnp.bfloat16)
    updown_sum = advance(updown_sum, orders[3], count, output)
    down_done = add(down_sum[0][0], after(down_sum[1], updown_sum[2])[0])
    for i, bit in enumerate(z_bits):
        attn_sum = advance(attn_sum, bit, count, updown_sum[2])
        if i + 1 < len(z_bits):
            updown_sum = advance(updown_sum, orders[4 + i], count, attn_sum[2])
    updown_done = add(updown_sum[0][0], after(updown_sum[1], attn_sum[2])[0])
    mine = add(attn_sum[0][0], attn_sum[1][0])
    other = add(attn_sum[0][1], attn_sum[1][1]).astype(jnp.bfloat16)
    other = flip(other, y_bit, count).astype(jnp.float32)
    first = jnp.where(half == 0, mine, other)[:, : 3 * side_count].reshape(part, 3, 1, side_count)
    second = jnp.where(half == 0, other, mine)[:, : 3 * side_count].reshape(part, 3, 1, side_count)
    attn_done = jnp.concatenate([first, second], axis=2).reshape(part, 3 * feature_count)
    done_lanes = (mine + other)[:, 3 * side_count :].T
    done_vectors, spot = [], 0
    for vector in vectors:
        size = vector.shape[0] // part
        done_vectors.append(done_lanes[spot : spot + size].reshape(-1))
        spot += size
    return (
        output[None],
        grad_in[None],
        done_vectors[0],
        done_vectors[1],
        attn_done,
        done_vectors[2],
        updown_done[:, ff_count:],
        done_vectors[3],
        done_vectors[4],
        done_vectors[5],
        updown_done[:, :ff_count],
        done_vectors[6],
        down_done,
        done_vectors[7],
    )


def solution(mesh):
    rows = P(AXES)
    tiles = P(AXES, None)
    pack = P(None, AXES, None)
    return jax.shard_map(
        functools.partial(shards, mesh.shape["dp"], mesh.shape["seq"]),
        mesh=mesh,
        in_specs=(
            pack, P(None, AXES), pack, rows, rows, tiles, rows, tiles, rows, rows, rows, tiles,
            rows, tiles, rows,
        ),
        out_specs=(
            pack, pack, rows, rows, tiles, rows, tiles, rows, rows, rows, tiles, rows, tiles, rows,
        ),
        check_vma=False,
    )
```

```python
import functools
import math

import jax
import jax.numpy as jnp
from jax import lax
from jax.experimental import pallas as pl
from jax.experimental.pallas import tpu as pltpu
from jax.sharding import PartitionSpec as P

HD = 64
AXES = ("dp", "seq")

branch_scale = 1.0 / math.sqrt(48.0)
norm_eps = 1e-05
neg_fill = -1e30
head_scale = HD ** (-0.5)


def layer_norm(values, norm_gain, norm_shift):
    center = values - jnp.mean(values, axis=-1, keepdims=True)
    spread = jnp.mean(center * center, axis=-1, keepdims=True)
    return center * lax.rsqrt(spread + norm_eps) * norm_gain + norm_shift


def gelu_and_slope(values):
    scale = math.sqrt(2.0 / math.pi)
    square = values * values
    bend = jnp.tanh(scale * values * (1.0 + 0.044715 * square))
    gate = 0.5 * (1.0 + bend)
    rise = scale * (1.0 + 3.0 * 0.044715 * square)
    return values * gate, gate + 0.5 * values * (1.0 - bend * bend) * rise


def product(first_op, second_op):
    return jnp.dot(first_op, second_op, preferred_element_type=jnp.float32)


def transpose_times(first_op, second_op):
    return jnp.einsum("tk,tn->kn", first_op, second_op, preferred_element_type=jnp.float32)


def times_transpose(first_op, second_op):
    return jnp.einsum("tn,kn->tk", first_op, second_op, preferred_element_type=jnp.float32)


def flip(array, bit, count):
    return lax.ppermute(array, AXES, [(i, i ^ bit) for i in range(count)])


def distance(place, order):
    return sum(bit for i, bit in enumerate(order) if (place >> i) & 1)


def assemble(pieces, order, me, count):
    size, rows, columns = pieces[0].shape

    def body(me_ref, *refs):
        sources, target, sem = refs[:-2], refs[-2], refs[-1]
        for place in range(count):
            owner = me_ref[0] ^ distance(place, order)
            pltpu.make_async_copy(
                sources[place // size].at[place % size], target.at[owner], sem
            ).start()
        pltpu.make_async_copy(target, target, sem).wait()

    return pl.pallas_call(
        body,
        grid_spec=pltpu.PrefetchScalarGridSpec(
            num_scalar_prefetch=1,
            grid=(1,),
            in_specs=[pl.BlockSpec(memory_space=pl.ANY)] * len(pieces),
            out_specs=pl.BlockSpec((count, rows, columns), lambda i, me_ref: (0, 0, 0)),
            scratch_shapes=[pltpu.SemaphoreType.DMA],
        ),
        out_shape=jax.ShapeDtypeStruct((count, rows, columns), pieces[0].dtype),
        cost_estimate=pl.CostEstimate(
            flops=0, transcendentals=0, bytes_accessed=4 * count * rows * columns
        ),
        name="assemble",
    )(me.reshape(1), *pieces)


def gather_rows(held, order, me, count, ties):
    stages = len(order)
    done = held.shape[0].bit_length() - 1
    for bit in order[done : stages - 2]:
        held = after(held, *ties.get(bit, ()))
        held = jnp.concatenate([held, flip(held, bit, count)], axis=0)
        early = held if bit == order[done] else early
    held = after(held, *ties.get(order[-2], ()))
    near = flip(held, order[-2], count)
    beside = flip(held, order[-1], count)
    near = after(near, *ties.get(order[-1], ()))
    pieces = [held, near, beside, flip(near, order[-1], count)]
    whole = assemble(pieces, order, me, count).reshape(count * held.shape[1], held.shape[2])
    return whole, early


def unpack(packed, parts):
    count, total, rows, columns = packed.shape
    rest = total - parts - 1

    def body(source, side_ref, one_ref, rest_ref, sem):
        pairs = [
            (source.at[:, i], side_ref.at[:, :, pl.ds(i * columns, columns)])
            for i in range(parts)
        ]
        pairs += [(source.at[:, parts], one_ref), (source.at[:, pl.ds(parts + 1, rest)], rest_ref)]
        copies = [
            pltpu.make_async_copy(first, second, sem.at[i])
            for i, (first, second) in enumerate(pairs)
        ]
        for copy in copies:
            copy.start()
        for copy in copies:
            copy.wait()

    shapes = [(count, rows, parts * columns), (count, rows, columns), (count, rest, rows, columns)]
    out = pl.pallas_call(
        body,
        grid=(1,),
        in_specs=[pl.BlockSpec(memory_space=pl.ANY)],
        out_specs=[
            pl.BlockSpec(shape, lambda i, rank=len(shape): (0,) * rank) for shape in shapes
        ],
        scratch_shapes=[pltpu.SemaphoreType.DMA((parts + 2,))],
        out_shape=[jax.ShapeDtypeStruct(shape, packed.dtype) for shape in shapes],
        cost_estimate=pl.CostEstimate(
            flops=0, transcendentals=0, bytes_accessed=4 * count * total * rows * columns
        ),
        name="unpack",
    )(packed)
    return [array.reshape(-1, array.shape[-1]) for array in out]


def disperse(parts, order, me, count):
    rows = parts[0].shape[0] // count
    columns = sum(part.shape[1] for part in parts)
    half = count // 2

    def body(me_ref, *refs):
        sources, (kept, gone, near, far) = refs[: len(parts)], refs[len(parts) : -4]
        near_sem, far_sem, kept_sem, gone_sem = refs[-4:]
        for target, sem, base in ((far, far_sem, half), (near, near_sem, 0)):
            for place in range(half):
                owner, left = me_ref[0] ^ distance(base + place, order[::-1]), 0
                for source in sources:
                    span = slice(left, left + source.shape[2])
                    pltpu.make_async_copy(
                        source.at[owner], target.at[place, :, span], sem
                    ).start()
                    left = span.stop
        pltpu.make_async_copy(far, far, far_sem).wait()
        send = pltpu.make_async_copy(far, gone, gone_sem)
        send.start()
        pltpu.make_async_copy(near, near, near_sem).wait()
        keep = pltpu.make_async_copy(near, kept, kept_sem)
        keep.start()
        send.wait()
        keep.wait()

    shape = (half, rows, columns)
    return pl.pallas_call(
        body,
        grid_spec=pltpu.PrefetchScalarGridSpec(
            num_scalar_prefetch=1,
            grid=(1,),
            in_specs=[pl.BlockSpec(memory_space=pl.ANY)] * len(parts),
            out_specs=[pl.BlockSpec(memory_space=pl.ANY)] * 2,
            scratch_shapes=[pltpu.VMEM(shape, parts[0].dtype)] * 2
            + [pltpu.SemaphoreType.DMA] * 4,
        ),
        out_shape=[jax.ShapeDtypeStruct(shape, parts[0].dtype)] * 2,
        cost_estimate=pl.CostEstimate(
            flops=0, transcendentals=0, bytes_accessed=4 * count * rows * columns
        ),
        name="disperse",
    )(me.reshape(1), *[part.reshape(count, rows, part.shape[1]) for part in parts])


def add(first_term, second_term):
    return first_term.astype(jnp.float32) + second_term.astype(jnp.float32)


def begin_sum(parts, order, me, count):
    kept, gone = disperse(parts, order, me, count)
    return kept, flip(gone, order[0], count), gone


def advance(state, bit, count, *ties):
    kept, other, _ = state
    kept = after(kept, *ties)
    half = kept.shape[0] // 2
    gone = add(kept[half:], other[half:]).astype(jnp.bfloat16)
    kept = add(kept[:half], other[:half]).astype(jnp.bfloat16)
    return kept, flip(gone, bit, count), gone


def after(array, *others):
    return lax.optimization_barrier((array, *others))[0]


def nt(first_op, second_op):
    return lax.dot_general(
        first_op, second_op, (((1,), (1,)), ((), ())), preferred_element_type=jnp.float32
    )


def nn(first_op, second_op):
    return lax.dot_general(
        first_op, second_op, (((1,), (0,)), ((), ())), preferred_element_type=jnp.float32
    )


def lane_mask(shape, axis, head):
    place = lax.broadcasted_iota(jnp.int32, shape, axis)
    return (place < HD) if head == 0 else (place >= HD)


def fwd_kernel(info, q_ref, k_ref, v_ref, o_ref, lse_ref, vt_s, acc_s, m_s):
    which = pl.program_id(1)
    rows, width = q_ref.shape

    @pl.when(which == 0)
    def _():
        for slot in range(4):
            turned = v_ref[slot * rows : (slot + 1) * rows, :].astype(jnp.float32).T
            top = lane_mask((width, rows), 0, 0)
            vt_s[slot, 0] = jnp.where(top, turned, 1.0).astype(jnp.bfloat16)
            vt_s[slot, 1] = jnp.where(top, 1.0, turned).astype(jnp.bfloat16)

    query = q_ref[...] * jnp.bfloat16(head_scale)
    queries = [
        jnp.where(lane_mask((rows, width), 1, head), query, jnp.bfloat16(0)) for head in range(2)
    ]
    block_id = info[which]

    def visit(slot, diagonal):
        keys = k_ref[pl.ds(pl.multiple_of(slot * rows, rows), rows), :]
        for head in range(2):
            scores = nt(keys, queries[head])
            if diagonal:
                below = lax.broadcasted_iota(jnp.int32, (rows, rows), 0) <= (
                    lax.broadcasted_iota(jnp.int32, (rows, rows), 1)
                )
                scores = jnp.where(below, scores, neg_fill)
                peak = jnp.max(scores, axis=0, keepdims=True)
                raised = jnp.exp(scores - peak).astype(jnp.bfloat16)
                acc_s[head] = nn(vt_s[slot, head], raised)
            else:
                before = m_s[head : head + 1, :]
                peak = jnp.maximum(before, jnp.max(scores, axis=0, keepdims=True))
                raised = jnp.exp(scores - peak).astype(jnp.bfloat16)
                acc_s[head] = acc_s[head] * jnp.exp(before - peak) + nn(vt_s[slot, head], raised)
            m_s[head : head + 1, :] = peak

    visit(which, True)

    def step(block, carry):
        visit(info[4 + block], False)
        return carry

    lax.fori_loop(info[2 + which], block_id, step, 0)
    first, second = acc_s[0], acc_s[1]
    total0, total1 = first[HD : HD + 1, :], second[0:1, :]
    out = jnp.where(lane_mask((width, rows), 0, 0), first / total0, second / total1)
    o_ref[...] = out.T.astype(jnp.bfloat16)
    lse_ref[0, 0, 0:1, :] = m_s[0:1, :] + jnp.log(total0)
    lse_ref[0, 0, 1:2, :] = m_s[1:2, :] + jnp.log(total1)


def bwd_kernel(
    info, q_ref, k_ref, v_ref, o_ref, lse_ref, ga_ref, gb_ref, dq_ref, keep_ref, send_ref,
    kt_s, dk_s, dv_s, dq_s,
):
    which = pl.program_id(1)
    rows, width = q_ref.shape

    @pl.when(which == 0)
    def _():
        for slot in range(4):
            keys = k_ref[slot * rows : (slot + 1) * rows, :]
            kt_s[slot] = keys.astype(jnp.float32).T.astype(jnp.bfloat16)
        dk_s[...] = jnp.zeros_like(dk_s)
        dv_s[...] = jnp.zeros_like(dv_s)

    query = q_ref[...] * jnp.bfloat16(head_scale)
    grad = jnp.where(which == 0, ga_ref[...], gb_ref[...])
    joint = (grad.astype(jnp.float32) * o_ref[...].astype(jnp.float32)).T
    queries, grads, dots = [], [], []
    for head in range(2):
        lanes = lane_mask((rows, width), 1, head)
        queries.append(jnp.where(lanes, query, jnp.bfloat16(0)))
        grads.append(jnp.where(lanes, grad, jnp.bfloat16(0)))
        dots.append(jnp.sum(joint[head * HD : (head + 1) * HD], axis=0, keepdims=True))
    block_id = info[which]
    dq_s[...] = jnp.zeros_like(dq_s)

    def visit(slot, diagonal):
        spot = pl.ds(pl.multiple_of(slot * rows, rows), rows)
        keys, values = k_ref[spot, :], v_ref[spot, :]
        for head in range(2):
            scores = nt(keys, queries[head])
            probs = jnp.exp(scores - lse_ref[0, 0, head : head + 1, :])
            if diagonal:
                below = lax.broadcasted_iota(jnp.int32, (rows, rows), 0) <= (
                    lax.broadcasted_iota(jnp.int32, (rows, rows), 1)
                )
                probs = jnp.where(below, probs, 0.0)
            dv_s[slot] += nn(probs.astype(jnp.bfloat16), grads[head])
            pulled = nt(values, grads[head])
            score_grad = (probs * (pulled - dots[head])).astype(jnp.bfloat16)
            dk_s[slot] += nn(score_grad, queries[head])
            part = nn(kt_s[slot], score_grad)
            span = slice(head * HD, (head + 1) * HD)
            dq_s[span, :] += part[span]

    visit(which, True)

    def step(block, carry):
        visit(info[4 + block], False)
        return carry

    lax.fori_loop(info[2 + which], block_id, step, 0)
    dq_ref[...] = (dq_s[...] * head_scale).T.astype(jnp.bfloat16)

    @pl.when(which == 1)
    def _():
        for slot in range(4):
            target = (keep_ref, send_ref)[slot // 2]
            spot = slice((slot % 2) * rows, (slot % 2 + 1) * rows)
            target[0, spot, :] = dk_s[slot].astype(jnp.bfloat16)
            target[1, spot, :] = dv_s[slot].astype(jnp.bfloat16)


def attend_forward(info, query, pair):
    rows, columns = query.shape[0] // 2, query.shape[1]
    width = 2 * HD
    near = columns // width
    return pl.pallas_call(
        fwd_kernel,
        grid_spec=pltpu.PrefetchScalarGridSpec(
            num_scalar_prefetch=1,
            grid=(near, 2),
            in_specs=[
                pl.BlockSpec((rows, width), lambda p, w, s: (w, p)),
                pl.BlockSpec((4 * rows, width), lambda p, w, s: (0, p)),
                pl.BlockSpec((4 * rows, width), lambda p, w, s: (0, near + p)),
            ],
            out_specs=[
                pl.BlockSpec((rows, width), lambda p, w, s: (w, p)),
                pl.BlockSpec((1, 1, 8, rows), lambda p, w, s: (w, p, 0, 0)),
            ],
            scratch_shapes=[
                pltpu.VMEM((4, 2, width, rows), jnp.bfloat16),
                pltpu.VMEM((2, width, rows), jnp.float32),
                pltpu.VMEM((8, rows), jnp.float32),
            ],
        ),
        out_shape=[
            jax.ShapeDtypeStruct((2 * rows, columns), jnp.bfloat16),
            jax.ShapeDtypeStruct((2, near, 8, rows), jnp.float32),
        ],
        cost_estimate=pl.CostEstimate(
            flops=near * 2 * 5 * 4 * rows * rows * width,
            bytes_accessed=16 * rows * columns,
            transcendentals=near * 2 * 5 * rows * rows,
        ),
        name="attend_forward",
    )(info, query, pair, pair)


def attend_backward(info, query, pair, out, logsum, grad_own, grad_far):
    rows, columns = query.shape[0] // 2, query.shape[1]
    width = 2 * HD
    near = columns // width
    return pl.pallas_call(
        bwd_kernel,
        grid_spec=pltpu.PrefetchScalarGridSpec(
            num_scalar_prefetch=1,
            grid=(near, 2),
            in_specs=[
                pl.BlockSpec((rows, width), lambda p, w, s: (w, p)),
                pl.BlockSpec((4 * rows, width), lambda p, w, s: (0, p)),
                pl.BlockSpec((4 * rows, width), lambda p, w, s: (0, near + p)),
                pl.BlockSpec((rows, width), lambda p, w, s: (w, p)),
                pl.BlockSpec((1, 1, 8, rows), lambda p, w, s: (w, p, 0, 0)),
                pl.BlockSpec((rows, width), lambda p, w, s: (0, p)),
                pl.BlockSpec((rows, width), lambda p, w, s: (0, p)),
            ],
            out_specs=[
                pl.BlockSpec((rows, width), lambda p, w, s: (w, p)),
                pl.BlockSpec((2, 2 * rows, width), lambda p, w, s: (0, 0, p)),
                pl.BlockSpec((2, 2 * rows, width), lambda p, w, s: (0, 0, p)),
            ],
            scratch_shapes=[
                pltpu.VMEM((4, width, rows), jnp.bfloat16),
                pltpu.VMEM((4, rows, width), jnp.float32),
                pltpu.VMEM((4, rows, width), jnp.float32),
                pltpu.VMEM((width, rows), jnp.float32),
            ],
        ),
        out_shape=[
            jax.ShapeDtypeStruct((2 * rows, columns), jnp.bfloat16),
            jax.ShapeDtypeStruct((2, 2 * rows, columns), jnp.bfloat16),
            jax.ShapeDtypeStruct((2, 2 * rows, columns), jnp.bfloat16),
        ],
        cost_estimate=pl.CostEstimate(
            flops=near * 2 * 5 * 10 * rows * rows * width,
            bytes_accessed=32 * rows * columns,
            transcendentals=near * 2 * 5 * rows * rows,
        ),
        name="attend_backward",
    )(info, query, pair, pair, out, logsum, grad_own, grad_far)


def shards(
    dp_count, seq_count, tokens, starts, cotangent, attn_gain, attn_shift, attn_weight, attn_bias,
    proj_weight, proj_bias, mlp_gain, mlp_shift, up_weight, up_bias, down_weight, down_bias,
):
    count = dp_count * seq_count
    bits = [1 << i for i in range(count.bit_length() - 1)]
    core_bit, y_bit, x_bit, z_bits = bits[0], bits[1], bits[2], bits[3:]
    place = lax.axis_index("seq")
    me = lax.axis_index("dp") * seq_count + place
    half = place // (seq_count // 2)
    feature_count = tokens.shape[2]
    row_count = tokens.shape[1]
    ff_count = up_weight.shape[1]
    part = feature_count // count
    side_count = feature_count // 2

    def across(array):
        return lax.ppermute(array, "seq", [(i, seq_count - 1 - i) for i in range(seq_count)])

    def beside(array):
        return lax.ppermute(array, "seq", [(i, i ^ 1) for i in range(seq_count)])

    vectors = [attn_gain, attn_shift, attn_bias, proj_bias, mlp_gain, mlp_shift, up_bias, down_bias]
    total = sum(vector.shape[0] for vector in vectors)
    joined, spot = 0, 0
    for vector in vectors:
        joined = joined + jnp.pad(vector, (spot, total - spot - vector.shape[0]))
        spot += vector.shape[0]
    columns = joined.reshape(-1, part).T
    columns = jnp.pad(columns, ((0, 0), (0, 128 - columns.shape[1])))
    thirds = [attn_weight[:, i * side_count : (i + 1) * side_count] for i in range(6)]
    first = jnp.concatenate(thirds[0::2] + [columns], axis=1)
    second = jnp.concatenate(thirds[1::2] + [columns], axis=1)
    mine = jnp.where(half == 0, first, second)
    theirs = flip(jnp.where(half == 0, second, first), y_bit, count)
    ff_parts = ff_count // feature_count
    last_start = starts[0, -128:].reshape(1, 128)
    last_far = across(last_start)
    inputs = tokens[0]
    inputs_far = across(after(inputs, last_far))
    inputs_side = beside(inputs)
    inputs_side_far = beside(inputs_far)
    everyone_low = lax.optimization_barrier(
        jnp.concatenate([inputs, inputs_far, inputs_side, inputs_side_far], axis=0)
    )
    everyone = everyone_low.astype(jnp.float32)
    mean = jnp.mean(everyone, axis=-1, keepdims=True)
    spread = lax.rsqrt(
        jnp.mean((everyone - mean) * (everyone - mean), axis=-1, keepdims=True) + norm_eps
    )
    attn_all, early = gather_rows(
        jnp.stack([mine, theirs]), [y_bit] + z_bits[::-1] + [x_bit, core_bit], me, count,
        {core_bit: (mean, spread)},
    )
    packed = lax.all_gather(
        after(
            jnp.concatenate(
                [
                    up_weight[:, i * feature_count : (i + 1) * feature_count]
                    for i in range(ff_parts)
                ]
                + [proj_weight, down_weight],
                axis=0,
            ),
            early,
        ).reshape(-1, part, feature_count),
        AXES, axis=0,
    )
    up_full, proj_full, down_full = unpack(packed, ff_parts)
    split = jnp.maximum(jnp.max(last_start), jnp.max(last_far)) > 0
    attn_full = attn_all[:, : 3 * side_count]
    lanes = attn_all[:, 3 * side_count :].astype(jnp.float32).T
    full_vectors, spot = [], 0
    for vector in vectors:
        size = vector.shape[0] // part
        rows = lanes[spot : spot + size].reshape(size, count, part)
        full_vectors.append(rows.transpose(1, 0, 2).reshape(-1))
        spot += size
    (
        attn_gain_full, attn_shift_full, attn_bias_full, proj_bias_full,
        mlp_gain_full, mlp_shift_full, up_bias_full, down_bias_full,
    ) = full_vectors

    far_place = seq_count - 1 - place
    spots = jnp.arange(8, dtype=jnp.int32)
    low = jnp.where(split, seq_count // 2, 0).astype(jnp.int32)
    block = spots - 4
    slot = jnp.where(
        block == place,
        0,
        jnp.where(block == far_place, 1, jnp.where(block == (place ^ 1), 2, 3)),
    )
    asked = jnp.where(spots % 2 == 0, place, far_place)
    info = jnp.where(
        spots < 2, asked, jnp.where(spots < 4, jnp.where(asked >= seq_count // 2, low, 0), slot)
    ).astype(jnp.int32)

    normed = (everyone - mean) * spread * attn_gain_full + attn_shift_full
    normed = normed.astype(jnp.bfloat16)
    normed_pair = normed[: 2 * row_count]
    query_bias = lax.dynamic_slice_in_dim(attn_bias_full, half * side_count, side_count)
    value_bias = lax.dynamic_slice_in_dim(
        attn_bias_full, feature_count + half * side_count, side_count
    )
    pair_bias = jnp.concatenate([jnp.zeros((side_count,), jnp.float32), value_bias])
    query = (product(normed_pair, attn_full[:, :side_count]) + query_bias).astype(jnp.bfloat16)
    pair = (product(normed, attn_full[:, side_count:]) + pair_bias).astype(jnp.bfloat16)
    out, logsum = attend_forward(info, query, pair)
    returned = across(out[row_count:])
    out_own = out[:row_count]
    attended = jnp.where(
        half == 0,
        jnp.concatenate([out_own, returned], axis=1),
        jnp.concatenate([returned, out_own], axis=1),
    )
    inputs = inputs.astype(jnp.float32)
    middle = inputs + branch_scale * (product(attended, proj_full) + proj_bias_full)
    normed_mlp = layer_norm(middle, mlp_gain_full, mlp_shift_full).astype(jnp.bfloat16)
    hidden_pre = product(normed_mlp, up_full) + up_bias_full
    hidden, slope = gelu_and_slope(hidden_pre)
    hidden, slope = lax.optimization_barrier(
        (hidden.astype(jnp.bfloat16), slope.astype(jnp.bfloat16))
    )

    out_grad = cotangent[0].astype(jnp.float32)
    down_in = (branch_scale * out_grad).astype(jnp.bfloat16)
    down_bias_grad = jnp.sum(down_in, axis=0, dtype=jnp.float32)
    down_order = [core_bit, x_bit, y_bit] + z_bits
    up_order = [core_bit, y_bit, x_bit] + z_bits
    down_weight_grad = transpose_times(hidden, down_in).astype(jnp.bfloat16)
    down_sum = begin_sum([down_weight_grad], down_order, me, count)
    hidden_grad = times_transpose(after(down_in, down_sum[2]), down_full)
    pre_grad = (hidden_grad * slope.astype(jnp.float32)).astype(jnp.bfloat16)
    down_sum = advance(down_sum, down_order[1], count, pre_grad)
    up_bias_grad = jnp.sum(pre_grad, axis=0, dtype=jnp.float32)
    mlp_pull = jax.vjp(layer_norm, middle, mlp_gain_full, mlp_shift_full)[1]
    middle_part, mlp_gain_grad, mlp_shift_grad = mlp_pull(
        times_transpose(after(pre_grad, down_sum[2]), up_full)
    )
    middle_grad = out_grad + middle_part
    proj_in = (branch_scale * middle_grad).astype(jnp.bfloat16)
    proj_bias_grad = jnp.sum(proj_in, axis=0, dtype=jnp.float32)
    proj_mine = lax.dynamic_slice_in_dim(proj_full, half * side_count, side_count)
    proj_theirs = lax.dynamic_slice_in_dim(proj_full, (1 - half) * side_count, side_count)
    grad_gone = times_transpose(proj_in, proj_theirs).astype(jnp.bfloat16)
    grad_far = across(grad_gone)
    grad_own = times_transpose(proj_in, proj_mine).astype(jnp.bfloat16)
    up_weight_grad = transpose_times(normed_mlp, after(pre_grad, grad_gone)).astype(jnp.bfloat16)
    proj_weight_grad = transpose_times(attended, after(proj_in, grad_gone)).astype(jnp.bfloat16)
    up_sum = begin_sum([up_weight_grad, proj_weight_grad], up_order, me, count)
    up_sum = advance(up_sum, up_order[1], count)
    query_grad, pair_grad, pair_gone = attend_backward(
        info, query, pair, out, logsum, after(grad_own, up_sum[2]), grad_far
    )
    down_sum = advance(down_sum, down_order[2], count, query_grad)
    pair_grad = add(after(pair_grad, down_sum[2]), beside(pair_gone)).astype(jnp.bfloat16)
    mixed_grad = jnp.concatenate([query_grad, pair_grad[0], pair_grad[1]], axis=1)
    normed_grad = times_transpose(mixed_grad, attn_full)
    far_grad = normed_grad[row_count:].astype(jnp.bfloat16)
    up_sum = advance(up_sum, up_order[2], count, far_grad)
    far_grad = across(far_grad)
    centered = after(everyone_low[: 2 * row_count], query_grad).astype(jnp.float32)
    centered = (centered - mean[: 2 * row_count]) * spread[: 2 * row_count]
    attn_gain_grad = jnp.sum(normed_grad * centered, axis=0)
    attn_shift_grad = jnp.sum(normed_grad, axis=0)
    attn_weight_grad = transpose_times(normed_pair, after(mixed_grad, up_sum[2])).astype(jnp.bfloat16)
    column_sums = jnp.sum(mixed_grad, axis=0, dtype=jnp.float32).reshape(3, side_count)[::2]
    attn_bias_grad = jnp.where(
        half == 0,
        jnp.pad(column_sums, ((0, 0), (0, side_count))),
        jnp.pad(column_sums, ((0, 0), (side_count, 0))),
    ).reshape(-1)
    vector_grads = [
        attn_gain_grad, attn_shift_grad, attn_bias_grad, proj_bias_grad,
        mlp_gain_grad, mlp_shift_grad, up_bias_grad, down_bias_grad,
    ]
    grad_columns = jnp.concatenate(
        [
            grad.reshape(count, -1, part).transpose(1, 0, 2).reshape(-1, feature_count)
            for grad in vector_grads
        ],
        axis=0,
    ).T
    grad_columns = jnp.pad(grad_columns, ((0, 0), (0, 128 - grad_columns.shape[1])))
    attn_order = [core_bit, x_bit] + z_bits + [y_bit]
    attn_sum = begin_sum(
        [attn_weight_grad, grad_columns.astype(jnp.bfloat16)], attn_order, me, count
    )
    down_sum = advance(down_sum, down_order[3], count, attn_sum[2])
    attn_sum = advance(attn_sum, attn_order[1], count, down_sum[2])
    output = middle + branch_scale * (
        product(after(hidden, attn_sum[2]), down_full) + down_bias_full
    )
    output = output.astype(jnp.bfloat16)
    for bit in down_order[4:]:
        down_sum = advance(down_sum, bit, count, output)
    up_sum = advance(up_sum, up_order[3], count, down_sum[2])
    attn_sum = advance(attn_sum, attn_order[2], count, up_sum[2])
    far_grad = after(far_grad, attn_sum[2])
    scaled = (normed_grad[:row_count] + far_grad.astype(jnp.float32)) * attn_gain_full
    centered_own = centered[:row_count]
    input_part = spread[:row_count] * (
        scaled
        - jnp.mean(scaled, axis=-1, keepdims=True)
        - centered_own * jnp.mean(scaled * centered_own, axis=-1, keepdims=True)
    )
    grad_in = (middle_grad + input_part).astype(jnp.bfloat16)
    down_done = add(down_sum[0][0], after(down_sum[1], grad_in)[0])
    for i in range(3, len(z_bits) + 2):
        up_sum = advance(up_sum, up_order[i + 1], count, attn_sum[2])
        attn_sum = advance(attn_sum, attn_order[i], count, up_sum[2])
    updown_done = add(up_sum[0][0], after(up_sum[1], attn_sum[2])[0])
    mine = add(attn_sum[0][0], attn_sum[1][0])
    other = add(attn_sum[0][1], attn_sum[1][1]).astype(jnp.bfloat16)
    other = flip(other, y_bit, count).astype(jnp.float32)
    first = jnp.where(half == 0, mine, other)[:, : 3 * side_count].reshape(part, 3, 1, side_count)
    second = jnp.where(half == 0, other, mine)[:, : 3 * side_count].reshape(part, 3, 1, side_count)
    attn_done = jnp.concatenate([first, second], axis=2).reshape(part, 3 * feature_count)
    done_lanes = (mine + other)[:, 3 * side_count :].T
    done_vectors, spot = [], 0
    for vector in vectors:
        size = vector.shape[0] // part
        done_vectors.append(done_lanes[spot : spot + size].reshape(-1))
        spot += size
    return (
        output[None],
        grad_in[None],
        done_vectors[0],
        done_vectors[1],
        attn_done,
        done_vectors[2],
        updown_done[:, ff_count:],
        done_vectors[3],
        done_vectors[4],
        done_vectors[5],
        updown_done[:, :ff_count],
        done_vectors[6],
        down_done,
        done_vectors[7],
    )


def solution(mesh):
    rows = P(AXES)
    tiles = P(AXES, None)
    pack = P(None, AXES, None)
    return jax.shard_map(
        functools.partial(shards, mesh.shape["dp"], mesh.shape["seq"]),
        mesh=mesh,
        in_specs=(
            pack, P(None, AXES), pack, rows, rows, tiles, rows, tiles, rows, rows, rows, tiles,
            rows, tiles, rows,
        ),
        out_specs=(
            pack, pack, rows, rows, tiles, rows, tiles, rows, rows, rows, tiles, rows, tiles, rows,
        ),
        check_vma=False,
    )
```

```python
import functools
import math

import jax
import jax.numpy as jnp
from jax import lax
from jax.experimental import pallas as pl
from jax.experimental.pallas import tpu as pltpu
from jax.sharding import PartitionSpec as P

HD = 64
AXES = ("dp", "seq")
NO_COST = pl.CostEstimate(flops=1, transcendentals=0, bytes_accessed=1)

branch_scale = 1.0 / math.sqrt(48.0)
norm_eps = 1e-05
neg_fill = -1e30
head_scale = HD ** (-0.5)


def layer_norm(values, norm_gain, norm_shift):
    center = values - jnp.mean(values, axis=-1, keepdims=True)
    spread = jnp.mean(center * center, axis=-1, keepdims=True)
    return center * lax.rsqrt(spread + norm_eps) * norm_gain + norm_shift


def gelu_and_slope(values):
    scale = math.sqrt(2.0 / math.pi)
    square = values * values
    bend = jnp.tanh(scale * values * (1.0 + 0.044715 * square))
    gate = 0.5 * (1.0 + bend)
    rise = scale * (1.0 + 3.0 * 0.044715 * square)
    return values * gate, gate + 0.5 * values * (1.0 - bend * bend) * rise


def product(first_op, second_op):
    return jnp.dot(first_op, second_op, preferred_element_type=jnp.float32)


def transpose_times(first_op, second_op):
    return jnp.einsum("tk,tn->kn", first_op, second_op, preferred_element_type=jnp.float32)


def times_transpose(first_op, second_op):
    return jnp.einsum("tn,kn->tk", first_op, second_op, preferred_element_type=jnp.float32)


def flip(array, bit, count):
    return lax.ppermute(array, AXES, [(i, i ^ bit) for i in range(count)])


def distance(place, order):
    return sum(bit for i, bit in enumerate(order) if (place >> i) & 1)


def assemble(pieces, order, me, count):
    size, rows, columns = pieces[0].shape

    def body(me_ref, *refs):
        sources, target, sem = refs[:-2], refs[-2], refs[-1]
        for place in range(count):
            owner = me_ref[0] ^ distance(place, order)
            pltpu.make_async_copy(
                sources[place // size].at[place % size], target.at[owner], sem
            ).start()
        pltpu.make_async_copy(target, target, sem).wait()

    return pl.pallas_call(
        body,
        grid_spec=pltpu.PrefetchScalarGridSpec(
            num_scalar_prefetch=1,
            grid=(1,),
            in_specs=[pl.BlockSpec(memory_space=pl.ANY)] * len(pieces),
            out_specs=pl.BlockSpec((count, rows, columns), lambda i, me_ref: (0, 0, 0)),
            scratch_shapes=[pltpu.SemaphoreType.DMA],
        ),
        out_shape=jax.ShapeDtypeStruct((count, rows, columns), pieces[0].dtype),
        cost_estimate=NO_COST,
        name="assemble",
    )(me.reshape(1), *pieces)


def gather_rows(held, order, me, count, ties):
    stages = len(order)
    done = held.shape[0].bit_length() - 1
    for bit in order[done : stages - 2]:
        held = after(held, *ties.get(bit, ()))
        held = jnp.concatenate([held, flip(held, bit, count)], axis=0)
    held = after(held, *ties.get(order[-2], ()))
    near = flip(held, order[-2], count)
    beside = flip(held, order[-1], count)
    near = after(near, *ties.get(order[-1], ()))
    pieces = [held, near, beside, flip(near, order[-1], count)]
    return assemble(pieces, order, me, count).reshape(count * held.shape[1], held.shape[2])


def unpack(packed, parts):
    count, total, rows, columns = packed.shape
    rest = total - parts - 1

    def body(source, side_ref, one_ref, rest_ref, held, come, go):
        def target(i):
            if i < parts:
                return side_ref.at[:, :, pl.ds(i * columns, columns)]
            return one_ref if i == parts else rest_ref.at[:, i - parts - 1]

        order = [parts] + list(range(parts)) + list(range(parts + 1, total))
        ins = [pltpu.make_async_copy(source.at[:, i], held.at[i], come.at[i]) for i in order]
        outs = [pltpu.make_async_copy(held.at[i], target(i), go.at[i]) for i in order]
        for copy in ins:
            copy.start()
        for first, second in zip(ins, outs):
            first.wait()
            second.start()
        for copy in outs:
            copy.wait()

    shapes = [(count, rows, parts * columns), (count, rows, columns), (count, rest, rows, columns)]
    out = pl.pallas_call(
        body,
        grid=(1,),
        in_specs=[pl.BlockSpec(memory_space=pl.ANY)],
        out_specs=[pl.BlockSpec(memory_space=pl.ANY)] * 3,
        scratch_shapes=[
            pltpu.VMEM((total, count, rows, columns), packed.dtype),
            pltpu.SemaphoreType.DMA((total,)),
            pltpu.SemaphoreType.DMA((total,)),
        ],
        out_shape=[jax.ShapeDtypeStruct(shape, packed.dtype) for shape in shapes],
        cost_estimate=NO_COST,
        name="unpack",
    )(packed)
    return [array.reshape(-1, array.shape[-1]) for array in out]


def disperse(parts, order, me, count):
    rows = parts[0].shape[0] // count
    columns = sum(part.shape[1] for part in parts)
    half = count // 2

    def body(me_ref, *refs):
        sources, (kept, gone, near, far) = refs[: len(parts)], refs[len(parts) : -4]
        near_sem, far_sem, kept_sem, gone_sem = refs[-4:]
        for target, sem, base in ((far, far_sem, half), (near, near_sem, 0)):
            for place in range(half):
                owner, left = me_ref[0] ^ distance(base + place, order[::-1]), 0
                for source in sources:
                    span = slice(left, left + source.shape[2])
                    pltpu.make_async_copy(
                        source.at[owner], target.at[place, :, span], sem
                    ).start()
                    left = span.stop
        pltpu.make_async_copy(far, far, far_sem).wait()
        send = pltpu.make_async_copy(far, gone, gone_sem)
        send.start()
        pltpu.make_async_copy(near, near, near_sem).wait()
        keep = pltpu.make_async_copy(near, kept, kept_sem)
        keep.start()
        send.wait()
        keep.wait()

    shape = (half, rows, columns)
    return pl.pallas_call(
        body,
        grid_spec=pltpu.PrefetchScalarGridSpec(
            num_scalar_prefetch=1,
            grid=(1,),
            in_specs=[pl.BlockSpec(memory_space=pl.ANY)] * len(parts),
            out_specs=[pl.BlockSpec(memory_space=pl.ANY)] * 2,
            scratch_shapes=[pltpu.VMEM(shape, parts[0].dtype)] * 2
            + [pltpu.SemaphoreType.DMA] * 4,
        ),
        out_shape=[jax.ShapeDtypeStruct(shape, parts[0].dtype)] * 2,
        cost_estimate=NO_COST,
        name="disperse",
    )(me.reshape(1), *[part.reshape(count, rows, part.shape[1]) for part in parts])


def add(first_term, second_term):
    return first_term.astype(jnp.float32) + second_term.astype(jnp.float32)


def begin_sum(parts, order, me, count):
    kept, gone = disperse(parts, order, me, count)
    return kept, flip(gone, order[0], count), gone


def advance(state, bit, count, *ties):
    kept, other, _ = state
    kept = after(kept, *ties)
    half = kept.shape[0] // 2
    gone = add(kept[half:], other[half:]).astype(jnp.bfloat16)
    kept = add(kept[:half], other[:half]).astype(jnp.bfloat16)
    return kept, flip(gone, bit, count), gone


def after(array, *others):
    return lax.optimization_barrier((array, *others))[0]


def nt(first_op, second_op):
    return lax.dot_general(
        first_op, second_op, (((1,), (1,)), ((), ())), preferred_element_type=jnp.float32
    )


def nn(first_op, second_op):
    return lax.dot_general(
        first_op, second_op, (((1,), (0,)), ((), ())), preferred_element_type=jnp.float32
    )


def lane_mask(shape, axis, head):
    place = lax.broadcasted_iota(jnp.int32, shape, axis)
    return (place < HD) if head == 0 else (place >= HD)


def fwd_kernel(info, q_ref, k_ref, v_ref, o_ref, lse_ref, vt_s, acc_s, m_s):
    which = pl.program_id(1)
    rows, width = q_ref.shape

    @pl.when(which == 0)
    def _():
        for slot in range(4):
            turned = v_ref[slot * rows : (slot + 1) * rows, :].astype(jnp.float32).T
            top = lane_mask((width, rows), 0, 0)
            vt_s[slot, 0] = jnp.where(top, turned, 1.0).astype(jnp.bfloat16)
            vt_s[slot, 1] = jnp.where(top, 1.0, turned).astype(jnp.bfloat16)

    query = q_ref[...] * jnp.bfloat16(head_scale)
    queries = [
        jnp.where(lane_mask((rows, width), 1, head), query, jnp.bfloat16(0)) for head in range(2)
    ]
    block_id = info[which]

    def visit(slot, diagonal):
        keys = k_ref[pl.ds(pl.multiple_of(slot * rows, rows), rows), :]
        for head in range(2):
            scores = nt(keys, queries[head])
            if diagonal:
                below = lax.broadcasted_iota(jnp.int32, (rows, rows), 0) <= (
                    lax.broadcasted_iota(jnp.int32, (rows, rows), 1)
                )
                scores = jnp.where(below, scores, neg_fill)
                peak = jnp.max(scores, axis=0, keepdims=True)
                raised = jnp.exp(scores - peak).astype(jnp.bfloat16)
                acc_s[head] = nn(vt_s[slot, head], raised)
            else:
                before = m_s[head : head + 1, :]
                peak = jnp.maximum(before, jnp.max(scores, axis=0, keepdims=True))
                raised = jnp.exp(scores - peak).astype(jnp.bfloat16)
                acc_s[head] = acc_s[head] * jnp.exp(before - peak) + nn(vt_s[slot, head], raised)
            m_s[head : head + 1, :] = peak

    visit(which, True)

    def step(block, carry):
        visit(info[4 + block], False)
        return carry

    lax.fori_loop(info[2 + which], block_id, step, 0)
    first, second = acc_s[0], acc_s[1]
    total0, total1 = first[HD : HD + 1, :], second[0:1, :]
    out = jnp.where(lane_mask((width, rows), 0, 0), first / total0, second / total1)
    o_ref[...] = out.T.astype(jnp.bfloat16)
    lse_ref[0, 0, 0:1, :] = m_s[0:1, :] + jnp.log(total0)
    lse_ref[0, 0, 1:2, :] = m_s[1:2, :] + jnp.log(total1)


def bwd_kernel(
    info, q_ref, k_ref, v_ref, o_ref, lse_ref, ga_ref, gb_ref, dq_ref, keep_ref, send_ref,
    kt_s, dk_s, dv_s, dq_s,
):
    which = pl.program_id(1)
    rows, width = q_ref.shape

    @pl.when(which == 0)
    def _():
        for slot in range(4):
            keys = k_ref[slot * rows : (slot + 1) * rows, :]
            kt_s[slot] = keys.astype(jnp.float32).T.astype(jnp.bfloat16)
        dk_s[...] = jnp.zeros_like(dk_s)
        dv_s[...] = jnp.zeros_like(dv_s)

    query = q_ref[...] * jnp.bfloat16(head_scale)
    grad = jnp.where(which == 0, ga_ref[...], gb_ref[...])
    joint = (grad.astype(jnp.float32) * o_ref[...].astype(jnp.float32)).T
    queries, grads, dots = [], [], []
    for head in range(2):
        lanes = lane_mask((rows, width), 1, head)
        queries.append(jnp.where(lanes, query, jnp.bfloat16(0)))
        grads.append(jnp.where(lanes, grad, jnp.bfloat16(0)))
        dots.append(jnp.sum(joint[head * HD : (head + 1) * HD], axis=0, keepdims=True))
    block_id = info[which]
    dq_s[...] = jnp.zeros_like(dq_s)

    def visit(slot, diagonal):
        spot = pl.ds(pl.multiple_of(slot * rows, rows), rows)
        keys, values = k_ref[spot, :], v_ref[spot, :]
        for head in range(2):
            scores = nt(keys, queries[head])
            probs = jnp.exp(scores - lse_ref[0, 0, head : head + 1, :])
            if diagonal:
                below = lax.broadcasted_iota(jnp.int32, (rows, rows), 0) <= (
                    lax.broadcasted_iota(jnp.int32, (rows, rows), 1)
                )
                probs = jnp.where(below, probs, 0.0)
            dv_s[slot] += nn(probs.astype(jnp.bfloat16), grads[head])
            pulled = nt(values, grads[head])
            score_grad = (probs * (pulled - dots[head])).astype(jnp.bfloat16)
            dk_s[slot] += nn(score_grad, queries[head])
            part = nn(kt_s[slot], score_grad)
            span = slice(head * HD, (head + 1) * HD)
            dq_s[span, :] += part[span]

    visit(which, True)

    def step(block, carry):
        visit(info[4 + block], False)
        return carry

    lax.fori_loop(info[2 + which], block_id, step, 0)
    dq_ref[...] = (dq_s[...] * head_scale).T.astype(jnp.bfloat16)

    @pl.when(which == 1)
    def _():
        for slot in range(4):
            target = (keep_ref, send_ref)[slot // 2]
            spot = slice((slot % 2) * rows, (slot % 2 + 1) * rows)
            target[0, spot, :] = dk_s[slot].astype(jnp.bfloat16)
            target[1, spot, :] = dv_s[slot].astype(jnp.bfloat16)


def attend_forward(info, query, pair):
    rows, columns = query.shape[0] // 2, query.shape[1]
    width = 2 * HD
    near = columns // width
    return pl.pallas_call(
        fwd_kernel,
        grid_spec=pltpu.PrefetchScalarGridSpec(
            num_scalar_prefetch=1,
            grid=(near, 2),
            in_specs=[
                pl.BlockSpec((rows, width), lambda p, w, s: (w, p)),
                pl.BlockSpec((4 * rows, width), lambda p, w, s: (0, p)),
                pl.BlockSpec((4 * rows, width), lambda p, w, s: (0, near + p)),
            ],
            out_specs=[
                pl.BlockSpec((rows, width), lambda p, w, s: (w, p)),
                pl.BlockSpec((1, 1, 8, rows), lambda p, w, s: (w, p, 0, 0)),
            ],
            scratch_shapes=[
                pltpu.VMEM((4, 2, width, rows), jnp.bfloat16),
                pltpu.VMEM((2, width, rows), jnp.float32),
                pltpu.VMEM((8, rows), jnp.float32),
            ],
        ),
        out_shape=[
            jax.ShapeDtypeStruct((2 * rows, columns), jnp.bfloat16),
            jax.ShapeDtypeStruct((2, near, 8, rows), jnp.float32),
        ],
        cost_estimate=NO_COST,
        name="attend_forward",
    )(info, query, pair, pair)


def attend_backward(info, query, pair, out, logsum, grad_own, grad_far):
    rows, columns = query.shape[0] // 2, query.shape[1]
    width = 2 * HD
    near = columns // width
    return pl.pallas_call(
        bwd_kernel,
        grid_spec=pltpu.PrefetchScalarGridSpec(
            num_scalar_prefetch=1,
            grid=(near, 2),
            in_specs=[
                pl.BlockSpec((rows, width), lambda p, w, s: (w, p)),
                pl.BlockSpec((4 * rows, width), lambda p, w, s: (0, p)),
                pl.BlockSpec((4 * rows, width), lambda p, w, s: (0, near + p)),
                pl.BlockSpec((rows, width), lambda p, w, s: (w, p)),
                pl.BlockSpec((1, 1, 8, rows), lambda p, w, s: (w, p, 0, 0)),
                pl.BlockSpec((rows, width), lambda p, w, s: (0, p)),
                pl.BlockSpec((rows, width), lambda p, w, s: (0, p)),
            ],
            out_specs=[
                pl.BlockSpec((rows, width), lambda p, w, s: (w, p)),
                pl.BlockSpec((2, 2 * rows, width), lambda p, w, s: (0, 0, p)),
                pl.BlockSpec((2, 2 * rows, width), lambda p, w, s: (0, 0, p)),
            ],
            scratch_shapes=[
                pltpu.VMEM((4, width, rows), jnp.bfloat16),
                pltpu.VMEM((4, rows, width), jnp.float32),
                pltpu.VMEM((4, rows, width), jnp.float32),
                pltpu.VMEM((width, rows), jnp.float32),
            ],
        ),
        out_shape=[
            jax.ShapeDtypeStruct((2 * rows, columns), jnp.bfloat16),
            jax.ShapeDtypeStruct((2, 2 * rows, columns), jnp.bfloat16),
            jax.ShapeDtypeStruct((2, 2 * rows, columns), jnp.bfloat16),
        ],
        cost_estimate=NO_COST,
        name="attend_backward",
    )(info, query, pair, pair, out, logsum, grad_own, grad_far)


def shards(
    dp_count, seq_count, tokens, starts, cotangent, attn_gain, attn_shift, attn_weight, attn_bias,
    proj_weight, proj_bias, mlp_gain, mlp_shift, up_weight, up_bias, down_weight, down_bias,
):
    count = dp_count * seq_count
    bits = [1 << i for i in range(count.bit_length() - 1)]
    core_bit, y_bit, x_bit, z_bits = bits[0], bits[1], bits[2], bits[3:]
    place = lax.axis_index("seq")
    me = lax.axis_index("dp") * seq_count + place
    half = place // (seq_count // 2)
    feature_count = tokens.shape[2]
    row_count = tokens.shape[1]
    ff_count = up_weight.shape[1]
    part = feature_count // count
    side_count = feature_count // 2

    def across(array):
        return lax.ppermute(array, "seq", [(i, seq_count - 1 - i) for i in range(seq_count)])

    def beside(array):
        return lax.ppermute(array, "seq", [(i, i ^ 1) for i in range(seq_count)])

    vectors = [attn_gain, attn_shift, attn_bias, proj_bias, mlp_gain, mlp_shift, up_bias, down_bias]
    total = sum(vector.shape[0] for vector in vectors)
    joined, spot = 0, 0
    for vector in vectors:
        joined = joined + jnp.pad(vector, (spot, total - spot - vector.shape[0]))
        spot += vector.shape[0]
    columns = joined.reshape(-1, part).T
    columns = jnp.pad(columns, ((0, 0), (0, 128 - columns.shape[1])))
    thirds = [attn_weight[:, i * side_count : (i + 1) * side_count] for i in range(6)]
    first = jnp.concatenate(thirds[0::2] + [columns], axis=1)
    second = jnp.concatenate(thirds[1::2] + [columns], axis=1)
    mine = jnp.where(half == 0, first, second)
    theirs = flip(jnp.where(half == 0, second, first), y_bit, count)
    ff_parts = ff_count // feature_count
    last_start = starts[0, -128:].reshape(1, 128)
    last_far = across(last_start)
    inputs = tokens[0]
    inputs_far = across(after(inputs, last_far))
    inputs_side = beside(inputs)
    inputs_side_far = beside(inputs_far)
    everyone_low = lax.optimization_barrier(
        jnp.concatenate([inputs, inputs_far, inputs_side, inputs_side_far], axis=0)
    )
    everyone = everyone_low.astype(jnp.float32)
    mean = jnp.mean(everyone, axis=-1, keepdims=True)
    spread = lax.rsqrt(
        jnp.mean((everyone - mean) * (everyone - mean), axis=-1, keepdims=True) + norm_eps
    )
    attn_all = gather_rows(
        jnp.stack([mine, theirs]), [y_bit] + z_bits[::-1] + [x_bit, core_bit], me, count,
        {core_bit: (mean, spread)},
    )
    packed = lax.all_gather(
        jnp.concatenate(
            [up_weight[:, i * feature_count : (i + 1) * feature_count] for i in range(ff_parts)]
            + [proj_weight, down_weight],
            axis=0,
        ).reshape(-1, part, feature_count),
        AXES, axis=0,
    )
    up_full, proj_full, down_full = unpack(packed, ff_parts)
    split = jnp.maximum(jnp.max(last_start), jnp.max(last_far)) > 0
    attn_full = attn_all[:, : 3 * side_count]
    lanes = attn_all[:, 3 * side_count :].astype(jnp.float32).T
    full_vectors, spot = [], 0
    for vector in vectors:
        size = vector.shape[0] // part
        rows = lanes[spot : spot + size].reshape(size, count, part)
        full_vectors.append(rows.transpose(1, 0, 2).reshape(-1))
        spot += size
    (
        attn_gain_full, attn_shift_full, attn_bias_full, proj_bias_full,
        mlp_gain_full, mlp_shift_full, up_bias_full, down_bias_full,
    ) = full_vectors

    far_place = seq_count - 1 - place
    spots = jnp.arange(8, dtype=jnp.int32)
    low = jnp.where(split, seq_count // 2, 0).astype(jnp.int32)
    block = spots - 4
    slot = jnp.where(
        block == place,
        0,
        jnp.where(block == far_place, 1, jnp.where(block == (place ^ 1), 2, 3)),
    )
    asked = jnp.where(spots % 2 == 0, place, far_place)
    info = jnp.where(
        spots < 2, asked, jnp.where(spots < 4, jnp.where(asked >= seq_count // 2, low, 0), slot)
    ).astype(jnp.int32)

    normed = (everyone - mean) * spread * attn_gain_full + attn_shift_full
    normed = normed.astype(jnp.bfloat16)
    normed_pair = normed[: 2 * row_count]
    query_bias = lax.dynamic_slice_in_dim(attn_bias_full, half * side_count, side_count)
    value_bias = lax.dynamic_slice_in_dim(
        attn_bias_full, feature_count + half * side_count, side_count
    )
    pair_bias = jnp.concatenate([jnp.zeros((side_count,), jnp.float32), value_bias])
    query = (product(normed_pair, attn_full[:, :side_count]) + query_bias).astype(jnp.bfloat16)
    pair = (product(normed, attn_full[:, side_count:]) + pair_bias).astype(jnp.bfloat16)
    out, logsum = attend_forward(info, query, pair)
    returned = across(out[row_count:])
    out_own = out[:row_count]
    attended = jnp.where(
        half == 0,
        jnp.concatenate([out_own, returned], axis=1),
        jnp.concatenate([returned, out_own], axis=1),
    )
    inputs = inputs.astype(jnp.float32)
    middle = inputs + branch_scale * (product(attended, proj_full) + proj_bias_full)
    normed_mlp = layer_norm(middle, mlp_gain_full, mlp_shift_full).astype(jnp.bfloat16)
    hidden_pre = product(normed_mlp, up_full) + up_bias_full
    hidden, slope = gelu_and_slope(hidden_pre)
    hidden, slope = lax.optimization_barrier(
        (hidden.astype(jnp.bfloat16), slope.astype(jnp.bfloat16))
    )

    out_grad = cotangent[0].astype(jnp.float32)
    down_in = (branch_scale * out_grad).astype(jnp.bfloat16)
    down_bias_grad = jnp.sum(down_in, axis=0, dtype=jnp.float32)
    down_order = [core_bit, x_bit, y_bit] + z_bits
    up_order = [core_bit, y_bit, x_bit] + z_bits
    down_weight_grad = transpose_times(hidden, down_in).astype(jnp.bfloat16)
    down_sum = begin_sum([down_weight_grad], down_order, me, count)
    hidden_grad = times_transpose(after(down_in, down_sum[2]), down_full)
    pre_grad = (hidden_grad * slope.astype(jnp.float32)).astype(jnp.bfloat16)
    down_sum = advance(down_sum, down_order[1], count, pre_grad)
    up_bias_grad = jnp.sum(pre_grad, axis=0, dtype=jnp.float32)
    mlp_pull = jax.vjp(layer_norm, middle, mlp_gain_full, mlp_shift_full)[1]
    middle_part, mlp_gain_grad, mlp_shift_grad = mlp_pull(
        times_transpose(after(pre_grad, down_sum[2]), up_full)
    )
    middle_grad = out_grad + middle_part
    proj_in = (branch_scale * middle_grad).astype(jnp.bfloat16)
    proj_bias_grad = jnp.sum(proj_in, axis=0, dtype=jnp.float32)
    proj_mine = lax.dynamic_slice_in_dim(proj_full, half * side_count, side_count)
    proj_theirs = lax.dynamic_slice_in_dim(proj_full, (1 - half) * side_count, side_count)
    grad_gone = times_transpose(proj_in, proj_theirs).astype(jnp.bfloat16)
    grad_far = across(grad_gone)
    grad_own = times_transpose(proj_in, proj_mine).astype(jnp.bfloat16)
    pre_grad = after(pre_grad, grad_own, grad_gone)
    up_weight_grad = transpose_times(normed_mlp, pre_grad).astype(jnp.bfloat16)
    proj_late = after(proj_in, grad_own, grad_gone)
    proj_weight_grad = transpose_times(attended, proj_late).astype(jnp.bfloat16)
    up_sum = begin_sum([up_weight_grad, proj_weight_grad], up_order, me, count)
    up_sum = advance(up_sum, up_order[1], count, grad_far)
    query_grad, pair_grad, pair_gone = attend_backward(
        info, query, pair, out, logsum, after(grad_own, up_sum[2]), grad_far
    )
    down_sum = advance(down_sum, down_order[2], count, query_grad)
    up_sum = advance(up_sum, up_order[2], count, down_sum[2], query_grad)
    pair_grad = add(after(pair_grad, up_sum[2]), beside(pair_gone)).astype(jnp.bfloat16)
    mixed_grad = jnp.concatenate([query_grad, pair_grad[0], pair_grad[1]], axis=1)
    normed_grad = times_transpose(mixed_grad, attn_full)
    down_sum = advance(down_sum, down_order[3], count, normed_grad)
    far_grad = across(normed_grad[row_count:].astype(jnp.bfloat16))
    centered = after(everyone_low[: 2 * row_count], query_grad).astype(jnp.float32)
    centered = (centered - mean[: 2 * row_count]) * spread[: 2 * row_count]
    attn_gain_grad = jnp.sum(normed_grad * centered, axis=0)
    attn_shift_grad = jnp.sum(normed_grad, axis=0)
    attn_weight_grad = transpose_times(normed_pair, after(mixed_grad, down_sum[2])).astype(jnp.bfloat16)
    column_sums = jnp.sum(mixed_grad, axis=0, dtype=jnp.float32).reshape(3, side_count)[::2]
    attn_bias_grad = jnp.where(
        half == 0,
        jnp.pad(column_sums, ((0, 0), (0, side_count))),
        jnp.pad(column_sums, ((0, 0), (side_count, 0))),
    ).reshape(-1)
    vector_grads = [
        attn_gain_grad, attn_shift_grad, attn_bias_grad, proj_bias_grad,
        mlp_gain_grad, mlp_shift_grad, up_bias_grad, down_bias_grad,
    ]
    grad_columns = jnp.concatenate(
        [
            grad.reshape(count, -1, part).transpose(1, 0, 2).reshape(-1, feature_count)
            for grad in vector_grads
        ],
        axis=0,
    ).T
    grad_columns = jnp.pad(grad_columns, ((0, 0), (0, 128 - grad_columns.shape[1])))
    attn_order = [core_bit, x_bit] + z_bits + [y_bit]
    attn_sum = begin_sum(
        [attn_weight_grad, grad_columns.astype(jnp.bfloat16)], attn_order, me, count
    )
    attn_sum = advance(attn_sum, attn_order[1], count)
    for bit in down_order[4:]:
        down_sum = advance(down_sum, bit, count, attn_sum[2])
    up_sum = advance(up_sum, up_order[3], count, down_sum[2])
    output = middle + branch_scale * (
        product(after(hidden, up_sum[2]), down_full) + down_bias_full
    )
    output = output.astype(jnp.bfloat16)
    attn_sum = advance(attn_sum, attn_order[2], count, output)
    far_grad = after(far_grad, attn_sum[2])
    scaled = (normed_grad[:row_count] + far_grad.astype(jnp.float32)) * attn_gain_full
    centered_own = centered[:row_count]
    input_part = spread[:row_count] * (
        scaled
        - jnp.mean(scaled, axis=-1, keepdims=True)
        - centered_own * jnp.mean(scaled * centered_own, axis=-1, keepdims=True)
    )
    grad_in = (middle_grad + input_part).astype(jnp.bfloat16)
    down_done = add(down_sum[0][0], after(down_sum[1], grad_in)[0])
    for i in range(3, len(z_bits) + 2):
        up_sum = advance(up_sum, up_order[i + 1], count, attn_sum[2])
        attn_sum = advance(attn_sum, attn_order[i], count, up_sum[2])
    updown_done = add(up_sum[0][0], after(up_sum[1], attn_sum[2])[0])
    mine = add(attn_sum[0][0], attn_sum[1][0])
    other = add(attn_sum[0][1], attn_sum[1][1]).astype(jnp.bfloat16)
    other = flip(other, y_bit, count).astype(jnp.float32)
    first = jnp.where(half == 0, mine, other)[:, : 3 * side_count].reshape(part, 3, 1, side_count)
    second = jnp.where(half == 0, other, mine)[:, : 3 * side_count].reshape(part, 3, 1, side_count)
    attn_done = jnp.concatenate([first, second], axis=2).reshape(part, 3 * feature_count)
    done_lanes = (mine + other)[:, 3 * side_count :].T
    done_vectors, spot = [], 0
    for vector in vectors:
        size = vector.shape[0] // part
        done_vectors.append(done_lanes[spot : spot + size].reshape(-1))
        spot += size
    return (
        output[None],
        grad_in[None],
        done_vectors[0],
        done_vectors[1],
        attn_done,
        done_vectors[2],
        updown_done[:, ff_count:],
        done_vectors[3],
        done_vectors[4],
        done_vectors[5],
        updown_done[:, :ff_count],
        done_vectors[6],
        down_done,
        done_vectors[7],
    )


def solution(mesh):
    rows = P(AXES)
    tiles = P(AXES, None)
    pack = P(None, AXES, None)
    return jax.shard_map(
        functools.partial(shards, mesh.shape["dp"], mesh.shape["seq"]),
        mesh=mesh,
        in_specs=(
            pack, P(None, AXES), pack, rows, rows, tiles, rows, tiles, rows, rows, rows, tiles,
            rows, tiles, rows,
        ),
        out_specs=(
            pack, pack, rows, rows, tiles, rows, tiles, rows, rows, rows, tiles, rows, tiles, rows,
        ),
        check_vma=False,
    )
```

```python
import functools
import math

import jax
import jax.numpy as jnp
from jax import lax
from jax.experimental import pallas as pl
from jax.experimental.pallas import tpu as pltpu
from jax.sharding import PartitionSpec as P

HD = 64
AXES = ("dp", "seq")
NO_COST = pl.CostEstimate(flops=1, transcendentals=0, bytes_accessed=1)

branch_scale = 1.0 / math.sqrt(48.0)
norm_eps = 1e-05
neg_fill = -1e30
head_scale = HD ** (-0.5)


def layer_norm(values, norm_gain, norm_shift):
    center = values - jnp.mean(values, axis=-1, keepdims=True)
    spread = jnp.mean(center * center, axis=-1, keepdims=True)
    return center * lax.rsqrt(spread + norm_eps) * norm_gain + norm_shift


def gelu_and_slope(values):
    scale = math.sqrt(2.0 / math.pi)
    square = values * values
    bend = jnp.tanh(scale * values * (1.0 + 0.044715 * square))
    gate = 0.5 * (1.0 + bend)
    rise = scale * (1.0 + 3.0 * 0.044715 * square)
    return values * gate, gate + 0.5 * values * (1.0 - bend * bend) * rise


def product(first_op, second_op):
    return jnp.dot(first_op, second_op, preferred_element_type=jnp.float32)


def transpose_times(first_op, second_op):
    return jnp.einsum("tk,tn->kn", first_op, second_op, preferred_element_type=jnp.float32)


def times_transpose(first_op, second_op):
    return jnp.einsum("tn,kn->tk", first_op, second_op, preferred_element_type=jnp.float32)


def flip(array, bit, count):
    return lax.ppermute(array, AXES, [(i, i ^ bit) for i in range(count)])


def distance(place, order):
    return sum(bit for i, bit in enumerate(order) if (place >> i) & 1)


def assemble(pieces, order, me, count):
    size, rows, columns = pieces[0].shape

    def body(me_ref, *refs):
        sources, target, sem = refs[:-2], refs[-2], refs[-1]
        for place in range(count):
            owner = me_ref[0] ^ distance(place, order)
            pltpu.make_async_copy(
                sources[place // size].at[place % size], target.at[owner], sem
            ).start()
        pltpu.make_async_copy(target, target, sem).wait()

    return pl.pallas_call(
        body,
        grid_spec=pltpu.PrefetchScalarGridSpec(
            num_scalar_prefetch=1,
            grid=(1,),
            in_specs=[pl.BlockSpec(memory_space=pl.ANY)] * len(pieces),
            out_specs=pl.BlockSpec((count, rows, columns), lambda i, me_ref: (0, 0, 0)),
            scratch_shapes=[pltpu.SemaphoreType.DMA],
        ),
        out_shape=jax.ShapeDtypeStruct((count, rows, columns), pieces[0].dtype),
        cost_estimate=NO_COST,
        name="assemble",
    )(me.reshape(1), *pieces)


def gather_rows(held, order, me, count, ties):
    stages = len(order)
    done = held.shape[0].bit_length() - 1
    for bit in order[done : stages - 2]:
        held = after(held, *ties.get(bit, ()))
        held = jnp.concatenate([held, flip(held, bit, count)], axis=0)
    held = after(held, *ties.get(order[-2], ()))
    near = flip(held, order[-2], count)
    beside = flip(held, order[-1], count)
    near = after(near, *ties.get(order[-1], ()))
    pieces = [held, near, beside, flip(near, order[-1], count)]
    return assemble(pieces, order, me, count).reshape(count * held.shape[1], held.shape[2])


def pack(side, one, rest, parts):
    rows, columns = one.shape

    def body(side_ref, one_ref, rest_ref, packed):
        for i in range(parts):
            packed[i] = side_ref[:, i * columns : (i + 1) * columns]
        packed[parts] = one_ref[...]
        packed[parts + 1 :] = rest_ref[...]

    rest = rest.reshape(-1, rows, columns)
    return pl.pallas_call(
        body,
        out_shape=jax.ShapeDtypeStruct((parts + 1 + rest.shape[0], rows, columns), one.dtype),
        cost_estimate=NO_COST,
        name="pack",
    )(side, one, rest)


def unpack(packed, parts):
    count, total, rows, columns = packed.shape
    rest = total - parts - 1

    def body(source, side_ref, one_ref, rest_ref, held, come, go):
        def target(i):
            if i < parts:
                return side_ref.at[:, :, pl.ds(i * columns, columns)]
            return one_ref if i == parts else rest_ref.at[:, i - parts - 1]

        order = [parts] + list(range(parts)) + list(range(parts + 1, total))
        ins = [pltpu.make_async_copy(source.at[:, i], held.at[i], come.at[i]) for i in order]
        outs = [pltpu.make_async_copy(held.at[i], target(i), go.at[i]) for i in order]
        for copy in ins:
            copy.start()
        for first, second in zip(ins, outs):
            first.wait()
            second.start()
        for copy in outs:
            copy.wait()

    shapes = [(count, rows, parts * columns), (count, rows, columns), (count, rest, rows, columns)]
    out = pl.pallas_call(
        body,
        grid=(1,),
        in_specs=[pl.BlockSpec(memory_space=pl.ANY)],
        out_specs=[pl.BlockSpec(memory_space=pl.ANY)] * 3,
        scratch_shapes=[
            pltpu.VMEM((total, count, rows, columns), packed.dtype),
            pltpu.SemaphoreType.DMA((total,)),
            pltpu.SemaphoreType.DMA((total,)),
        ],
        out_shape=[jax.ShapeDtypeStruct(shape, packed.dtype) for shape in shapes],
        cost_estimate=NO_COST,
        name="unpack",
    )(packed)
    return [array.reshape(-1, array.shape[-1]) for array in out]


def disperse(parts, order, me, count):
    rows = parts[0].shape[0] // count
    columns = sum(part.shape[1] for part in parts)
    half = count // 2

    def body(me_ref, *refs):
        sources, (kept, gone, near, far) = refs[: len(parts)], refs[len(parts) : -4]
        near_sem, far_sem, kept_sem, gone_sem = refs[-4:]
        for target, sem, base in ((far, far_sem, half), (near, near_sem, 0)):
            for place in range(half):
                owner, left = me_ref[0] ^ distance(base + place, order[::-1]), 0
                for source in sources:
                    span = slice(left, left + source.shape[2])
                    pltpu.make_async_copy(
                        source.at[owner], target.at[place, :, span], sem
                    ).start()
                    left = span.stop
        pltpu.make_async_copy(far, far, far_sem).wait()
        send = pltpu.make_async_copy(far, gone, gone_sem)
        send.start()
        pltpu.make_async_copy(near, near, near_sem).wait()
        keep = pltpu.make_async_copy(near, kept, kept_sem)
        keep.start()
        send.wait()
        keep.wait()

    shape = (half, rows, columns)
    return pl.pallas_call(
        body,
        grid_spec=pltpu.PrefetchScalarGridSpec(
            num_scalar_prefetch=1,
            grid=(1,),
            in_specs=[pl.BlockSpec(memory_space=pl.ANY)] * len(parts),
            out_specs=[pl.BlockSpec(memory_space=pl.ANY)] * 2,
            scratch_shapes=[pltpu.VMEM(shape, parts[0].dtype)] * 2
            + [pltpu.SemaphoreType.DMA] * 4,
        ),
        out_shape=[jax.ShapeDtypeStruct(shape, parts[0].dtype)] * 2,
        cost_estimate=NO_COST,
        name="disperse",
    )(me.reshape(1), *[part.reshape(count, rows, part.shape[1]) for part in parts])


def add(first_term, second_term):
    return first_term.astype(jnp.float32) + second_term.astype(jnp.float32)


def begin_sum(parts, order, me, count):
    kept, gone = disperse(parts, order, me, count)
    return kept, flip(gone, order[0], count), gone


def advance(state, bit, count, *ties):
    kept, other, _ = state
    kept = after(kept, *ties)
    half = kept.shape[0] // 2
    gone = add(kept[half:], other[half:]).astype(jnp.bfloat16)
    kept = add(kept[:half], other[:half]).astype(jnp.bfloat16)
    return kept, flip(gone, bit, count), gone


def after(array, *others):
    return lax.optimization_barrier((array, *others))[0]


def nt(first_op, second_op):
    return lax.dot_general(
        first_op, second_op, (((1,), (1,)), ((), ())), preferred_element_type=jnp.float32
    )


def nn(first_op, second_op):
    return lax.dot_general(
        first_op, second_op, (((1,), (0,)), ((), ())), preferred_element_type=jnp.float32
    )


def lane_mask(shape, axis, head):
    place = lax.broadcasted_iota(jnp.int32, shape, axis)
    return (place < HD) if head == 0 else (place >= HD)


def fwd_kernel(info, q_ref, k_ref, v_ref, o_ref, lse_ref, vt_s, acc_s, m_s):
    which = pl.program_id(1)
    rows, width = q_ref.shape

    @pl.when(which == 0)
    def _():
        for slot in range(4):
            turned = v_ref[slot * rows : (slot + 1) * rows, :].astype(jnp.float32).T
            top = lane_mask((width, rows), 0, 0)
            vt_s[slot, 0] = jnp.where(top, turned, 1.0).astype(jnp.bfloat16)
            vt_s[slot, 1] = jnp.where(top, 1.0, turned).astype(jnp.bfloat16)

    query = q_ref[...] * jnp.bfloat16(head_scale)
    queries = [
        jnp.where(lane_mask((rows, width), 1, head), query, jnp.bfloat16(0)) for head in range(2)
    ]
    block_id = info[which]

    def visit(slot, diagonal):
        keys = k_ref[pl.ds(pl.multiple_of(slot * rows, rows), rows), :]
        for head in range(2):
            scores = nt(keys, queries[head])
            if diagonal:
                below = lax.broadcasted_iota(jnp.int32, (rows, rows), 0) <= (
                    lax.broadcasted_iota(jnp.int32, (rows, rows), 1)
                )
                scores = jnp.where(below, scores, neg_fill)
                peak = jnp.max(scores, axis=0, keepdims=True)
                raised = jnp.exp(scores - peak).astype(jnp.bfloat16)
                acc_s[head] = nn(vt_s[slot, head], raised)
            else:
                before = m_s[head : head + 1, :]
                peak = jnp.maximum(before, jnp.max(scores, axis=0, keepdims=True))
                raised = jnp.exp(scores - peak).astype(jnp.bfloat16)
                acc_s[head] = acc_s[head] * jnp.exp(before - peak) + nn(vt_s[slot, head], raised)
            m_s[head : head + 1, :] = peak

    visit(which, True)

    def step(block, carry):
        visit(info[4 + block], False)
        return carry

    lax.fori_loop(info[2 + which], block_id, step, 0)
    first, second = acc_s[0], acc_s[1]
    total0, total1 = first[HD : HD + 1, :], second[0:1, :]
    out = jnp.where(lane_mask((width, rows), 0, 0), first / total0, second / total1)
    o_ref[...] = out.T.astype(jnp.bfloat16)
    lse_ref[0, 0, 0:1, :] = m_s[0:1, :] + jnp.log(total0)
    lse_ref[0, 0, 1:2, :] = m_s[1:2, :] + jnp.log(total1)


def bwd_kernel(
    info, q_ref, k_ref, v_ref, o_ref, lse_ref, ga_ref, gb_ref, dq_ref, keep_ref, send_ref,
    kt_s, dk_s, dv_s, dq_s,
):
    which = pl.program_id(1)
    rows, width = q_ref.shape

    @pl.when(which == 0)
    def _():
        for slot in range(4):
            keys = k_ref[slot * rows : (slot + 1) * rows, :]
            kt_s[slot] = keys.astype(jnp.float32).T.astype(jnp.bfloat16)
        dk_s[...] = jnp.zeros_like(dk_s)
        dv_s[...] = jnp.zeros_like(dv_s)

    query = q_ref[...] * jnp.bfloat16(head_scale)
    grad = jnp.where(which == 0, ga_ref[...], gb_ref[...])
    joint = (grad.astype(jnp.float32) * o_ref[...].astype(jnp.float32)).T
    queries, grads, dots = [], [], []
    for head in range(2):
        lanes = lane_mask((rows, width), 1, head)
        queries.append(jnp.where(lanes, query, jnp.bfloat16(0)))
        grads.append(jnp.where(lanes, grad, jnp.bfloat16(0)))
        dots.append(jnp.sum(joint[head * HD : (head + 1) * HD], axis=0, keepdims=True))
    block_id = info[which]
    dq_s[...] = jnp.zeros_like(dq_s)

    def visit(slot, diagonal):
        spot = pl.ds(pl.multiple_of(slot * rows, rows), rows)
        keys, values = k_ref[spot, :], v_ref[spot, :]
        for head in range(2):
            scores = nt(keys, queries[head])
            probs = jnp.exp(scores - lse_ref[0, 0, head : head + 1, :])
            if diagonal:
                below = lax.broadcasted_iota(jnp.int32, (rows, rows), 0) <= (
                    lax.broadcasted_iota(jnp.int32, (rows, rows), 1)
                )
                probs = jnp.where(below, probs, 0.0)
            dv_s[slot] += nn(probs.astype(jnp.bfloat16), grads[head])
            pulled = nt(values, grads[head])
            score_grad = (probs * (pulled - dots[head])).astype(jnp.bfloat16)
            dk_s[slot] += nn(score_grad, queries[head])
            part = nn(kt_s[slot], score_grad)
            span = slice(head * HD, (head + 1) * HD)
            dq_s[span, :] += part[span]

    visit(which, True)

    def step(block, carry):
        visit(info[4 + block], False)
        return carry

    lax.fori_loop(info[2 + which], block_id, step, 0)
    dq_ref[...] = (dq_s[...] * head_scale).T.astype(jnp.bfloat16)

    @pl.when(which == 1)
    def _():
        for slot in range(4):
            target = (keep_ref, send_ref)[slot // 2]
            spot = slice((slot % 2) * rows, (slot % 2 + 1) * rows)
            target[0, spot, :] = dk_s[slot].astype(jnp.bfloat16)
            target[1, spot, :] = dv_s[slot].astype(jnp.bfloat16)


def attend_forward(info, query, pair):
    rows, columns = query.shape[0] // 2, query.shape[1]
    width = 2 * HD
    near = columns // width
    return pl.pallas_call(
        fwd_kernel,
        grid_spec=pltpu.PrefetchScalarGridSpec(
            num_scalar_prefetch=1,
            grid=(near, 2),
            in_specs=[
                pl.BlockSpec((rows, width), lambda p, w, s: (w, p)),
                pl.BlockSpec((4 * rows, width), lambda p, w, s: (0, p)),
                pl.BlockSpec((4 * rows, width), lambda p, w, s: (0, near + p)),
            ],
            out_specs=[
                pl.BlockSpec((rows, width), lambda p, w, s: (w, p)),
                pl.BlockSpec((1, 1, 8, rows), lambda p, w, s: (w, p, 0, 0)),
            ],
            scratch_shapes=[
                pltpu.VMEM((4, 2, width, rows), jnp.bfloat16),
                pltpu.VMEM((2, width, rows), jnp.float32),
                pltpu.VMEM((8, rows), jnp.float32),
            ],
        ),
        out_shape=[
            jax.ShapeDtypeStruct((2 * rows, columns), jnp.bfloat16),
            jax.ShapeDtypeStruct((2, near, 8, rows), jnp.float32),
        ],
        cost_estimate=NO_COST,
        name="attend_forward",
    )(info, query, pair, pair)


def attend_backward(info, query, pair, out, logsum, grad_own, grad_far):
    rows, columns = query.shape[0] // 2, query.shape[1]
    width = 2 * HD
    near = columns // width
    return pl.pallas_call(
        bwd_kernel,
        grid_spec=pltpu.PrefetchScalarGridSpec(
            num_scalar_prefetch=1,
            grid=(near, 2),
            in_specs=[
                pl.BlockSpec((rows, width), lambda p, w, s: (w, p)),
                pl.BlockSpec((4 * rows, width), lambda p, w, s: (0, p)),
                pl.BlockSpec((4 * rows, width), lambda p, w, s: (0, near + p)),
                pl.BlockSpec((rows, width), lambda p, w, s: (w, p)),
                pl.BlockSpec((1, 1, 8, rows), lambda p, w, s: (w, p, 0, 0)),
                pl.BlockSpec((rows, width), lambda p, w, s: (0, p)),
                pl.BlockSpec((rows, width), lambda p, w, s: (0, p)),
            ],
            out_specs=[
                pl.BlockSpec((rows, width), lambda p, w, s: (w, p)),
                pl.BlockSpec((2, 2 * rows, width), lambda p, w, s: (0, 0, p)),
                pl.BlockSpec((2, 2 * rows, width), lambda p, w, s: (0, 0, p)),
            ],
            scratch_shapes=[
                pltpu.VMEM((4, width, rows), jnp.bfloat16),
                pltpu.VMEM((4, rows, width), jnp.float32),
                pltpu.VMEM((4, rows, width), jnp.float32),
                pltpu.VMEM((width, rows), jnp.float32),
            ],
        ),
        out_shape=[
            jax.ShapeDtypeStruct((2 * rows, columns), jnp.bfloat16),
            jax.ShapeDtypeStruct((2, 2 * rows, columns), jnp.bfloat16),
            jax.ShapeDtypeStruct((2, 2 * rows, columns), jnp.bfloat16),
        ],
        cost_estimate=NO_COST,
        name="attend_backward",
    )(info, query, pair, pair, out, logsum, grad_own, grad_far)


def shards(
    dp_count, seq_count, tokens, starts, cotangent, attn_gain, attn_shift, attn_weight, attn_bias,
    proj_weight, proj_bias, mlp_gain, mlp_shift, up_weight, up_bias, down_weight, down_bias,
):
    count = dp_count * seq_count
    bits = [1 << i for i in range(count.bit_length() - 1)]
    core_bit, y_bit, x_bit, z_bits = bits[0], bits[1], bits[2], bits[3:]
    place = lax.axis_index("seq")
    me = lax.axis_index("dp") * seq_count + place
    half = place // (seq_count // 2)
    feature_count = tokens.shape[2]
    row_count = tokens.shape[1]
    ff_count = up_weight.shape[1]
    part = feature_count // count
    side_count = feature_count // 2

    def across(array):
        return lax.ppermute(array, "seq", [(i, seq_count - 1 - i) for i in range(seq_count)])

    def beside(array):
        return lax.ppermute(array, "seq", [(i, i ^ 1) for i in range(seq_count)])

    vectors = [attn_gain, attn_shift, attn_bias, proj_bias, mlp_gain, mlp_shift, up_bias, down_bias]
    total = sum(vector.shape[0] for vector in vectors)
    joined, spot = 0, 0
    for vector in vectors:
        joined = joined + jnp.pad(vector, (spot, total - spot - vector.shape[0]))
        spot += vector.shape[0]
    columns = joined.reshape(-1, part).T
    columns = jnp.pad(columns, ((0, 0), (0, 128 - columns.shape[1])))
    thirds = [attn_weight[:, i * side_count : (i + 1) * side_count] for i in range(6)]
    first = jnp.concatenate(thirds[0::2] + [columns], axis=1)
    second = jnp.concatenate(thirds[1::2] + [columns], axis=1)
    mine = jnp.where(half == 0, first, second)
    theirs = flip(jnp.where(half == 0, second, first), y_bit, count)
    ff_parts = ff_count // feature_count
    last_start = starts[0, -128:].reshape(1, 128)
    last_far = across(last_start)
    inputs = tokens[0]
    inputs_far = across(after(inputs, last_far))
    inputs_side = beside(inputs)
    inputs_side_far = beside(inputs_far)
    everyone_low = lax.optimization_barrier(
        jnp.concatenate([inputs, inputs_far, inputs_side, inputs_side_far], axis=0)
    )
    everyone = everyone_low.astype(jnp.float32)
    mean = jnp.mean(everyone, axis=-1, keepdims=True)
    spread = lax.rsqrt(
        jnp.mean((everyone - mean) * (everyone - mean), axis=-1, keepdims=True) + norm_eps
    )
    attn_all = gather_rows(
        jnp.stack([mine, theirs]), [y_bit] + z_bits[::-1] + [x_bit, core_bit], me, count,
        {core_bit: (mean, spread)},
    )
    packed = pack(up_weight, proj_weight, down_weight, ff_parts)
    packed = lax.all_gather(packed, AXES, axis=0)
    up_full, proj_full, down_full = unpack(packed, ff_parts)
    split = jnp.maximum(jnp.max(last_start), jnp.max(last_far)) > 0
    attn_full = attn_all[:, : 3 * side_count]
    lanes = attn_all[:, 3 * side_count :].astype(jnp.float32).T
    full_vectors, spot = [], 0
    for vector in vectors:
        size = vector.shape[0] // part
        rows = lanes[spot : spot + size].reshape(size, count, part)
        full_vectors.append(rows.transpose(1, 0, 2).reshape(-1))
        spot += size
    (
        attn_gain_full, attn_shift_full, attn_bias_full, proj_bias_full,
        mlp_gain_full, mlp_shift_full, up_bias_full, down_bias_full,
    ) = full_vectors

    far_place = seq_count - 1 - place
    spots = jnp.arange(8, dtype=jnp.int32)
    low = jnp.where(split, seq_count // 2, 0).astype(jnp.int32)
    block = spots - 4
    slot = jnp.where(
        block == place,
        0,
        jnp.where(block == far_place, 1, jnp.where(block == (place ^ 1), 2, 3)),
    )
    asked = jnp.where(spots % 2 == 0, place, far_place)
    info = jnp.where(
        spots < 2, asked, jnp.where(spots < 4, jnp.where(asked >= seq_count // 2, low, 0), slot)
    ).astype(jnp.int32)

    normed = (everyone - mean) * spread * attn_gain_full + attn_shift_full
    normed = normed.astype(jnp.bfloat16)
    normed_pair = normed[: 2 * row_count]
    query_bias = lax.dynamic_slice_in_dim(attn_bias_full, half * side_count, side_count)
    value_bias = lax.dynamic_slice_in_dim(
        attn_bias_full, feature_count + half * side_count, side_count
    )
    pair_bias = jnp.concatenate([jnp.zeros((side_count,), jnp.float32), value_bias])
    query = (product(normed_pair, attn_full[:, :side_count]) + query_bias).astype(jnp.bfloat16)
    pair = (product(normed, attn_full[:, side_count:]) + pair_bias).astype(jnp.bfloat16)
    out, logsum = attend_forward(info, query, pair)
    returned = across(out[row_count:])
    out_own = out[:row_count]
    attended = jnp.where(
        half == 0,
        jnp.concatenate([out_own, returned], axis=1),
        jnp.concatenate([returned, out_own], axis=1),
    )
    inputs = inputs.astype(jnp.float32)
    middle = inputs + branch_scale * (product(attended, proj_full) + proj_bias_full)
    normed_mlp = layer_norm(middle, mlp_gain_full, mlp_shift_full).astype(jnp.bfloat16)
    hidden_pre = product(normed_mlp, up_full) + up_bias_full
    hidden, slope = gelu_and_slope(hidden_pre)
    hidden, slope = lax.optimization_barrier(
        (hidden.astype(jnp.bfloat16), slope.astype(jnp.bfloat16))
    )

    out_grad = cotangent[0].astype(jnp.float32)
    down_in = (branch_scale * out_grad).astype(jnp.bfloat16)
    down_bias_grad = jnp.sum(down_in, axis=0, dtype=jnp.float32)
    down_order = [core_bit, x_bit, y_bit] + z_bits
    up_order = [core_bit, y_bit, x_bit] + z_bits
    down_weight_grad = transpose_times(hidden, down_in).astype(jnp.bfloat16)
    down_sum = begin_sum([down_weight_grad], down_order, me, count)
    hidden_grad = times_transpose(after(down_in, down_sum[2]), down_full)
    pre_grad = (hidden_grad * slope.astype(jnp.float32)).astype(jnp.bfloat16)
    down_sum = advance(down_sum, down_order[1], count, pre_grad)
    up_bias_grad = jnp.sum(pre_grad, axis=0, dtype=jnp.float32)
    mlp_pull = jax.vjp(layer_norm, middle, mlp_gain_full, mlp_shift_full)[1]
    middle_part, mlp_gain_grad, mlp_shift_grad = mlp_pull(
        times_transpose(after(pre_grad, down_sum[2]), up_full)
    )
    middle_grad = out_grad + middle_part
    proj_in = (branch_scale * middle_grad).astype(jnp.bfloat16)
    proj_bias_grad = jnp.sum(proj_in, axis=0, dtype=jnp.float32)
    proj_mine = lax.dynamic_slice_in_dim(proj_full, half * side_count, side_count)
    proj_theirs = lax.dynamic_slice_in_dim(proj_full, (1 - half) * side_count, side_count)
    grad_gone = times_transpose(proj_in, proj_theirs).astype(jnp.bfloat16)
    grad_far = across(grad_gone)
    grad_own = times_transpose(proj_in, proj_mine).astype(jnp.bfloat16)
    pre_grad = after(pre_grad, grad_gone)
    up_weight_grad = transpose_times(normed_mlp, pre_grad).astype(jnp.bfloat16)
    proj_late = after(proj_in, grad_gone)
    proj_weight_grad = transpose_times(attended, proj_late).astype(jnp.bfloat16)
    up_weight_grad = after(up_weight_grad, grad_far)
    up_sum = begin_sum([up_weight_grad, proj_weight_grad], up_order, me, count)
    up_sum = advance(up_sum, up_order[1], count, grad_far)
    query_grad, pair_grad, pair_gone = attend_backward(
        info, query, pair, out, logsum, after(grad_own, up_sum[2]), grad_far
    )
    down_sum = advance(down_sum, down_order[2], count, query_grad)
    up_sum = advance(up_sum, up_order[2], count, down_sum[2], query_grad)
    pair_grad = add(after(pair_grad, up_sum[2]), beside(pair_gone)).astype(jnp.bfloat16)
    mixed_grad = jnp.concatenate([query_grad, pair_grad[0], pair_grad[1]], axis=1)
    normed_grad = times_transpose(mixed_grad, attn_full)
    down_sum = advance(down_sum, down_order[3], count, normed_grad)
    far_grad = across(normed_grad[row_count:].astype(jnp.bfloat16))
    centered = after(everyone_low[: 2 * row_count], query_grad).astype(jnp.float32)
    centered = (centered - mean[: 2 * row_count]) * spread[: 2 * row_count]
    attn_gain_grad = jnp.sum(normed_grad * centered, axis=0)
    attn_shift_grad = jnp.sum(normed_grad, axis=0)
    attn_weight_grad = transpose_times(normed_pair, after(mixed_grad, down_sum[2])).astype(jnp.bfloat16)
    column_sums = jnp.sum(mixed_grad, axis=0, dtype=jnp.float32).reshape(3, side_count)[::2]
    attn_bias_grad = jnp.where(
        half == 0,
        jnp.pad(column_sums, ((0, 0), (0, side_count))),
        jnp.pad(column_sums, ((0, 0), (side_count, 0))),
    ).reshape(-1)
    vector_grads = [
        attn_gain_grad, attn_shift_grad, attn_bias_grad, proj_bias_grad,
        mlp_gain_grad, mlp_shift_grad, up_bias_grad, down_bias_grad,
    ]
    grad_columns = jnp.concatenate(
        [
            grad.reshape(count, -1, part).transpose(1, 0, 2).reshape(-1, feature_count)
            for grad in vector_grads
        ],
        axis=0,
    ).T
    grad_columns = jnp.pad(grad_columns, ((0, 0), (0, 128 - grad_columns.shape[1])))
    attn_order = [core_bit, x_bit] + z_bits + [y_bit]
    attn_sum = begin_sum(
        [attn_weight_grad, grad_columns.astype(jnp.bfloat16)], attn_order, me, count
    )
    up_sum = advance(up_sum, up_order[3], count, attn_sum[2])
    attn_sum = advance(attn_sum, attn_order[1], count, up_sum[2])
    output = middle + branch_scale * (
        product(after(hidden, attn_sum[2]), down_full) + down_bias_full
    )
    output = output.astype(jnp.bfloat16)
    for bit in down_order[4:]:
        down_sum = advance(down_sum, bit, count, output)
    attn_sum = advance(attn_sum, attn_order[2], count, down_sum[2])
    far_grad = after(far_grad, attn_sum[2])
    scaled = (normed_grad[:row_count] + far_grad.astype(jnp.float32)) * attn_gain_full
    centered_own = centered[:row_count]
    input_part = spread[:row_count] * (
        scaled
        - jnp.mean(scaled, axis=-1, keepdims=True)
        - centered_own * jnp.mean(scaled * centered_own, axis=-1, keepdims=True)
    )
    grad_in = (middle_grad + input_part).astype(jnp.bfloat16)
    down_done = add(down_sum[0][0], after(down_sum[1], grad_in)[0])
    for i in range(3, len(z_bits) + 2):
        up_sum = advance(up_sum, up_order[i + 1], count, attn_sum[2])
        attn_sum = advance(attn_sum, attn_order[i], count, up_sum[2])
    updown_done = add(up_sum[0][0], after(up_sum[1], attn_sum[2])[0])
    mine = add(attn_sum[0][0], attn_sum[1][0])
    other = add(attn_sum[0][1], attn_sum[1][1]).astype(jnp.bfloat16)
    other = flip(other, y_bit, count).astype(jnp.float32)
    first = jnp.where(half == 0, mine, other)[:, : 3 * side_count].reshape(part, 3, 1, side_count)
    second = jnp.where(half == 0, other, mine)[:, : 3 * side_count].reshape(part, 3, 1, side_count)
    attn_done = jnp.concatenate([first, second], axis=2).reshape(part, 3 * feature_count)
    done_lanes = (mine + other)[:, 3 * side_count :].T
    done_vectors, spot = [], 0
    for vector in vectors:
        size = vector.shape[0] // part
        done_vectors.append(done_lanes[spot : spot + size].reshape(-1))
        spot += size
    return (
        output[None],
        grad_in[None],
        done_vectors[0],
        done_vectors[1],
        attn_done,
        done_vectors[2],
        updown_done[:, ff_count:],
        done_vectors[3],
        done_vectors[4],
        done_vectors[5],
        updown_done[:, :ff_count],
        done_vectors[6],
        down_done,
        done_vectors[7],
    )


def solution(mesh):
    rows = P(AXES)
    tiles = P(AXES, None)
    pack = P(None, AXES, None)
    return jax.shard_map(
        functools.partial(shards, mesh.shape["dp"], mesh.shape["seq"]),
        mesh=mesh,
        in_specs=(
            pack, P(None, AXES), pack, rows, rows, tiles, rows, tiles, rows, rows, rows, tiles,
            rows, tiles, rows,
        ),
        out_specs=(
            pack, pack, rows, rows, tiles, rows, tiles, rows, rows, rows, tiles, rows, tiles, rows,
        ),
        check_vma=False,
    )
```

```python
import functools
import math

import jax
import jax.numpy as jnp
from jax import lax
from jax.experimental import pallas as pl
from jax.experimental.pallas import tpu as pltpu
from jax.sharding import PartitionSpec as P

HD = 64
AXES = ("dp", "seq")
NO_COST = pl.CostEstimate(flops=1, transcendentals=0, bytes_accessed=1)

branch_scale = 1.0 / math.sqrt(48.0)
norm_eps = 1e-05
neg_fill = -1e30
head_scale = HD ** (-0.5)


def layer_norm(values, norm_gain, norm_shift):
    center = values - jnp.mean(values, axis=-1, keepdims=True)
    spread = jnp.mean(center * center, axis=-1, keepdims=True)
    return center * lax.rsqrt(spread + norm_eps) * norm_gain + norm_shift


def gelu_and_slope(values):
    scale = math.sqrt(2.0 / math.pi)
    square = values * values
    gate = 0.5 * jnp.tanh(values * (scale + scale * 0.044715 * square)) + 0.5
    hidden = values * gate
    rise = 2.0 * scale + 6.0 * scale * 0.044715 * square
    return hidden, gate + hidden * (1.0 - gate) * rise


def product(first_op, second_op):
    return jnp.dot(first_op, second_op, preferred_element_type=jnp.float32)


def transpose_times(first_op, second_op):
    return jnp.einsum("tk,tn->kn", first_op, second_op, preferred_element_type=jnp.float32)


def times_transpose(first_op, second_op):
    return jnp.einsum("tn,kn->tk", first_op, second_op, preferred_element_type=jnp.float32)


def flip(array, bit, count):
    return lax.ppermute(array, AXES, [(i, i ^ bit) for i in range(count)])


def distance(place, order):
    return sum(bit for i, bit in enumerate(order) if (place >> i) & 1)


def assemble(pieces, order, me, count):
    size, rows, columns = pieces[0].shape

    def body(me_ref, *refs):
        sources, target, sem = refs[:-2], refs[-2], refs[-1]
        for place in range(count):
            owner = me_ref[0] ^ distance(place, order)
            pltpu.make_async_copy(
                sources[place // size].at[place % size], target.at[owner], sem
            ).start()
        pltpu.make_async_copy(target, target, sem).wait()

    return pl.pallas_call(
        body,
        grid_spec=pltpu.PrefetchScalarGridSpec(
            num_scalar_prefetch=1,
            grid=(1,),
            in_specs=[pl.BlockSpec(memory_space=pl.ANY)] * len(pieces),
            out_specs=pl.BlockSpec((count, rows, columns), lambda i, me_ref: (0, 0, 0)),
            scratch_shapes=[pltpu.SemaphoreType.DMA],
        ),
        out_shape=jax.ShapeDtypeStruct((count, rows, columns), pieces[0].dtype),
        cost_estimate=NO_COST,
        name="assemble",
    )(me.reshape(1), *pieces)


def gather_rows(held, order, me, count, ties):
    stages = len(order)
    done = held.shape[0].bit_length() - 1
    for bit in order[done : stages - 2]:
        held = after(held, *ties.get(bit, ()))
        held = jnp.concatenate([held, flip(held, bit, count)], axis=0)
    held = after(held, *ties.get(order[-2], ()))
    near = flip(held, order[-2], count)
    beside = flip(held, order[-1], count)
    near = after(near, *ties.get(order[-1], ()))
    pieces = [held, near, beside, flip(near, order[-1], count)]
    return assemble(pieces, order, me, count).reshape(count * held.shape[1], held.shape[2])


def pack(side, one, rest, parts):
    rows, columns = one.shape

    def body(side_ref, one_ref, rest_ref, packed):
        for i in range(parts):
            packed[i] = side_ref[:, i * columns : (i + 1) * columns]
        packed[parts] = one_ref[...]
        packed[parts + 1 :] = rest_ref[...]

    rest = rest.reshape(-1, rows, columns)
    return pl.pallas_call(
        body,
        out_shape=jax.ShapeDtypeStruct((parts + 1 + rest.shape[0], rows, columns), one.dtype),
        cost_estimate=NO_COST,
        name="pack",
    )(side, one, rest)


def unpack(packed, parts):
    count, total, rows, columns = packed.shape
    rest = total - parts - 1

    def body(source, side_ref, one_ref, rest_ref, held, come, go):
        def target(i):
            if i < parts:
                return side_ref.at[:, :, pl.ds(i * columns, columns)]
            return one_ref if i == parts else rest_ref.at[:, i - parts - 1]

        order = [parts] + list(range(parts)) + list(range(parts + 1, total))
        ins = [pltpu.make_async_copy(source.at[:, i], held.at[i], come.at[i]) for i in order]
        outs = [pltpu.make_async_copy(held.at[i], target(i), go.at[i]) for i in order]
        for copy in ins:
            copy.start()
        for first, second in zip(ins, outs):
            first.wait()
            second.start()
        for copy in outs:
            copy.wait()

    shapes = [(count, rows, parts * columns), (count, rows, columns), (count, rest, rows, columns)]
    out = pl.pallas_call(
        body,
        grid=(1,),
        in_specs=[pl.BlockSpec(memory_space=pl.ANY)],
        out_specs=[pl.BlockSpec(memory_space=pl.ANY)] * 3,
        scratch_shapes=[
            pltpu.VMEM((total, count, rows, columns), packed.dtype),
            pltpu.SemaphoreType.DMA((total,)),
            pltpu.SemaphoreType.DMA((total,)),
        ],
        out_shape=[jax.ShapeDtypeStruct(shape, packed.dtype) for shape in shapes],
        cost_estimate=NO_COST,
        name="unpack",
    )(packed)
    return [array.reshape(-1, array.shape[-1]) for array in out]


def disperse(parts, order, me, count):
    rows = parts[0].shape[0] // count
    columns = sum(part.shape[1] for part in parts)
    half = count // 2

    def body(me_ref, *refs):
        sources, (kept, gone, near, far) = refs[: len(parts)], refs[len(parts) : -4]
        near_sem, far_sem, kept_sem, gone_sem = refs[-4:]
        for target, sem, base in ((far, far_sem, half), (near, near_sem, 0)):
            for place in range(half):
                owner, left = me_ref[0] ^ distance(base + place, order[::-1]), 0
                for source in sources:
                    span = slice(left, left + source.shape[2])
                    pltpu.make_async_copy(
                        source.at[owner], target.at[place, :, span], sem
                    ).start()
                    left = span.stop
        pltpu.make_async_copy(far, far, far_sem).wait()
        send = pltpu.make_async_copy(far, gone, gone_sem)
        send.start()
        pltpu.make_async_copy(near, near, near_sem).wait()
        keep = pltpu.make_async_copy(near, kept, kept_sem)
        keep.start()
        send.wait()
        keep.wait()

    shape = (half, rows, columns)
    return pl.pallas_call(
        body,
        grid_spec=pltpu.PrefetchScalarGridSpec(
            num_scalar_prefetch=1,
            grid=(1,),
            in_specs=[pl.BlockSpec(memory_space=pl.ANY)] * len(parts),
            out_specs=[pl.BlockSpec(memory_space=pl.ANY)] * 2,
            scratch_shapes=[pltpu.VMEM(shape, parts[0].dtype)] * 2
            + [pltpu.SemaphoreType.DMA] * 4,
        ),
        out_shape=[jax.ShapeDtypeStruct(shape, parts[0].dtype)] * 2,
        cost_estimate=NO_COST,
        name="disperse",
    )(me.reshape(1), *[part.reshape(count, rows, part.shape[1]) for part in parts])


def add(first_term, second_term):
    return first_term.astype(jnp.float32) + second_term.astype(jnp.float32)


def begin_sum(parts, order, me, count):
    kept, gone = disperse(parts, order, me, count)
    return kept, flip(gone, order[0], count), gone


def advance(state, bit, count, *ties):
    kept, other, _ = state
    kept = after(kept, *ties)
    half = kept.shape[0] // 2
    gone = add(kept[half:], other[half:]).astype(jnp.bfloat16)
    kept = add(kept[:half], other[:half]).astype(jnp.bfloat16)
    return kept, flip(gone, bit, count), gone


def after(array, *others):
    return lax.optimization_barrier((array, *others))[0]


def nt(first_op, second_op):
    return lax.dot_general(
        first_op, second_op, (((1,), (1,)), ((), ())), preferred_element_type=jnp.float32
    )


def nn(first_op, second_op):
    return lax.dot_general(
        first_op, second_op, (((1,), (0,)), ((), ())), preferred_element_type=jnp.float32
    )


def lane_mask(shape, axis, head):
    place = lax.broadcasted_iota(jnp.int32, shape, axis)
    return (place < HD) if head == 0 else (place >= HD)


def fwd_kernel(info, q_ref, k_ref, v_ref, o_ref, lse_ref, vt_s, acc_s, m_s):
    which = pl.program_id(1)
    rows, width = q_ref.shape

    @pl.when(which == 0)
    def _():
        for slot in range(4):
            turned = v_ref[slot * rows : (slot + 1) * rows, :].astype(jnp.float32).T
            top = lane_mask((width, rows), 0, 0)
            vt_s[slot, 0] = jnp.where(top, turned, 1.0).astype(jnp.bfloat16)
            vt_s[slot, 1] = jnp.where(top, 1.0, turned).astype(jnp.bfloat16)

    query = q_ref[...] * jnp.bfloat16(head_scale)
    queries = [
        jnp.where(lane_mask((rows, width), 1, head), query, jnp.bfloat16(0)) for head in range(2)
    ]
    block_id = info[which]

    def visit(slot, start, size, first):
        keys = k_ref[pl.ds(pl.multiple_of(slot * rows + start, size), size), :]
        keep = slice(start, rows)
        for head in range(2):
            scores = nt(keys, queries[head][keep])
            if size < rows:
                below = lax.broadcasted_iota(jnp.int32, scores.shape, 0) <= (
                    lax.broadcasted_iota(jnp.int32, scores.shape, 1)
                )
                scores = jnp.where(below, scores, neg_fill)
            values = vt_s[slot, head, :, start : start + size]
            if first:
                peak = jnp.max(scores, axis=0, keepdims=True)
                raised = jnp.exp(scores - peak).astype(jnp.bfloat16)
                acc_s[head, :, keep] = nn(values, raised)
            else:
                before = m_s[head : head + 1, keep]
                peak = jnp.maximum(before, jnp.max(scores, axis=0, keepdims=True))
                raised = jnp.exp(scores - peak).astype(jnp.bfloat16)
                acc_s[head, :, keep] = (
                    acc_s[head, :, keep] * jnp.exp(before - peak) + nn(values, raised)
                )
            m_s[head : head + 1, keep] = peak

    visit(which, 0, rows // 2, True)
    visit(which, rows // 2, rows // 2, False)

    def step(block, carry):
        visit(info[4 + block], 0, rows, False)
        return carry

    lax.fori_loop(info[2 + which], block_id, step, 0)
    first, second = acc_s[0], acc_s[1]
    total0, total1 = first[HD : HD + 1, :], second[0:1, :]
    out = jnp.where(lane_mask((width, rows), 0, 0), first / total0, second / total1)
    o_ref[...] = out.T.astype(jnp.bfloat16)
    lse_ref[0, 0, 0:1, :] = m_s[0:1, :] + jnp.log(total0)
    lse_ref[0, 0, 1:2, :] = m_s[1:2, :] + jnp.log(total1)


def bwd_kernel(
    info, q_ref, k_ref, v_ref, o_ref, lse_ref, ga_ref, gb_ref, dq_ref, keep_ref, send_ref,
    kt_s, dk_s, dv_s, dq_s,
):
    which = pl.program_id(1)
    rows, width = q_ref.shape

    @pl.when(which == 0)
    def _():
        for slot in range(4):
            keys = k_ref[slot * rows : (slot + 1) * rows, :]
            kt_s[slot] = keys.astype(jnp.float32).T.astype(jnp.bfloat16)
        dk_s[...] = jnp.zeros_like(dk_s)
        dv_s[...] = jnp.zeros_like(dv_s)

    query = q_ref[...] * jnp.bfloat16(head_scale)
    grad = jnp.where(which == 0, ga_ref[...], gb_ref[...])
    joint = (grad.astype(jnp.float32) * o_ref[...].astype(jnp.float32)).T
    queries, grads, dots = [], [], []
    for head in range(2):
        lanes = lane_mask((rows, width), 1, head)
        queries.append(jnp.where(lanes, query, jnp.bfloat16(0)))
        grads.append(jnp.where(lanes, grad, jnp.bfloat16(0)))
        dots.append(jnp.sum(joint[head * HD : (head + 1) * HD], axis=0, keepdims=True))
    block_id = info[which]
    dq_s[...] = jnp.zeros_like(dq_s)

    def visit(slot, start, size):
        spot = pl.ds(pl.multiple_of(slot * rows + start, size), size)
        keys, values = k_ref[spot, :], v_ref[spot, :]
        keep, span = slice(start, rows), slice(start, start + size)
        for head in range(2):
            some, pulls = queries[head][keep], grads[head][keep]
            scores = nt(keys, some)
            probs = jnp.exp(scores - lse_ref[0, 0, head : head + 1, keep])
            if size < rows:
                below = lax.broadcasted_iota(jnp.int32, scores.shape, 0) <= (
                    lax.broadcasted_iota(jnp.int32, scores.shape, 1)
                )
                probs = jnp.where(below, probs, 0.0)
            dv_s[slot, span] += nn(probs.astype(jnp.bfloat16), pulls)
            pulled = nt(values, pulls)
            score_grad = (probs * (pulled - dots[head][:, keep])).astype(jnp.bfloat16)
            dk_s[slot, span] += nn(score_grad, some)
            part = nn(kt_s[slot, :, span], score_grad)
            lanes = slice(head * HD, (head + 1) * HD)
            dq_s[lanes, keep] += part[lanes]

    visit(which, 0, rows // 2)
    visit(which, rows // 2, rows // 2)

    def step(block, carry):
        visit(info[4 + block], 0, rows)
        return carry

    lax.fori_loop(info[2 + which], block_id, step, 0)
    dq_ref[...] = (dq_s[...] * head_scale).T.astype(jnp.bfloat16)

    @pl.when(which == 1)
    def _():
        for slot in range(4):
            target = (keep_ref, send_ref)[slot // 2]
            spot = slice((slot % 2) * rows, (slot % 2 + 1) * rows)
            target[0, spot, :] = dk_s[slot].astype(jnp.bfloat16)
            target[1, spot, :] = dv_s[slot].astype(jnp.bfloat16)


def attend_forward(info, query, pair):
    rows, columns = query.shape[0] // 2, query.shape[1]
    width = 2 * HD
    near = columns // width
    return pl.pallas_call(
        fwd_kernel,
        grid_spec=pltpu.PrefetchScalarGridSpec(
            num_scalar_prefetch=1,
            grid=(near, 2),
            in_specs=[
                pl.BlockSpec((rows, width), lambda p, w, s: (w, p)),
                pl.BlockSpec((4 * rows, width), lambda p, w, s: (0, p)),
                pl.BlockSpec((4 * rows, width), lambda p, w, s: (0, near + p)),
            ],
            out_specs=[
                pl.BlockSpec((rows, width), lambda p, w, s: (w, p)),
                pl.BlockSpec((1, 1, 8, rows), lambda p, w, s: (w, p, 0, 0)),
            ],
            scratch_shapes=[
                pltpu.VMEM((4, 2, width, rows), jnp.bfloat16),
                pltpu.VMEM((2, width, rows), jnp.float32),
                pltpu.VMEM((8, rows), jnp.float32),
            ],
        ),
        out_shape=[
            jax.ShapeDtypeStruct((2 * rows, columns), jnp.bfloat16),
            jax.ShapeDtypeStruct((2, near, 8, rows), jnp.float32),
        ],
        cost_estimate=NO_COST,
        name="attend_forward",
    )(info, query, pair, pair)


def attend_backward(info, query, pair, out, logsum, grad_own, grad_far):
    rows, columns = query.shape[0] // 2, query.shape[1]
    width = 2 * HD
    near = columns // width
    return pl.pallas_call(
        bwd_kernel,
        grid_spec=pltpu.PrefetchScalarGridSpec(
            num_scalar_prefetch=1,
            grid=(near, 2),
            in_specs=[
                pl.BlockSpec((rows, width), lambda p, w, s: (w, p)),
                pl.BlockSpec((4 * rows, width), lambda p, w, s: (0, p)),
                pl.BlockSpec((4 * rows, width), lambda p, w, s: (0, near + p)),
                pl.BlockSpec((rows, width), lambda p, w, s: (w, p)),
                pl.BlockSpec((1, 1, 8, rows), lambda p, w, s: (w, p, 0, 0)),
                pl.BlockSpec((rows, width), lambda p, w, s: (0, p)),
                pl.BlockSpec((rows, width), lambda p, w, s: (0, p)),
            ],
            out_specs=[
                pl.BlockSpec((rows, width), lambda p, w, s: (w, p)),
                pl.BlockSpec((2, 2 * rows, width), lambda p, w, s: (0, 0, p)),
                pl.BlockSpec((2, 2 * rows, width), lambda p, w, s: (0, 0, p)),
            ],
            scratch_shapes=[
                pltpu.VMEM((4, width, rows), jnp.bfloat16),
                pltpu.VMEM((4, rows, width), jnp.float32),
                pltpu.VMEM((4, rows, width), jnp.float32),
                pltpu.VMEM((width, rows), jnp.float32),
            ],
        ),
        out_shape=[
            jax.ShapeDtypeStruct((2 * rows, columns), jnp.bfloat16),
            jax.ShapeDtypeStruct((2, 2 * rows, columns), jnp.bfloat16),
            jax.ShapeDtypeStruct((2, 2 * rows, columns), jnp.bfloat16),
        ],
        cost_estimate=NO_COST,
        name="attend_backward",
    )(info, query, pair, pair, out, logsum, grad_own, grad_far)


def shards(
    dp_count, seq_count, tokens, starts, cotangent, attn_gain, attn_shift, attn_weight, attn_bias,
    proj_weight, proj_bias, mlp_gain, mlp_shift, up_weight, up_bias, down_weight, down_bias,
):
    count = dp_count * seq_count
    bits = [1 << i for i in range(count.bit_length() - 1)]
    core_bit, y_bit, x_bit, z_bits = bits[0], bits[1], bits[2], bits[3:]
    place = lax.axis_index("seq")
    me = lax.axis_index("dp") * seq_count + place
    half = place // (seq_count // 2)
    feature_count = tokens.shape[2]
    row_count = tokens.shape[1]
    ff_count = up_weight.shape[1]
    part = feature_count // count
    side_count = feature_count // 2

    def across(array):
        return lax.ppermute(array, "seq", [(i, seq_count - 1 - i) for i in range(seq_count)])

    def beside(array):
        return lax.ppermute(array, "seq", [(i, i ^ 1) for i in range(seq_count)])

    vectors = [attn_gain, attn_shift, attn_bias, proj_bias, mlp_gain, mlp_shift, up_bias, down_bias]
    total = sum(vector.shape[0] for vector in vectors)
    joined, spot = 0, 0
    for vector in vectors:
        joined = joined + jnp.pad(vector, (spot, total - spot - vector.shape[0]))
        spot += vector.shape[0]
    columns = joined.reshape(-1, part).T
    columns = jnp.pad(columns, ((0, 0), (0, 128 - columns.shape[1])))
    thirds = [attn_weight[:, i * side_count : (i + 1) * side_count] for i in range(6)]
    first = jnp.concatenate(thirds[0::2] + [columns], axis=1)
    second = jnp.concatenate(thirds[1::2] + [columns], axis=1)
    mine = jnp.where(half == 0, first, second)
    theirs = flip(jnp.where(half == 0, second, first), y_bit, count)
    ff_parts = ff_count // feature_count
    last_start = starts[0, -128:].reshape(1, 128)
    last_far = across(last_start)
    inputs = tokens[0]
    inputs_far = across(after(inputs, last_far))
    inputs_side = beside(inputs)
    inputs_side_far = beside(inputs_far)
    everyone_low = lax.optimization_barrier(
        jnp.concatenate([inputs, inputs_far, inputs_side, inputs_side_far], axis=0)
    )
    everyone = everyone_low.astype(jnp.float32)
    mean = jnp.mean(everyone, axis=-1, keepdims=True)
    spread = lax.rsqrt(
        jnp.mean((everyone - mean) * (everyone - mean), axis=-1, keepdims=True) + norm_eps
    )
    attn_all = gather_rows(
        jnp.stack([mine, theirs]), [y_bit] + z_bits[::-1] + [x_bit, core_bit], me, count,
        {core_bit: (mean, spread)},
    )
    packed = pack(up_weight, proj_weight, down_weight, ff_parts)
    packed = lax.all_gather(packed, AXES, axis=0)
    up_full, proj_full, down_full = unpack(packed, ff_parts)
    split = jnp.maximum(jnp.max(last_start), jnp.max(last_far)) > 0
    attn_full = attn_all[:, : 3 * side_count]
    lanes = attn_all[:, 3 * side_count :].astype(jnp.float32).T
    full_vectors, spot = [], 0
    for vector in vectors:
        size = vector.shape[0] // part
        rows = lanes[spot : spot + size].reshape(size, count, part)
        full_vectors.append(rows.transpose(1, 0, 2).reshape(-1))
        spot += size
    (
        attn_gain_full, attn_shift_full, attn_bias_full, proj_bias_full,
        mlp_gain_full, mlp_shift_full, up_bias_full, down_bias_full,
    ) = full_vectors

    far_place = seq_count - 1 - place
    spots = jnp.arange(8, dtype=jnp.int32)
    low = jnp.where(split, seq_count // 2, 0).astype(jnp.int32)
    block = spots - 4
    slot = jnp.where(
        block == place,
        0,
        jnp.where(block == far_place, 1, jnp.where(block == (place ^ 1), 2, 3)),
    )
    asked = jnp.where(spots % 2 == 0, place, far_place)
    info = jnp.where(
        spots < 2, asked, jnp.where(spots < 4, jnp.where(asked >= seq_count // 2, low, 0), slot)
    ).astype(jnp.int32)

    normed = (everyone - mean) * spread * attn_gain_full + attn_shift_full
    normed = normed.astype(jnp.bfloat16)
    normed_pair = normed[: 2 * row_count]
    query_bias = lax.dynamic_slice_in_dim(attn_bias_full, half * side_count, side_count)
    value_bias = lax.dynamic_slice_in_dim(
        attn_bias_full, feature_count + half * side_count, side_count
    )
    pair_bias = jnp.concatenate([jnp.zeros((side_count,), jnp.float32), value_bias])
    query = (product(normed_pair, attn_full[:, :side_count]) + query_bias).astype(jnp.bfloat16)
    pair = (product(normed, attn_full[:, side_count:]) + pair_bias).astype(jnp.bfloat16)
    out, logsum = attend_forward(info, query, pair)
    returned = across(out[row_count:])
    out_own = out[:row_count]
    attended = jnp.where(
        half == 0,
        jnp.concatenate([out_own, returned], axis=1),
        jnp.concatenate([returned, out_own], axis=1),
    )
    inputs = inputs.astype(jnp.float32)
    middle = inputs + branch_scale * (product(attended, proj_full) + proj_bias_full)
    normed_mlp = layer_norm(middle, mlp_gain_full, mlp_shift_full).astype(jnp.bfloat16)
    hidden_pre = product(normed_mlp, up_full) + up_bias_full
    hidden, slope = gelu_and_slope(hidden_pre)
    hidden, slope = lax.optimization_barrier(
        (hidden.astype(jnp.bfloat16), slope.astype(jnp.bfloat16))
    )

    out_grad = cotangent[0].astype(jnp.float32)
    down_in = (branch_scale * out_grad).astype(jnp.bfloat16)
    down_bias_grad = jnp.sum(down_in, axis=0, dtype=jnp.float32)
    down_order = [core_bit, x_bit, y_bit] + z_bits
    up_order = [core_bit, y_bit, x_bit] + z_bits
    down_weight_grad = transpose_times(hidden, down_in).astype(jnp.bfloat16)
    down_sum = begin_sum([down_weight_grad], down_order, me, count)
    hidden_grad = times_transpose(after(down_in, down_sum[2]), down_full)
    pre_grad = (hidden_grad * slope.astype(jnp.float32)).astype(jnp.bfloat16)
    up_bias_grad = jnp.sum(pre_grad, axis=0, dtype=jnp.float32)
    mlp_pull = jax.vjp(layer_norm, middle, mlp_gain_full, mlp_shift_full)[1]
    middle_part, mlp_gain_grad, mlp_shift_grad = mlp_pull(
        times_transpose(pre_grad, up_full)
    )
    middle_grad = out_grad + middle_part
    proj_in = (branch_scale * middle_grad).astype(jnp.bfloat16)
    proj_bias_grad = jnp.sum(proj_in, axis=0, dtype=jnp.float32)
    proj_mine = lax.dynamic_slice_in_dim(proj_full, half * side_count, side_count)
    proj_theirs = lax.dynamic_slice_in_dim(proj_full, (1 - half) * side_count, side_count)
    grad_gone = times_transpose(proj_in, proj_theirs).astype(jnp.bfloat16)
    grad_far = across(grad_gone)
    grad_own = times_transpose(proj_in, proj_mine).astype(jnp.bfloat16)
    pre_grad = after(pre_grad, grad_gone)
    up_weight_grad = transpose_times(normed_mlp, pre_grad).astype(jnp.bfloat16)
    proj_late = after(proj_in, grad_gone)
    proj_weight_grad = transpose_times(attended, proj_late).astype(jnp.bfloat16)
    up_weight_grad = after(up_weight_grad, grad_far, down_sum[1])
    up_sum = begin_sum([up_weight_grad, proj_weight_grad], up_order, me, count)
    down_sum = advance(down_sum, down_order[1], count, up_sum[2])
    up_sum = advance(up_sum, up_order[1], count, down_sum[2])
    query_grad, pair_grad, pair_gone = attend_backward(
        info, query, pair, out, logsum, after(grad_own, up_sum[2]), grad_far
    )
    down_sum = advance(down_sum, down_order[2], count, query_grad)
    up_sum = advance(up_sum, up_order[2], count, down_sum[2], query_grad)
    pair_grad = add(after(pair_grad, up_sum[2]), beside(pair_gone)).astype(jnp.bfloat16)
    mixed_grad = jnp.concatenate([query_grad, pair_grad[0], pair_grad[1]], axis=1)
    normed_grad = times_transpose(mixed_grad, attn_full)
    down_sum = advance(down_sum, down_order[3], count, normed_grad)
    far_grad = across(normed_grad[row_count:].astype(jnp.bfloat16))
    centered = after(everyone_low[: 2 * row_count], query_grad).astype(jnp.float32)
    centered = (centered - mean[: 2 * row_count]) * spread[: 2 * row_count]
    attn_gain_grad = jnp.sum(normed_grad * centered, axis=0)
    attn_shift_grad = jnp.sum(normed_grad, axis=0)
    attn_weight_grad = transpose_times(normed_pair, after(mixed_grad, down_sum[2])).astype(jnp.bfloat16)
    column_sums = jnp.sum(mixed_grad, axis=0, dtype=jnp.float32).reshape(3, side_count)[::2]
    attn_bias_grad = jnp.where(
        half == 0,
        jnp.pad(column_sums, ((0, 0), (0, side_count))),
        jnp.pad(column_sums, ((0, 0), (side_count, 0))),
    ).reshape(-1)
    vector_grads = [
        attn_gain_grad, attn_shift_grad, attn_bias_grad, proj_bias_grad,
        mlp_gain_grad, mlp_shift_grad, up_bias_grad, down_bias_grad,
    ]
    grad_columns = jnp.concatenate(
        [
            grad.reshape(count, -1, part).transpose(1, 0, 2).reshape(-1, feature_count)
            for grad in vector_grads
        ],
        axis=0,
    ).T
    grad_columns = jnp.pad(grad_columns, ((0, 0), (0, 128 - grad_columns.shape[1])))
    attn_order = [core_bit, x_bit] + z_bits + [y_bit]
    attn_sum = begin_sum(
        [attn_weight_grad, grad_columns.astype(jnp.bfloat16)], attn_order, me, count
    )
    up_sum = advance(up_sum, up_order[3], count, attn_sum[2])
    attn_sum = advance(attn_sum, attn_order[1], count, up_sum[2])
    output = middle + branch_scale * (
        product(after(hidden, attn_sum[2]), down_full) + down_bias_full
    )
    output = output.astype(jnp.bfloat16)
    for bit in down_order[4:]:
        down_sum = advance(down_sum, bit, count, output)
    attn_sum = advance(attn_sum, attn_order[2], count, down_sum[2])
    far_grad = after(far_grad, attn_sum[2])
    scaled = (normed_grad[:row_count] + far_grad.astype(jnp.float32)) * attn_gain_full
    centered_own = centered[:row_count]
    input_part = spread[:row_count] * (
        scaled
        - jnp.mean(scaled, axis=-1, keepdims=True)
        - centered_own * jnp.mean(scaled * centered_own, axis=-1, keepdims=True)
    )
    grad_in = (middle_grad + input_part).astype(jnp.bfloat16)
    down_done = add(down_sum[0][0], after(down_sum[1], grad_in)[0])
    for i in range(3, len(z_bits) + 2):
        up_sum = advance(up_sum, up_order[i + 1], count, attn_sum[2])
        attn_sum = advance(attn_sum, attn_order[i], count, up_sum[2])
    updown_done = add(up_sum[0][0], after(up_sum[1], attn_sum[2])[0])
    mine = add(attn_sum[0][0], attn_sum[1][0])
    other = add(attn_sum[0][1], attn_sum[1][1]).astype(jnp.bfloat16)
    other = flip(other, y_bit, count).astype(jnp.float32)
    first = jnp.where(half == 0, mine, other)[:, : 3 * side_count].reshape(part, 3, 1, side_count)
    second = jnp.where(half == 0, other, mine)[:, : 3 * side_count].reshape(part, 3, 1, side_count)
    attn_done = jnp.concatenate([first, second], axis=2).reshape(part, 3 * feature_count)
    done_lanes = (mine + other)[:, 3 * side_count :].T
    done_vectors, spot = [], 0
    for vector in vectors:
        size = vector.shape[0] // part
        done_vectors.append(done_lanes[spot : spot + size].reshape(-1))
        spot += size
    return (
        output[None],
        grad_in[None],
        done_vectors[0],
        done_vectors[1],
        attn_done,
        done_vectors[2],
        updown_done[:, ff_count:],
        done_vectors[3],
        done_vectors[4],
        done_vectors[5],
        updown_done[:, :ff_count],
        done_vectors[6],
        down_done,
        done_vectors[7],
    )


def solution(mesh):
    rows = P(AXES)
    tiles = P(AXES, None)
    pack = P(None, AXES, None)
    return jax.shard_map(
        functools.partial(shards, mesh.shape["dp"], mesh.shape["seq"]),
        mesh=mesh,
        in_specs=(
            pack, P(None, AXES), pack, rows, rows, tiles, rows, tiles, rows, rows, rows, tiles,
            rows, tiles, rows,
        ),
        out_specs=(
            pack, pack, rows, rows, tiles, rows, tiles, rows, rows, rows, tiles, rows, tiles, rows,
        ),
        check_vma=False,
    )
```

```python
import functools
import math

import jax
import jax.numpy as jnp
from jax import lax
from jax.experimental import pallas as pl
from jax.experimental.pallas import tpu as pltpu
from jax.sharding import PartitionSpec as P

HD = 64
AXES = ("dp", "seq")
NO_COST = pl.CostEstimate(flops=1, transcendentals=0, bytes_accessed=1)

branch_scale = 1.0 / math.sqrt(48.0)
norm_eps = 1e-05
neg_fill = -1e30
head_scale = HD ** (-0.5)


def layer_norm(values, norm_gain, norm_shift):
    center = values - jnp.mean(values, axis=-1, keepdims=True)
    spread = jnp.mean(center * center, axis=-1, keepdims=True)
    return center * lax.rsqrt(spread + norm_eps) * norm_gain + norm_shift


def gelu_and_slope(values):
    scale = math.sqrt(2.0 / math.pi)
    square = values * values
    gate = 0.5 * jnp.tanh(values * (scale + scale * 0.044715 * square)) + 0.5
    hidden = values * gate
    rise = 2.0 * scale + 6.0 * scale * 0.044715 * square
    return hidden, gate + hidden * (1.0 - gate) * rise


def product(first_op, second_op):
    return jnp.dot(first_op, second_op, preferred_element_type=jnp.float32)


def transpose_times(first_op, second_op):
    return jnp.einsum("tk,tn->kn", first_op, second_op, preferred_element_type=jnp.float32)


def times_transpose(first_op, second_op):
    return jnp.einsum("tn,kn->tk", first_op, second_op, preferred_element_type=jnp.float32)


def flip(array, bit, count):
    return lax.ppermute(array, AXES, [(i, i ^ bit) for i in range(count)])


def distance(place, order):
    return sum(bit for i, bit in enumerate(order) if (place >> i) & 1)


def assemble(pieces, order, me, count):
    size, rows, columns = pieces[0].shape

    def body(me_ref, *refs):
        sources, target, sem = refs[:-2], refs[-2], refs[-1]
        for place in range(count):
            owner = me_ref[0] ^ distance(place, order)
            pltpu.make_async_copy(
                sources[place // size].at[place % size], target.at[owner], sem
            ).start()
        pltpu.make_async_copy(target, target, sem).wait()

    return pl.pallas_call(
        body,
        grid_spec=pltpu.PrefetchScalarGridSpec(
            num_scalar_prefetch=1,
            grid=(1,),
            in_specs=[pl.BlockSpec(memory_space=pl.ANY)] * len(pieces),
            out_specs=pl.BlockSpec((count, rows, columns), lambda i, me_ref: (0, 0, 0)),
            scratch_shapes=[pltpu.SemaphoreType.DMA],
        ),
        out_shape=jax.ShapeDtypeStruct((count, rows, columns), pieces[0].dtype),
        cost_estimate=NO_COST,
        name="assemble",
    )(me.reshape(1), *pieces)


def gather_rows(held, order, me, count, ties):
    stages = len(order)
    done = held.shape[0].bit_length() - 1
    for bit in order[done : stages - 2]:
        held = after(held, *ties.get(bit, ()))
        held = jnp.concatenate([held, flip(held, bit, count)], axis=0)
    held = after(held, *ties.get(order[-2], ()))
    near = flip(held, order[-2], count)
    beside = flip(held, order[-1], count)
    near = after(near, *ties.get(order[-1], ()))
    pieces = [held, near, beside, flip(near, order[-1], count)]
    return assemble(pieces, order, me, count).reshape(count * held.shape[1], held.shape[2])


def pack(side, one, rest, parts):
    rows, columns = one.shape

    def body(side_ref, one_ref, rest_ref, packed):
        for i in range(parts):
            packed[i] = side_ref[:, i * columns : (i + 1) * columns]
        packed[parts] = one_ref[...]
        packed[parts + 1 :] = rest_ref[...]

    rest = rest.reshape(-1, rows, columns)
    return pl.pallas_call(
        body,
        out_shape=jax.ShapeDtypeStruct((parts + 1 + rest.shape[0], rows, columns), one.dtype),
        cost_estimate=NO_COST,
        name="pack",
    )(side, one, rest)


def unpack(packed, parts):
    count, total, rows, columns = packed.shape
    rest = total - parts - 1

    def body(source, side_ref, one_ref, rest_ref, held, come, go):
        def target(i):
            if i < parts:
                return side_ref.at[:, :, pl.ds(i * columns, columns)]
            return one_ref if i == parts else rest_ref.at[:, i - parts - 1]

        order = [parts] + list(range(parts)) + list(range(parts + 1, total))
        ins = [pltpu.make_async_copy(source.at[:, i], held.at[i], come.at[i]) for i in order]
        outs = [pltpu.make_async_copy(held.at[i], target(i), go.at[i]) for i in order]
        for copy in ins:
            copy.start()
        for first, second in zip(ins, outs):
            first.wait()
            second.start()
        for copy in outs:
            copy.wait()

    shapes = [(count, rows, parts * columns), (count, rows, columns), (count, rest, rows, columns)]
    out = pl.pallas_call(
        body,
        grid=(1,),
        in_specs=[pl.BlockSpec(memory_space=pl.ANY)],
        out_specs=[pl.BlockSpec(memory_space=pl.ANY)] * 3,
        scratch_shapes=[
            pltpu.VMEM((total, count, rows, columns), packed.dtype),
            pltpu.SemaphoreType.DMA((total,)),
            pltpu.SemaphoreType.DMA((total,)),
        ],
        out_shape=[jax.ShapeDtypeStruct(shape, packed.dtype) for shape in shapes],
        cost_estimate=NO_COST,
        name="unpack",
    )(packed)
    return [array.reshape(-1, array.shape[-1]) for array in out]


def disperse(parts, order, me, count):
    rows = parts[0].shape[0] // count
    columns = sum(part.shape[1] for part in parts)
    half = count // 2

    def body(me_ref, *refs):
        sources, (kept, gone, near, far) = refs[: len(parts)], refs[len(parts) : -4]
        near_sem, far_sem, kept_sem, gone_sem = refs[-4:]
        for target, sem, base in ((far, far_sem, half), (near, near_sem, 0)):
            for place in range(half):
                owner, left = me_ref[0] ^ distance(base + place, order[::-1]), 0
                for source in sources:
                    span = slice(left, left + source.shape[2])
                    pltpu.make_async_copy(
                        source.at[owner], target.at[place, :, span], sem
                    ).start()
                    left = span.stop
        pltpu.make_async_copy(far, far, far_sem).wait()
        send = pltpu.make_async_copy(far, gone, gone_sem)
        send.start()
        pltpu.make_async_copy(near, near, near_sem).wait()
        keep = pltpu.make_async_copy(near, kept, kept_sem)
        keep.start()
        send.wait()
        keep.wait()

    shape = (half, rows, columns)
    return pl.pallas_call(
        body,
        grid_spec=pltpu.PrefetchScalarGridSpec(
            num_scalar_prefetch=1,
            grid=(1,),
            in_specs=[pl.BlockSpec(memory_space=pl.ANY)] * len(parts),
            out_specs=[pl.BlockSpec(memory_space=pl.ANY)] * 2,
            scratch_shapes=[pltpu.VMEM(shape, parts[0].dtype)] * 2
            + [pltpu.SemaphoreType.DMA] * 4,
        ),
        out_shape=[jax.ShapeDtypeStruct(shape, parts[0].dtype)] * 2,
        cost_estimate=NO_COST,
        name="disperse",
    )(me.reshape(1), *[part.reshape(count, rows, part.shape[1]) for part in parts])


def add(first_term, second_term):
    return first_term.astype(jnp.float32) + second_term.astype(jnp.float32)


def begin_sum(parts, order, me, count):
    kept, gone = disperse(parts, order, me, count)
    return kept, flip(gone, order[0], count), gone


def advance(state, bit, count, *ties):
    kept, other, _ = state
    kept = after(kept, *ties)
    half = kept.shape[0] // 2
    gone = add(kept[half:], other[half:]).astype(jnp.bfloat16)
    kept = add(kept[:half], other[:half]).astype(jnp.bfloat16)
    return kept, flip(gone, bit, count), gone


def after(array, *others):
    return lax.optimization_barrier((array, *others))[0]


def nt(first_op, second_op):
    return lax.dot_general(
        first_op, second_op, (((1,), (1,)), ((), ())), preferred_element_type=jnp.float32
    )


def nn(first_op, second_op):
    return lax.dot_general(
        first_op, second_op, (((1,), (0,)), ((), ())), preferred_element_type=jnp.float32
    )


def lane_mask(shape, axis, head):
    place = lax.broadcasted_iota(jnp.int32, shape, axis)
    return (place < HD) if head == 0 else (place >= HD)


def fwd_kernel(info, q_ref, k_ref, v_ref, o_ref, lse_ref, vt_s, acc_s, m_s):
    which = pl.program_id(1)
    rows, width = q_ref.shape

    @pl.when(which == 0)
    def _():
        for slot in range(4):
            turned = v_ref[slot * rows : (slot + 1) * rows, :].astype(jnp.float32).T
            top = lane_mask((width, rows), 0, 0)
            vt_s[slot, 0] = jnp.where(top, turned, 1.0).astype(jnp.bfloat16)
            vt_s[slot, 1] = jnp.where(top, 1.0, turned).astype(jnp.bfloat16)

    query = q_ref[...] * jnp.bfloat16(head_scale)
    queries = [
        jnp.where(lane_mask((rows, width), 1, head), query, jnp.bfloat16(0)) for head in range(2)
    ]
    block_id = info[which]

    def visit(slot, diagonal):
        keys = k_ref[pl.ds(pl.multiple_of(slot * rows, rows), rows), :]
        for head in range(2):
            scores = nt(keys, queries[head])
            if diagonal:
                below = lax.broadcasted_iota(jnp.int32, (rows, rows), 0) <= (
                    lax.broadcasted_iota(jnp.int32, (rows, rows), 1)
                )
                scores = jnp.where(below, scores, neg_fill)
                peak = jnp.max(scores, axis=0, keepdims=True)
                raised = jnp.exp(scores - peak).astype(jnp.bfloat16)
                acc_s[head] = nn(vt_s[slot, head], raised)
            else:
                before = m_s[head : head + 1, :]
                peak = jnp.maximum(before, jnp.max(scores, axis=0, keepdims=True))
                raised = jnp.exp(scores - peak).astype(jnp.bfloat16)
                acc_s[head] = acc_s[head] * jnp.exp(before - peak) + nn(vt_s[slot, head], raised)
            m_s[head : head + 1, :] = peak

    visit(which, True)

    def step(block, carry):
        visit(info[4 + block], False)
        return carry

    lax.fori_loop(info[2 + which], block_id, step, 0)
    first, second = acc_s[0], acc_s[1]
    total0, total1 = first[HD : HD + 1, :], second[0:1, :]
    out = jnp.where(lane_mask((width, rows), 0, 0), first / total0, second / total1)
    o_ref[...] = out.T.astype(jnp.bfloat16)
    lse_ref[0, 0, 0:1, :] = m_s[0:1, :] + jnp.log(total0)
    lse_ref[0, 0, 1:2, :] = m_s[1:2, :] + jnp.log(total1)


def bwd_kernel(
    info, q_ref, k_ref, v_ref, o_ref, lse_ref, ga_ref, gb_ref, dq_ref, keep_ref, send_ref,
    kt_s, dk_s, dv_s, dq_s,
):
    which = pl.program_id(1)
    rows, width = q_ref.shape

    @pl.when(which == 0)
    def _():
        for slot in range(4):
            keys = k_ref[slot * rows : (slot + 1) * rows, :]
            kt_s[slot] = keys.astype(jnp.float32).T.astype(jnp.bfloat16)
        dk_s[...] = jnp.zeros_like(dk_s)
        dv_s[...] = jnp.zeros_like(dv_s)

    query = q_ref[...] * jnp.bfloat16(head_scale)
    grad = jnp.where(which == 0, ga_ref[...], gb_ref[...])
    joint = (grad.astype(jnp.float32) * o_ref[...].astype(jnp.float32)).T
    queries, grads, dots = [], [], []
    for head in range(2):
        lanes = lane_mask((rows, width), 1, head)
        queries.append(jnp.where(lanes, query, jnp.bfloat16(0)))
        grads.append(jnp.where(lanes, grad, jnp.bfloat16(0)))
        dots.append(jnp.sum(joint[head * HD : (head + 1) * HD], axis=0, keepdims=True))
    block_id = info[which]
    dq_s[...] = jnp.zeros_like(dq_s)

    def visit(slot, start, size):
        spot = pl.ds(pl.multiple_of(slot * rows + start, size), size)
        keys, values = k_ref[spot, :], v_ref[spot, :]
        keep, span = slice(start, rows), slice(start, start + size)
        for head in range(2):
            some, pulls = queries[head][keep], grads[head][keep]
            scores = nt(keys, some)
            probs = jnp.exp(scores - lse_ref[0, 0, head : head + 1, keep])
            if size < rows:
                below = lax.broadcasted_iota(jnp.int32, scores.shape, 0) <= (
                    lax.broadcasted_iota(jnp.int32, scores.shape, 1)
                )
                probs = jnp.where(below, probs, 0.0)
            dv_s[slot, span] += nn(probs.astype(jnp.bfloat16), pulls)
            pulled = nt(values, pulls)
            score_grad = (probs * (pulled - dots[head][:, keep])).astype(jnp.bfloat16)
            dk_s[slot, span] += nn(score_grad, some)
            part = nn(kt_s[slot, :, span], score_grad)
            lanes = slice(head * HD, (head + 1) * HD)
            dq_s[lanes, keep] += part[lanes]

    visit(which, 0, rows // 2)
    visit(which, rows // 2, rows // 2)

    def step(block, carry):
        visit(info[4 + block], 0, rows)
        return carry

    lax.fori_loop(info[2 + which], block_id, step, 0)
    dq_ref[...] = (dq_s[...] * head_scale).T.astype(jnp.bfloat16)

    @pl.when(which == 1)
    def _():
        for slot in range(4):
            target = (keep_ref, send_ref)[slot // 2]
            spot = slice((slot % 2) * rows, (slot % 2 + 1) * rows)
            target[0, spot, :] = dk_s[slot].astype(jnp.bfloat16)
            target[1, spot, :] = dv_s[slot].astype(jnp.bfloat16)


def attend_forward(info, query, pair):
    rows, columns = query.shape[0] // 2, query.shape[1]
    width = 2 * HD
    near = columns // width
    return pl.pallas_call(
        fwd_kernel,
        grid_spec=pltpu.PrefetchScalarGridSpec(
            num_scalar_prefetch=1,
            grid=(near, 2),
            in_specs=[
                pl.BlockSpec((rows, width), lambda p, w, s: (w, p)),
                pl.BlockSpec((4 * rows, width), lambda p, w, s: (0, p)),
                pl.BlockSpec((4 * rows, width), lambda p, w, s: (0, near + p)),
            ],
            out_specs=[
                pl.BlockSpec((rows, width), lambda p, w, s: (w, p)),
                pl.BlockSpec((1, 1, 8, rows), lambda p, w, s: (w, p, 0, 0)),
            ],
            scratch_shapes=[
                pltpu.VMEM((4, 2, width, rows), jnp.bfloat16),
                pltpu.VMEM((2, width, rows), jnp.float32),
                pltpu.VMEM((8, rows), jnp.float32),
            ],
        ),
        out_shape=[
            jax.ShapeDtypeStruct((2 * rows, columns), jnp.bfloat16),
            jax.ShapeDtypeStruct((2, near, 8, rows), jnp.float32),
        ],
        cost_estimate=NO_COST,
        name="attend_forward",
    )(info, query, pair, pair)


def attend_backward(info, query, pair, out, logsum, grad_own, grad_far):
    rows, columns = query.shape[0] // 2, query.shape[1]
    width = 2 * HD
    near = columns // width
    return pl.pallas_call(
        bwd_kernel,
        grid_spec=pltpu.PrefetchScalarGridSpec(
            num_scalar_prefetch=1,
            grid=(near, 2),
            in_specs=[
                pl.BlockSpec((rows, width), lambda p, w, s: (w, p)),
                pl.BlockSpec((4 * rows, width), lambda p, w, s: (0, p)),
                pl.BlockSpec((4 * rows, width), lambda p, w, s: (0, near + p)),
                pl.BlockSpec((rows, width), lambda p, w, s: (w, p)),
                pl.BlockSpec((1, 1, 8, rows), lambda p, w, s: (w, p, 0, 0)),
                pl.BlockSpec((rows, width), lambda p, w, s: (0, p)),
                pl.BlockSpec((rows, width), lambda p, w, s: (0, p)),
            ],
            out_specs=[
                pl.BlockSpec((rows, width), lambda p, w, s: (w, p)),
                pl.BlockSpec((2, 2 * rows, width), lambda p, w, s: (0, 0, p)),
                pl.BlockSpec((2, 2 * rows, width), lambda p, w, s: (0, 0, p)),
            ],
            scratch_shapes=[
                pltpu.VMEM((4, width, rows), jnp.bfloat16),
                pltpu.VMEM((4, rows, width), jnp.float32),
                pltpu.VMEM((4, rows, width), jnp.float32),
                pltpu.VMEM((width, rows), jnp.float32),
            ],
        ),
        out_shape=[
            jax.ShapeDtypeStruct((2 * rows, columns), jnp.bfloat16),
            jax.ShapeDtypeStruct((2, 2 * rows, columns), jnp.bfloat16),
            jax.ShapeDtypeStruct((2, 2 * rows, columns), jnp.bfloat16),
        ],
        cost_estimate=NO_COST,
        name="attend_backward",
    )(info, query, pair, pair, out, logsum, grad_own, grad_far)


def shards(
    dp_count, seq_count, tokens, starts, cotangent, attn_gain, attn_shift, attn_weight, attn_bias,
    proj_weight, proj_bias, mlp_gain, mlp_shift, up_weight, up_bias, down_weight, down_bias,
):
    count = dp_count * seq_count
    bits = [1 << i for i in range(count.bit_length() - 1)]
    core_bit, y_bit, x_bit, z_bits = bits[0], bits[1], bits[2], bits[3:]
    place = lax.axis_index("seq")
    me = lax.axis_index("dp") * seq_count + place
    half = place // (seq_count // 2)
    feature_count = tokens.shape[2]
    row_count = tokens.shape[1]
    ff_count = up_weight.shape[1]
    part = feature_count // count
    side_count = feature_count // 2

    def across(array):
        return lax.ppermute(array, "seq", [(i, seq_count - 1 - i) for i in range(seq_count)])

    def beside(array):
        return lax.ppermute(array, "seq", [(i, i ^ 1) for i in range(seq_count)])

    vectors = [attn_gain, attn_shift, attn_bias, proj_bias, mlp_gain, mlp_shift, up_bias, down_bias]
    total = sum(vector.shape[0] for vector in vectors)
    joined, spot = 0, 0
    for vector in vectors:
        joined = joined + jnp.pad(vector, (spot, total - spot - vector.shape[0]))
        spot += vector.shape[0]
    columns = joined.reshape(-1, part).T
    columns = jnp.pad(columns, ((0, 0), (0, 128 - columns.shape[1])))
    thirds = [attn_weight[:, i * side_count : (i + 1) * side_count] for i in range(6)]
    first = jnp.concatenate(thirds[0::2] + [columns], axis=1)
    second = jnp.concatenate(thirds[1::2] + [columns], axis=1)
    mine = jnp.where(half == 0, first, second)
    theirs = flip(jnp.where(half == 0, second, first), y_bit, count)
    ff_parts = ff_count // feature_count
    last_start = starts[0, -128:].reshape(1, 128)
    last_far = across(last_start)
    inputs = tokens[0]
    inputs_far = across(after(inputs, last_far))
    inputs_side = beside(inputs)
    inputs_side_far = beside(inputs_far)
    everyone_low = lax.optimization_barrier(
        jnp.concatenate([inputs, inputs_far, inputs_side, inputs_side_far], axis=0)
    )
    everyone = everyone_low.astype(jnp.float32)
    mean = jnp.mean(everyone, axis=-1, keepdims=True)
    spread = lax.rsqrt(
        jnp.mean((everyone - mean) * (everyone - mean), axis=-1, keepdims=True) + norm_eps
    )
    attn_all = gather_rows(
        jnp.stack([mine, theirs]), [y_bit] + z_bits[::-1] + [x_bit, core_bit], me, count,
        {core_bit: (mean, spread)},
    )
    packed = pack(up_weight, proj_weight, down_weight, ff_parts)
    packed = lax.all_gather(packed, AXES, axis=0)
    up_full, proj_full, down_full = unpack(packed, ff_parts)
    split = jnp.maximum(jnp.max(last_start), jnp.max(last_far)) > 0
    attn_full = attn_all[:, : 3 * side_count]
    lanes = attn_all[:, 3 * side_count :].astype(jnp.float32).T
    full_vectors, spot = [], 0
    for vector in vectors:
        size = vector.shape[0] // part
        rows = lanes[spot : spot + size].reshape(size, count, part)
        full_vectors.append(rows.transpose(1, 0, 2).reshape(-1))
        spot += size
    (
        attn_gain_full, attn_shift_full, attn_bias_full, proj_bias_full,
        mlp_gain_full, mlp_shift_full, up_bias_full, down_bias_full,
    ) = full_vectors

    far_place = seq_count - 1 - place
    spots = jnp.arange(8, dtype=jnp.int32)
    low = jnp.where(split, seq_count // 2, 0).astype(jnp.int32)
    block = spots - 4
    slot = jnp.where(
        block == place,
        0,
        jnp.where(block == far_place, 1, jnp.where(block == (place ^ 1), 2, 3)),
    )
    asked = jnp.where(spots % 2 == 0, place, far_place)
    info = jnp.where(
        spots < 2, asked, jnp.where(spots < 4, jnp.where(asked >= seq_count // 2, low, 0), slot)
    ).astype(jnp.int32)

    normed = (everyone - mean) * spread * attn_gain_full + attn_shift_full
    normed = normed.astype(jnp.bfloat16)
    normed_pair = normed[: 2 * row_count]
    query_bias = lax.dynamic_slice_in_dim(attn_bias_full, half * side_count, side_count)
    value_bias = lax.dynamic_slice_in_dim(
        attn_bias_full, feature_count + half * side_count, side_count
    )
    pair_bias = jnp.concatenate([jnp.zeros((side_count,), jnp.float32), value_bias])
    query = (product(normed_pair, attn_full[:, :side_count]) + query_bias).astype(jnp.bfloat16)
    pair = (product(normed, attn_full[:, side_count:]) + pair_bias).astype(jnp.bfloat16)
    out, logsum = attend_forward(info, query, pair)
    returned = across(out[row_count:])
    out_own = out[:row_count]
    attended = jnp.where(
        half == 0,
        jnp.concatenate([out_own, returned], axis=1),
        jnp.concatenate([returned, out_own], axis=1),
    )
    inputs = inputs.astype(jnp.float32)
    middle = inputs + branch_scale * (product(attended, proj_full) + proj_bias_full)
    normed_mlp = layer_norm(middle, mlp_gain_full, mlp_shift_full).astype(jnp.bfloat16)
    hidden_pre = product(normed_mlp, up_full) + up_bias_full
    hidden, slope = gelu_and_slope(hidden_pre)
    hidden, slope = lax.optimization_barrier(
        (hidden.astype(jnp.bfloat16), slope.astype(jnp.bfloat16))
    )

    out_grad = cotangent[0].astype(jnp.float32)
    down_in = (branch_scale * out_grad).astype(jnp.bfloat16)
    down_bias_grad = jnp.sum(down_in, axis=0, dtype=jnp.float32)
    down_order = [core_bit, x_bit, y_bit] + z_bits
    up_order = [core_bit, y_bit, x_bit] + z_bits
    down_weight_grad = transpose_times(hidden, down_in).astype(jnp.bfloat16)
    down_sum = begin_sum([down_weight_grad], down_order, me, count)
    hidden_grad = times_transpose(after(down_in, down_sum[2]), down_full)
    pre_grad = (hidden_grad * slope.astype(jnp.float32)).astype(jnp.bfloat16)
    up_bias_grad = jnp.sum(pre_grad, axis=0, dtype=jnp.float32)
    mlp_pull = jax.vjp(layer_norm, middle, mlp_gain_full, mlp_shift_full)[1]
    middle_part, mlp_gain_grad, mlp_shift_grad = mlp_pull(
        times_transpose(pre_grad, up_full)
    )
    middle_grad = out_grad + middle_part
    proj_in = (branch_scale * middle_grad).astype(jnp.bfloat16)
    proj_bias_grad = jnp.sum(proj_in, axis=0, dtype=jnp.float32)
    proj_mine = lax.dynamic_slice_in_dim(proj_full, half * side_count, side_count)
    proj_theirs = lax.dynamic_slice_in_dim(proj_full, (1 - half) * side_count, side_count)
    grad_gone = times_transpose(proj_in, proj_theirs).astype(jnp.bfloat16)
    grad_far = across(grad_gone)
    grad_own = times_transpose(proj_in, proj_mine).astype(jnp.bfloat16)
    pre_grad = after(pre_grad, grad_gone)
    up_weight_grad = transpose_times(normed_mlp, pre_grad).astype(jnp.bfloat16)
    proj_late = after(proj_in, grad_gone)
    proj_weight_grad = transpose_times(attended, proj_late).astype(jnp.bfloat16)
    up_weight_grad = after(up_weight_grad, grad_far, down_sum[1])
    up_sum = begin_sum([up_weight_grad, proj_weight_grad], up_order, me, count)
    down_sum = advance(down_sum, down_order[1], count, up_sum[2])
    up_sum = advance(up_sum, up_order[1], count, down_sum[2])
    query_grad, pair_grad, pair_gone = attend_backward(
        info, query, pair, out, logsum, after(grad_own, up_sum[2]), grad_far
    )
    down_sum = advance(down_sum, down_order[2], count, query_grad)
    up_sum = advance(up_sum, up_order[2], count, down_sum[2], query_grad)
    pair_grad = add(after(pair_grad, up_sum[2]), beside(pair_gone)).astype(jnp.bfloat16)
    mixed_grad = jnp.concatenate([query_grad, pair_grad[0], pair_grad[1]], axis=1)
    normed_grad = times_transpose(mixed_grad, attn_full)
    down_sum = advance(down_sum, down_order[3], count, normed_grad)
    far_grad = across(normed_grad[row_count:].astype(jnp.bfloat16))
    centered = after(everyone_low[: 2 * row_count], query_grad).astype(jnp.float32)
    centered = (centered - mean[: 2 * row_count]) * spread[: 2 * row_count]
    attn_gain_grad = jnp.sum(normed_grad * centered, axis=0)
    attn_shift_grad = jnp.sum(normed_grad, axis=0)
    attn_weight_grad = transpose_times(normed_pair, after(mixed_grad, down_sum[2])).astype(jnp.bfloat16)
    column_sums = jnp.sum(mixed_grad, axis=0, dtype=jnp.float32).reshape(3, side_count)[::2]
    attn_bias_grad = jnp.where(
        half == 0,
        jnp.pad(column_sums, ((0, 0), (0, side_count))),
        jnp.pad(column_sums, ((0, 0), (side_count, 0))),
    ).reshape(-1)
    vector_grads = [
        attn_gain_grad, attn_shift_grad, attn_bias_grad, proj_bias_grad,
        mlp_gain_grad, mlp_shift_grad, up_bias_grad, down_bias_grad,
    ]
    grad_columns = jnp.concatenate(
        [
            grad.reshape(count, -1, part).transpose(1, 0, 2).reshape(-1, feature_count)
            for grad in vector_grads
        ],
        axis=0,
    ).T
    grad_columns = jnp.pad(grad_columns, ((0, 0), (0, 128 - grad_columns.shape[1])))
    attn_order = [core_bit, x_bit] + z_bits + [y_bit]
    attn_sum = begin_sum(
        [attn_weight_grad, grad_columns.astype(jnp.bfloat16)], attn_order, me, count
    )
    up_sum = advance(up_sum, up_order[3], count, attn_sum[2])
    attn_sum = advance(attn_sum, attn_order[1], count, up_sum[2])
    output = middle + branch_scale * (
        product(after(hidden, attn_sum[2]), down_full) + down_bias_full
    )
    output = output.astype(jnp.bfloat16)
    for bit in down_order[4:]:
        down_sum = advance(down_sum, bit, count, output)
    for i in range(3, len(z_bits) + 2):
        up_sum = advance(up_sum, up_order[i + 1], count, down_sum[2], attn_sum[2])
        attn_sum = advance(attn_sum, attn_order[i - 1], count, up_sum[2])
    attn_sum = advance(attn_sum, attn_order[-2], count)
    far_grad = after(far_grad, attn_sum[2])
    scaled = (normed_grad[:row_count] + far_grad.astype(jnp.float32)) * attn_gain_full
    centered_own = centered[:row_count]
    input_part = spread[:row_count] * (
        scaled
        - jnp.mean(scaled, axis=-1, keepdims=True)
        - centered_own * jnp.mean(scaled * centered_own, axis=-1, keepdims=True)
    )
    grad_in = (middle_grad + input_part).astype(jnp.bfloat16)
    down_done = add(down_sum[0][0], after(down_sum[1], grad_in)[0])
    updown_done = add(up_sum[0][0], after(up_sum[1], attn_sum[2])[0])
    mine = add(attn_sum[0][0], attn_sum[1][0])
    other = add(attn_sum[0][1], attn_sum[1][1]).astype(jnp.bfloat16)
    other = flip(other, y_bit, count).astype(jnp.float32)
    first = jnp.where(half == 0, mine, other)[:, : 3 * side_count].reshape(part, 3, 1, side_count)
    second = jnp.where(half == 0, other, mine)[:, : 3 * side_count].reshape(part, 3, 1, side_count)
    attn_done = jnp.concatenate([first, second], axis=2).reshape(part, 3 * feature_count)
    done_lanes = (mine + other)[:, 3 * side_count :].T
    done_vectors, spot = [], 0
    for vector in vectors:
        size = vector.shape[0] // part
        done_vectors.append(done_lanes[spot : spot + size].reshape(-1))
        spot += size
    return (
        output[None],
        grad_in[None],
        done_vectors[0],
        done_vectors[1],
        attn_done,
        done_vectors[2],
        updown_done[:, ff_count:],
        done_vectors[3],
        done_vectors[4],
        done_vectors[5],
        updown_done[:, :ff_count],
        done_vectors[6],
        down_done,
        done_vectors[7],
    )


def solution(mesh):
    rows = P(AXES)
    tiles = P(AXES, None)
    pack = P(None, AXES, None)
    return jax.shard_map(
        functools.partial(shards, mesh.shape["dp"], mesh.shape["seq"]),
        mesh=mesh,
        in_specs=(
            pack, P(None, AXES), pack, rows, rows, tiles, rows, tiles, rows, rows, rows, tiles,
            rows, tiles, rows,
        ),
        out_specs=(
            pack, pack, rows, rows, tiles, rows, tiles, rows, rows, rows, tiles, rows, tiles, rows,
        ),
        check_vma=False,
    )
```

```python
import functools
import math

import jax
import jax.numpy as jnp
from jax import lax
from jax.experimental import pallas as pl
from jax.experimental.pallas import tpu as pltpu
from jax.sharding import PartitionSpec as P

HD = 64
AXES = ("dp", "seq")
NO_COST = pl.CostEstimate(flops=1, transcendentals=0, bytes_accessed=1)

branch_scale = 1.0 / math.sqrt(48.0)
norm_eps = 1e-05
neg_fill = -1e30
head_scale = HD ** (-0.5)


def layer_norm(values, norm_gain, norm_shift):
    center = values - jnp.mean(values, axis=-1, keepdims=True)
    spread = jnp.mean(center * center, axis=-1, keepdims=True)
    return center * lax.rsqrt(spread + norm_eps) * norm_gain + norm_shift


def gelu_and_slope(values):
    scale = math.sqrt(2.0 / math.pi)
    square = values * values
    gate = 0.5 * jnp.tanh(values * (scale + scale * 0.044715 * square)) + 0.5
    hidden = values * gate
    rise = 2.0 * scale + 6.0 * scale * 0.044715 * square
    return hidden, gate + hidden * (1.0 - gate) * rise


def product(first_op, second_op):
    return jnp.dot(first_op, second_op, preferred_element_type=jnp.float32)


def transpose_times(first_op, second_op):
    return jnp.einsum("tk,tn->kn", first_op, second_op, preferred_element_type=jnp.float32)


def times_transpose(first_op, second_op):
    return jnp.einsum("tn,kn->tk", first_op, second_op, preferred_element_type=jnp.float32)


def flip(array, bit, count):
    return lax.ppermute(array, AXES, [(i, i ^ bit) for i in range(count)])


def distance(place, order):
    return sum(bit for i, bit in enumerate(order) if (place >> i) & 1)


def assemble(pieces, order, me, count):
    size, rows, columns = pieces[0].shape

    def body(me_ref, *refs):
        sources, target, sem = refs[:-2], refs[-2], refs[-1]
        for place in range(count):
            owner = me_ref[0] ^ distance(place, order)
            pltpu.make_async_copy(
                sources[place // size].at[place % size], target.at[owner], sem
            ).start()
        pltpu.make_async_copy(target, target, sem).wait()

    return pl.pallas_call(
        body,
        grid_spec=pltpu.PrefetchScalarGridSpec(
            num_scalar_prefetch=1,
            grid=(1,),
            in_specs=[pl.BlockSpec(memory_space=pl.ANY)] * len(pieces),
            out_specs=pl.BlockSpec((count, rows, columns), lambda i, me_ref: (0, 0, 0)),
            scratch_shapes=[pltpu.SemaphoreType.DMA],
        ),
        out_shape=jax.ShapeDtypeStruct((count, rows, columns), pieces[0].dtype),
        cost_estimate=NO_COST,
        name="assemble",
    )(me.reshape(1), *pieces)


def gather_rows(held, order, me, count, ties):
    stages = len(order)
    done = held.shape[0].bit_length() - 1
    for bit in order[done : stages - 2]:
        held = after(held, *ties.get(bit, ()))
        held = jnp.concatenate([held, flip(held, bit, count)], axis=0)
    held = after(held, *ties.get(order[-2], ()))
    near = flip(held, order[-2], count)
    beside = flip(held, order[-1], count)
    near = after(near, *ties.get(order[-1], ()))
    pieces = [held, near, beside, flip(near, order[-1], count)]
    return assemble(pieces, order, me, count).reshape(count * held.shape[1], held.shape[2])


def pack(side, one, rest, parts):
    rows, columns = one.shape

    def body(side_ref, one_ref, rest_ref, packed):
        for i in range(parts):
            packed[i] = side_ref[:, i * columns : (i + 1) * columns]
        packed[parts] = one_ref[...]
        packed[parts + 1 :] = rest_ref[...]

    rest = rest.reshape(-1, rows, columns)
    return pl.pallas_call(
        body,
        out_shape=jax.ShapeDtypeStruct((parts + 1 + rest.shape[0], rows, columns), one.dtype),
        cost_estimate=NO_COST,
        name="pack",
    )(side, one, rest)


def unpack(packed, parts):
    count, total, rows, columns = packed.shape
    rest = total - parts - 1

    def body(source, side_ref, one_ref, rest_ref, held, come, go):
        def target(i):
            if i < parts:
                return side_ref.at[:, :, pl.ds(i * columns, columns)]
            return one_ref if i == parts else rest_ref.at[:, i - parts - 1]

        order = [parts] + list(range(parts)) + list(range(parts + 1, total))
        ins = [pltpu.make_async_copy(source.at[:, i], held.at[i], come.at[i]) for i in order]
        outs = [pltpu.make_async_copy(held.at[i], target(i), go.at[i]) for i in order]
        for copy in ins:
            copy.start()
        for first, second in zip(ins, outs):
            first.wait()
            second.start()
        for copy in outs:
            copy.wait()

    shapes = [(count, rows, parts * columns), (count, rows, columns), (count, rest, rows, columns)]
    out = pl.pallas_call(
        body,
        grid=(1,),
        in_specs=[pl.BlockSpec(memory_space=pl.ANY)],
        out_specs=[pl.BlockSpec(memory_space=pl.ANY)] * 3,
        scratch_shapes=[
            pltpu.VMEM((total, count, rows, columns), packed.dtype),
            pltpu.SemaphoreType.DMA((total,)),
            pltpu.SemaphoreType.DMA((total,)),
        ],
        out_shape=[jax.ShapeDtypeStruct(shape, packed.dtype) for shape in shapes],
        cost_estimate=NO_COST,
        name="unpack",
    )(packed)
    return [array.reshape(-1, array.shape[-1]) for array in out]


def disperse(parts, order, me, count):
    rows = parts[0].shape[0] // count
    columns = sum(part.shape[1] for part in parts)
    half = count // 2

    def body(me_ref, *refs):
        sources, (kept, gone, near, far) = refs[: len(parts)], refs[len(parts) : -4]
        near_sem, far_sem, kept_sem, gone_sem = refs[-4:]
        for target, sem, base in ((far, far_sem, half), (near, near_sem, 0)):
            for place in range(half):
                owner, left = me_ref[0] ^ distance(base + place, order[::-1]), 0
                for source in sources:
                    span = slice(left, left + source.shape[2])
                    pltpu.make_async_copy(
                        source.at[owner], target.at[place, :, span], sem
                    ).start()
                    left = span.stop
        pltpu.make_async_copy(far, far, far_sem).wait()
        send = pltpu.make_async_copy(far, gone, gone_sem)
        send.start()
        pltpu.make_async_copy(near, near, near_sem).wait()
        keep = pltpu.make_async_copy(near, kept, kept_sem)
        keep.start()
        send.wait()
        keep.wait()

    shape = (half, rows, columns)
    return pl.pallas_call(
        body,
        grid_spec=pltpu.PrefetchScalarGridSpec(
            num_scalar_prefetch=1,
            grid=(1,),
            in_specs=[pl.BlockSpec(memory_space=pl.ANY)] * len(parts),
            out_specs=[pl.BlockSpec(memory_space=pl.ANY)] * 2,
            scratch_shapes=[pltpu.VMEM(shape, parts[0].dtype)] * 2
            + [pltpu.SemaphoreType.DMA] * 4,
        ),
        out_shape=[jax.ShapeDtypeStruct(shape, parts[0].dtype)] * 2,
        cost_estimate=NO_COST,
        name="disperse",
    )(me.reshape(1), *[part.reshape(count, rows, part.shape[1]) for part in parts])


def add(first_term, second_term):
    return first_term.astype(jnp.float32) + second_term.astype(jnp.float32)


def begin_sum(parts, order, me, count):
    kept, gone = disperse(parts, order, me, count)
    return kept, flip(gone, order[0], count), gone


def advance(state, bit, count, *ties):
    kept, other, _ = state
    kept = after(kept, *ties)
    half = kept.shape[0] // 2
    gone = add(kept[half:], other[half:]).astype(jnp.bfloat16)
    kept = add(kept[:half], other[:half]).astype(jnp.bfloat16)
    return kept, flip(gone, bit, count), gone


def after(array, *others):
    return lax.optimization_barrier((array, *others))[0]


def nt(first_op, second_op):
    return lax.dot_general(
        first_op, second_op, (((1,), (1,)), ((), ())), preferred_element_type=jnp.float32
    )


def nn(first_op, second_op):
    return lax.dot_general(
        first_op, second_op, (((1,), (0,)), ((), ())), preferred_element_type=jnp.float32
    )


def lane_mask(shape, axis, head):
    place = lax.broadcasted_iota(jnp.int32, shape, axis)
    return (place < HD) if head == 0 else (place >= HD)


def fwd_kernel(info, q_ref, k_ref, v_ref, o_ref, lse_ref, vt_s, acc_s, m_s):
    which = pl.program_id(1)
    rows, width = q_ref.shape

    @pl.when(which == 0)
    def _():
        for slot in range(4):
            turned = v_ref[slot * rows : (slot + 1) * rows, :].astype(jnp.float32).T
            top = lane_mask((width, rows), 0, 0)
            vt_s[slot, 0] = jnp.where(top, turned, 1.0).astype(jnp.bfloat16)
            vt_s[slot, 1] = jnp.where(top, 1.0, turned).astype(jnp.bfloat16)

    query = q_ref[...] * jnp.bfloat16(head_scale)
    queries = [
        jnp.where(lane_mask((rows, width), 1, head), query, jnp.bfloat16(0)) for head in range(2)
    ]
    block_id = info[which]

    def visit(slot, diagonal):
        keys = k_ref[pl.ds(pl.multiple_of(slot * rows, rows), rows), :]
        for head in range(2):
            scores = nt(keys, queries[head])
            if diagonal:
                below = lax.broadcasted_iota(jnp.int32, (rows, rows), 0) <= (
                    lax.broadcasted_iota(jnp.int32, (rows, rows), 1)
                )
                scores = jnp.where(below, scores, neg_fill)
                peak = jnp.max(scores, axis=0, keepdims=True)
                raised = jnp.exp(scores - peak).astype(jnp.bfloat16)
                acc_s[head] = nn(vt_s[slot, head], raised)
            else:
                before = m_s[head : head + 1, :]
                peak = jnp.maximum(before, jnp.max(scores, axis=0, keepdims=True))
                raised = jnp.exp(scores - peak).astype(jnp.bfloat16)
                acc_s[head] = acc_s[head] * jnp.exp(before - peak) + nn(vt_s[slot, head], raised)
            m_s[head : head + 1, :] = peak

    visit(which, True)

    def step(block, carry):
        visit(info[4 + block], False)
        return carry

    lax.fori_loop(info[2 + which], block_id, step, 0)
    first, second = acc_s[0], acc_s[1]
    total0, total1 = first[HD : HD + 1, :], second[0:1, :]
    out = jnp.where(lane_mask((width, rows), 0, 0), first / total0, second / total1)
    o_ref[...] = out.T.astype(jnp.bfloat16)
    lse_ref[0, 0, 0:1, :] = m_s[0:1, :] + jnp.log(total0)
    lse_ref[0, 0, 1:2, :] = m_s[1:2, :] + jnp.log(total1)


def bwd_kernel(
    info, q_ref, k_ref, v_ref, o_ref, lse_ref, ga_ref, gb_ref, dq_ref, keep_ref, send_ref,
    kt_s, dk_s, dv_s, dq_s,
):
    which = pl.program_id(1)
    rows, width = q_ref.shape

    @pl.when(which == 0)
    def _():
        for slot in range(4):
            keys = k_ref[slot * rows : (slot + 1) * rows, :]
            kt_s[slot] = keys.astype(jnp.float32).T.astype(jnp.bfloat16)
        dk_s[...] = jnp.zeros_like(dk_s)
        dv_s[...] = jnp.zeros_like(dv_s)

    query = q_ref[...] * jnp.bfloat16(head_scale)
    grad = jnp.where(which == 0, ga_ref[...], gb_ref[...])
    joint = (grad.astype(jnp.float32) * o_ref[...].astype(jnp.float32)).T
    queries, grads, dots = [], [], []
    for head in range(2):
        lanes = lane_mask((rows, width), 1, head)
        queries.append(jnp.where(lanes, query, jnp.bfloat16(0)))
        grads.append(jnp.where(lanes, grad, jnp.bfloat16(0)))
        dots.append(jnp.sum(joint[head * HD : (head + 1) * HD], axis=0, keepdims=True))
    block_id = info[which]
    dq_s[...] = jnp.zeros_like(dq_s)

    def visit(slot, start, size):
        spot = pl.ds(pl.multiple_of(slot * rows + start, size), size)
        keys, values = k_ref[spot, :], v_ref[spot, :]
        keep, span = slice(start, rows), slice(start, start + size)
        for head in range(2):
            some, pulls = queries[head][keep], grads[head][keep]
            scores = nt(keys, some)
            probs = jnp.exp(scores - lse_ref[0, 0, head : head + 1, keep])
            if size < rows:
                below = lax.broadcasted_iota(jnp.int32, scores.shape, 0) <= (
                    lax.broadcasted_iota(jnp.int32, scores.shape, 1)
                )
                probs = jnp.where(below, probs, 0.0)
            dv_s[slot, span] += nn(probs.astype(jnp.bfloat16), pulls)
            pulled = nt(values, pulls)
            score_grad = (probs * (pulled - dots[head][:, keep])).astype(jnp.bfloat16)
            dk_s[slot, span] += nn(score_grad, some)
            part = nn(kt_s[slot, :, span], score_grad)
            lanes = slice(head * HD, (head + 1) * HD)
            dq_s[lanes, keep] += part[lanes]

    visit(which, 0, rows // 2)
    visit(which, rows // 2, rows // 2)

    def step(block, carry):
        visit(info[4 + block], 0, rows)
        return carry

    lax.fori_loop(info[2 + which], block_id, step, 0)
    dq_ref[...] = (dq_s[...] * head_scale).T.astype(jnp.bfloat16)

    @pl.when(which == 1)
    def _():
        for slot in range(4):
            target = (keep_ref, send_ref)[slot // 2]
            spot = slice((slot % 2) * rows, (slot % 2 + 1) * rows)
            target[0, spot, :] = dk_s[slot].astype(jnp.bfloat16)
            target[1, spot, :] = dv_s[slot].astype(jnp.bfloat16)


def attend_forward(info, query, pair):
    rows, columns = query.shape[0] // 2, query.shape[1]
    width = 2 * HD
    near = columns // width
    return pl.pallas_call(
        fwd_kernel,
        grid_spec=pltpu.PrefetchScalarGridSpec(
            num_scalar_prefetch=1,
            grid=(near, 2),
            in_specs=[
                pl.BlockSpec((rows, width), lambda p, w, s: (w, p)),
                pl.BlockSpec((4 * rows, width), lambda p, w, s: (0, p)),
                pl.BlockSpec((4 * rows, width), lambda p, w, s: (0, near + p)),
            ],
            out_specs=[
                pl.BlockSpec((rows, width), lambda p, w, s: (w, p)),
                pl.BlockSpec((1, 1, 8, rows), lambda p, w, s: (w, p, 0, 0)),
            ],
            scratch_shapes=[
                pltpu.VMEM((4, 2, width, rows), jnp.bfloat16),
                pltpu.VMEM((2, width, rows), jnp.float32),
                pltpu.VMEM((8, rows), jnp.float32),
            ],
        ),
        out_shape=[
            jax.ShapeDtypeStruct((2 * rows, columns), jnp.bfloat16),
            jax.ShapeDtypeStruct((2, near, 8, rows), jnp.float32),
        ],
        cost_estimate=NO_COST,
        name="attend_forward",
    )(info, query, pair, pair)


def attend_backward(info, query, pair, out, logsum, grad_own, grad_far):
    rows, columns = query.shape[0] // 2, query.shape[1]
    width = 2 * HD
    near = columns // width
    return pl.pallas_call(
        bwd_kernel,
        grid_spec=pltpu.PrefetchScalarGridSpec(
            num_scalar_prefetch=1,
            grid=(near, 2),
            in_specs=[
                pl.BlockSpec((rows, width), lambda p, w, s: (w, p)),
                pl.BlockSpec((4 * rows, width), lambda p, w, s: (0, p)),
                pl.BlockSpec((4 * rows, width), lambda p, w, s: (0, near + p)),
                pl.BlockSpec((rows, width), lambda p, w, s: (w, p)),
                pl.BlockSpec((1, 1, 8, rows), lambda p, w, s: (w, p, 0, 0)),
                pl.BlockSpec((rows, width), lambda p, w, s: (0, p)),
                pl.BlockSpec((rows, width), lambda p, w, s: (0, p)),
            ],
            out_specs=[
                pl.BlockSpec((rows, width), lambda p, w, s: (w, p)),
                pl.BlockSpec((2, 2 * rows, width), lambda p, w, s: (0, 0, p)),
                pl.BlockSpec((2, 2 * rows, width), lambda p, w, s: (0, 0, p)),
            ],
            scratch_shapes=[
                pltpu.VMEM((4, width, rows), jnp.bfloat16),
                pltpu.VMEM((4, rows, width), jnp.float32),
                pltpu.VMEM((4, rows, width), jnp.float32),
                pltpu.VMEM((width, rows), jnp.float32),
            ],
        ),
        out_shape=[
            jax.ShapeDtypeStruct((2 * rows, columns), jnp.bfloat16),
            jax.ShapeDtypeStruct((2, 2 * rows, columns), jnp.bfloat16),
            jax.ShapeDtypeStruct((2, 2 * rows, columns), jnp.bfloat16),
        ],
        cost_estimate=NO_COST,
        name="attend_backward",
    )(info, query, pair, pair, out, logsum, grad_own, grad_far)


def shards(
    dp_count, seq_count, tokens, starts, cotangent, attn_gain, attn_shift, attn_weight, attn_bias,
    proj_weight, proj_bias, mlp_gain, mlp_shift, up_weight, up_bias, down_weight, down_bias,
):
    count = dp_count * seq_count
    bits = [1 << i for i in range(count.bit_length() - 1)]
    core_bit, y_bit, x_bit, z_bits = bits[0], bits[1], bits[2], bits[3:]
    place = lax.axis_index("seq")
    me = lax.axis_index("dp") * seq_count + place
    half = place // (seq_count // 2)
    feature_count = tokens.shape[2]
    row_count = tokens.shape[1]
    ff_count = up_weight.shape[1]
    part = feature_count // count
    side_count = feature_count // 2

    def across(array):
        return lax.ppermute(array, "seq", [(i, seq_count - 1 - i) for i in range(seq_count)])

    def beside(array):
        return lax.ppermute(array, "seq", [(i, i ^ 1) for i in range(seq_count)])

    vectors = [attn_gain, attn_shift, attn_bias, proj_bias, mlp_gain, mlp_shift, up_bias, down_bias]
    total = sum(vector.shape[0] for vector in vectors)
    joined, spot = 0, 0
    for vector in vectors:
        joined = joined + jnp.pad(vector, (spot, total - spot - vector.shape[0]))
        spot += vector.shape[0]
    columns = joined.reshape(-1, part).T
    columns = jnp.pad(columns, ((0, 0), (0, 128 - columns.shape[1])))
    thirds = [attn_weight[:, i * side_count : (i + 1) * side_count] for i in range(6)]
    first = jnp.concatenate(thirds[0::2] + [columns], axis=1)
    second = jnp.concatenate(thirds[1::2] + [columns], axis=1)
    mine = jnp.where(half == 0, first, second)
    theirs = flip(jnp.where(half == 0, second, first), y_bit, count)
    ff_parts = ff_count // feature_count
    last_start = starts[0, -128:].reshape(1, 128)
    last_far = across(last_start)
    inputs = tokens[0]
    inputs_far = across(after(inputs, last_far))
    inputs_side = beside(inputs)
    inputs_side_far = beside(inputs_far)
    everyone_low = lax.optimization_barrier(
        jnp.concatenate([inputs, inputs_far, inputs_side, inputs_side_far], axis=0)
    )
    everyone = everyone_low.astype(jnp.float32)
    mean = jnp.mean(everyone, axis=-1, keepdims=True)
    spread = lax.rsqrt(
        jnp.mean((everyone - mean) * (everyone - mean), axis=-1, keepdims=True) + norm_eps
    )
    attn_all = gather_rows(
        jnp.stack([mine, theirs]), [y_bit] + z_bits[::-1] + [x_bit, core_bit], me, count,
        {core_bit: (mean, spread)},
    )
    packed = pack(up_weight, proj_weight, down_weight, ff_parts)
    packed = lax.all_gather(packed, AXES, axis=0)
    up_full, proj_full, down_full = unpack(packed, ff_parts)
    split = jnp.maximum(jnp.max(last_start), jnp.max(last_far)) > 0
    attn_full = attn_all[:, : 3 * side_count]
    lanes = attn_all[:, 3 * side_count :].astype(jnp.float32).T
    full_vectors, spot = [], 0
    for vector in vectors:
        size = vector.shape[0] // part
        rows = lanes[spot : spot + size].reshape(size, count, part)
        full_vectors.append(rows.transpose(1, 0, 2).reshape(-1))
        spot += size
    (
        attn_gain_full, attn_shift_full, attn_bias_full, proj_bias_full,
        mlp_gain_full, mlp_shift_full, up_bias_full, down_bias_full,
    ) = full_vectors

    far_place = seq_count - 1 - place
    spots = jnp.arange(8, dtype=jnp.int32)
    low = jnp.where(split, seq_count // 2, 0).astype(jnp.int32)
    block = spots - 4
    slot = jnp.where(
        block == place,
        0,
        jnp.where(block == far_place, 1, jnp.where(block == (place ^ 1), 2, 3)),
    )
    asked = jnp.where(spots % 2 == 0, place, far_place)
    info = jnp.where(
        spots < 2, asked, jnp.where(spots < 4, jnp.where(asked >= seq_count // 2, low, 0), slot)
    ).astype(jnp.int32)

    normed = (everyone - mean) * spread * attn_gain_full + attn_shift_full
    normed = normed.astype(jnp.bfloat16)
    normed_pair = normed[: 2 * row_count]
    query_bias = lax.dynamic_slice_in_dim(attn_bias_full, half * side_count, side_count)
    value_bias = lax.dynamic_slice_in_dim(
        attn_bias_full, feature_count + half * side_count, side_count
    )
    pair_bias = jnp.concatenate([jnp.zeros((side_count,), jnp.float32), value_bias])
    query = (product(normed_pair, attn_full[:, :side_count]) + query_bias).astype(jnp.bfloat16)
    pair = (product(normed, attn_full[:, side_count:]) + pair_bias).astype(jnp.bfloat16)
    out, logsum = attend_forward(info, query, pair)
    returned = across(out[row_count:])
    out_own = out[:row_count]
    attended = jnp.where(
        half == 0,
        jnp.concatenate([out_own, returned], axis=1),
        jnp.concatenate([returned, out_own], axis=1),
    )
    inputs = inputs.astype(jnp.float32)
    middle = inputs + branch_scale * (product(attended, proj_full) + proj_bias_full)
    normed_mlp = layer_norm(middle, mlp_gain_full, mlp_shift_full).astype(jnp.bfloat16)
    hidden_pre = product(normed_mlp, up_full) + up_bias_full
    hidden, slope = gelu_and_slope(hidden_pre)
    hidden, slope = lax.optimization_barrier(
        (hidden.astype(jnp.bfloat16), slope.astype(jnp.bfloat16))
    )

    out_grad = cotangent[0].astype(jnp.float32)
    down_in = (branch_scale * out_grad).astype(jnp.bfloat16)
    down_bias_grad = jnp.sum(down_in, axis=0, dtype=jnp.float32)
    down_order = [core_bit, x_bit, y_bit] + z_bits
    up_order = [core_bit, y_bit, x_bit] + z_bits
    down_weight_grad = transpose_times(hidden, down_in).astype(jnp.bfloat16)
    down_sum = begin_sum([down_weight_grad], down_order, me, count)
    hidden_grad = times_transpose(after(down_in, down_sum[2]), down_full)
    pre_grad = (hidden_grad * slope.astype(jnp.float32)).astype(jnp.bfloat16)
    up_bias_grad = jnp.sum(pre_grad, axis=0, dtype=jnp.float32)
    mlp_pull = jax.vjp(layer_norm, middle, mlp_gain_full, mlp_shift_full)[1]
    middle_part, mlp_gain_grad, mlp_shift_grad = mlp_pull(
        times_transpose(pre_grad, up_full)
    )
    middle_grad = out_grad + middle_part
    proj_in = (branch_scale * middle_grad).astype(jnp.bfloat16)
    proj_bias_grad = jnp.sum(proj_in, axis=0, dtype=jnp.float32)
    proj_mine = lax.dynamic_slice_in_dim(proj_full, half * side_count, side_count)
    proj_theirs = lax.dynamic_slice_in_dim(proj_full, (1 - half) * side_count, side_count)
    grad_gone = times_transpose(proj_in, proj_theirs).astype(jnp.bfloat16)
    grad_far = across(grad_gone)
    grad_own = times_transpose(proj_in, proj_mine).astype(jnp.bfloat16)
    pre_grad = after(pre_grad, grad_gone)
    up_weight_grad = transpose_times(normed_mlp, pre_grad).astype(jnp.bfloat16)
    proj_late = after(proj_in, grad_gone)
    proj_weight_grad = transpose_times(attended, proj_late).astype(jnp.bfloat16)
    up_weight_grad = after(up_weight_grad, grad_far, down_sum[1])
    up_sum = begin_sum([up_weight_grad, proj_weight_grad], up_order, me, count)
    down_sum = advance(down_sum, down_order[1], count, up_sum[2])
    up_sum = advance(up_sum, up_order[1], count, down_sum[2])
    query_grad, pair_grad, pair_gone = attend_backward(
        info, query, pair, out, logsum, after(grad_own, up_sum[2]), grad_far
    )
    down_sum = advance(down_sum, down_order[2], count, query_grad)
    up_sum = advance(up_sum, up_order[2], count, down_sum[2], query_grad)
    pair_grad = add(after(pair_grad, up_sum[2]), beside(pair_gone)).astype(jnp.bfloat16)
    mixed_grad = jnp.concatenate([query_grad, pair_grad[0], pair_grad[1]], axis=1)
    normed_grad = times_transpose(mixed_grad, attn_full)
    down_sum = advance(down_sum, down_order[3], count, normed_grad)
    far_grad = across(normed_grad[row_count:].astype(jnp.bfloat16))
    centered = after(everyone_low[: 2 * row_count], query_grad).astype(jnp.float32)
    centered = (centered - mean[: 2 * row_count]) * spread[: 2 * row_count]
    attn_gain_grad = jnp.sum(normed_grad * centered, axis=0)
    attn_shift_grad = jnp.sum(normed_grad, axis=0)
    attn_weight_grad = transpose_times(normed_pair, after(mixed_grad, down_sum[2])).astype(jnp.bfloat16)
    column_sums = jnp.sum(mixed_grad, axis=0, dtype=jnp.float32).reshape(3, side_count)[::2]
    attn_bias_grad = jnp.where(
        half == 0,
        jnp.pad(column_sums, ((0, 0), (0, side_count))),
        jnp.pad(column_sums, ((0, 0), (side_count, 0))),
    ).reshape(-1)
    vector_grads = [
        attn_gain_grad, attn_shift_grad, attn_bias_grad, proj_bias_grad,
        mlp_gain_grad, mlp_shift_grad, up_bias_grad, down_bias_grad,
    ]
    grad_columns = jnp.concatenate(
        [
            grad.reshape(count, -1, part).transpose(1, 0, 2).reshape(-1, feature_count)
            for grad in vector_grads
        ],
        axis=0,
    ).T
    grad_columns = jnp.pad(grad_columns, ((0, 0), (0, 128 - grad_columns.shape[1])))
    attn_order = [core_bit, x_bit] + z_bits + [y_bit]
    for bit in down_order[4:]:
        down_sum = advance(down_sum, bit, count, attn_weight_grad)
    attn_sum = begin_sum(
        [after(attn_weight_grad, down_sum[2]), grad_columns.astype(jnp.bfloat16)], attn_order, me, count
    )
    up_sum = advance(up_sum, up_order[3], count, attn_sum[2])
    attn_sum = advance(attn_sum, attn_order[1], count, up_sum[2])
    down_done = add(down_sum[0][0], after(down_sum[1], attn_sum[2])[0])
    output = middle + branch_scale * (
        product(after(hidden, attn_sum[2], down_done), down_full) + down_bias_full
    )
    output = output.astype(jnp.bfloat16)
    attn_sum = advance(attn_sum, attn_order[2], count, output)
    far_grad = after(far_grad, attn_sum[2])
    scaled = (normed_grad[:row_count] + far_grad.astype(jnp.float32)) * attn_gain_full
    centered_own = centered[:row_count]
    input_part = spread[:row_count] * (
        scaled
        - jnp.mean(scaled, axis=-1, keepdims=True)
        - centered_own * jnp.mean(scaled * centered_own, axis=-1, keepdims=True)
    )
    grad_in = (middle_grad + input_part).astype(jnp.bfloat16)
    for i in range(3, len(z_bits) + 2):
        up_sum = advance(up_sum, up_order[i + 1], count, attn_sum[2])
        attn_sum = advance(attn_sum, attn_order[i], count, up_sum[2])
    updown_done = add(up_sum[0][0], after(up_sum[1], attn_sum[2])[0])
    mine = add(attn_sum[0][0], attn_sum[1][0])
    other = add(attn_sum[0][1], attn_sum[1][1]).astype(jnp.bfloat16)
    other = flip(other, y_bit, count).astype(jnp.float32)
    first = jnp.where(half == 0, mine, other)[:, : 3 * side_count].reshape(part, 3, 1, side_count)
    second = jnp.where(half == 0, other, mine)[:, : 3 * side_count].reshape(part, 3, 1, side_count)
    attn_done = jnp.concatenate([first, second], axis=2).reshape(part, 3 * feature_count)
    done_lanes = (mine + other)[:, 3 * side_count :].T
    done_vectors, spot = [], 0
    for vector in vectors:
        size = vector.shape[0] // part
        done_vectors.append(done_lanes[spot : spot + size].reshape(-1))
        spot += size
    return (
        output[None],
        grad_in[None],
        done_vectors[0],
        done_vectors[1],
        attn_done,
        done_vectors[2],
        updown_done[:, ff_count:],
        done_vectors[3],
        done_vectors[4],
        done_vectors[5],
        updown_done[:, :ff_count],
        done_vectors[6],
        down_done,
        done_vectors[7],
    )


def solution(mesh):
    rows = P(AXES)
    tiles = P(AXES, None)
    pack = P(None, AXES, None)
    return jax.shard_map(
        functools.partial(shards, mesh.shape["dp"], mesh.shape["seq"]),
        mesh=mesh,
        in_specs=(
            pack, P(None, AXES), pack, rows, rows, tiles, rows, tiles, rows, rows, rows, tiles,
            rows, tiles, rows,
        ),
        out_specs=(
            pack, pack, rows, rows, tiles, rows, tiles, rows, rows, rows, tiles, rows, tiles, rows,
        ),
        check_vma=False,
    )
```
